32 devices in a mesh: seq: 8 (over z, y), batch: 4 (over x, core).
Axes of the slice: x: 2, y: 2, z: 4, core: 2. Of those that a mesh axis runs over, the one named last changes fastest.
Arguments:
- inputs: bfloat16 [8, 2048, 768], P('batch', 'seq'), may hold values from -6 to 6
- lengths: int32 [8], P('batch'), may hold values from 512 to 2048, as said below
- cotangent: bfloat16 [8, 2048, 768], P('batch', 'seq'), may hold values from -6 to 6
- local_query: bfloat16 [768, 768], replicated, may hold values from -0.21875 to 0.21875
- local_query_bias: float32 [768], replicated, may hold values from -3 to 3
- local_key: bfloat16 [768, 768], replicated, may hold values from -0.21875 to 0.21875
- local_value: bfloat16 [768, 768], replicated, may hold values from -0.21875 to 0.21875
- local_value_bias: float32 [768], replicated, may hold values from -3 to 3
- local_output: bfloat16 [768, 768], replicated, may hold values from -0.875 to 0.875
- local_output_bias: float32 [768], replicated, may hold values from -3 to 3
- pooled_query: bfloat16 [768, 768], replicated, may hold values from -0.15625 to 0.15625
- pooled_query_bias: float32 [768], replicated, may hold values from -3 to 3
- pooled_output: bfloat16 [768, 768], replicated, may hold values from -1.25 to 1.25
- pooled_output_bias: float32 [768], replicated, may hold values from -3 to 3
- conv_key: float32 [768, 5], replicated, may hold values from -2.5 to 2.5
- conv_value: float32 [768, 5], replicated, may hold values from -2.5 to 2.5
- conv_value_bias: float32 [768], replicated, may hold values from -3 to 3
- norm_gain: float32 [768], replicated, may hold values from 0.5 to 1.5
- norm_shift: float32 [768], replicated, may hold values from -1.75 to 1.75
- expand_weight: bfloat16 [768, 3072], replicated, may hold values from -0.21875 to 0.21875
- expand_bias: float32 [3072], replicated, may hold values from -3 to 3
- reduce_weight: bfloat16 [3072, 768], replicated, may hold values from -0.109375 to 0.109375
- reduce_bias: float32 [768], replicated, may hold values from -3 to 3
- final_gain: float32 [768], replicated, may hold values from 0.5 to 1.5
- final_shift: float32 [768], replicated, may hold values from -1.75 to 1.75
Outputs:
- outputs: bfloat16 [8, 2048, 768], P('batch', 'seq')
- input_grad: bfloat16 [8, 2048, 768], P('batch', 'seq')
- grad_local_query: float32 [768, 768], P('seq')
- grad_local_query_bias: float32 [768], P('seq')
- grad_local_key: float32 [768, 768], P('seq')
- grad_local_value: float32 [768, 768], P('seq')
- grad_local_value_bias: float32 [768], P('seq')
- grad_local_output: float32 [768, 768], P('seq')
- grad_local_output_bias: float32 [768], P('seq')
- grad_pooled_query: float32 [768, 768], P('seq')
- grad_pooled_query_bias: float32 [768], P('seq')
- grad_pooled_output: float32 [768, 768], P('seq')
- grad_pooled_output_bias: float32 [768], P('seq')
- grad_conv_key: float32 [768, 5], P('seq')
- grad_conv_value: float32 [768, 5], P('seq')
- grad_conv_value_bias: float32 [768], P('seq')
- grad_norm_gain: float32 [768], P('seq')
- grad_norm_shift: float32 [768], P('seq')
- grad_expand_weight: float32 [768, 3072], P('seq')
- grad_expand_bias: float32 [3072], P('seq')
- grad_reduce_weight: float32 [3072, 768], P('seq')
- grad_reduce_bias: float32 [768], P('seq')
- grad_final_gain: float32 [768], P('seq')
- grad_final_shift: float32 [768], P('seq')
The draws below stay inside these ranges and needn't reach their ends.
Inputs may be any that keep to these rules, and one draw needn't show every extreme that they name: `lengths`: each document fills its slots from the first one and is padded at its end; documents b with the same b // 2 form a group, and in each group one document, drawn from the seed, fills all 2048 slots.
All inputs are finite; a program needn't handle non-finite values.
Results may differ from the reference program's by a relative error of at most 0.029.
The reference program's roundings to bfloat16 on the way count: a program that leaves them out, or rounds other values in their place, can miss the bound.
Values may be sent and summed in bfloat16 or wider, within the bound.
No kernel may reach another device: no remote copies, remote signals or barrier semaphores. Data moves between devices by JAX's collectives and lax.ppermute only.
A program may use at most 192 MiB of HBM per device.

```python
import math
import jax
import jax.numpy as jnp
from jax import lax

D = 768
HEADS = 12
HD = 64
FF = 3072
WIN = 128
PWIN = 512
KER = 5
STRIDE = 4
DOC_DEV = 2
SEQ_LEN = 2048
DOCS = 8


def draw_lengths(key, part):
    first_key, second_key = jax.random.split(key)
    ragged = jax.random.randint(first_key, (DOCS,), SEQ_LEN // 4, SEQ_LEN + 1)
    chosen = jax.random.randint(second_key, (DOCS // DOC_DEV,), 0, DOC_DEV)
    places = jnp.arange(DOCS, dtype=jnp.int32)
    full_one = places % DOC_DEV == chosen[places // DOC_DEV]
    return jnp.where(full_one, SEQ_LEN, ragged).astype(jnp.int32)


def spiked(array, own_key, source, target, blocks, factor):
    def block_of(axis_at):
        return (jnp.arange(array.shape[axis_at]) // (array.shape[axis_at] // blocks)).reshape((-1,) + (1,) * (array.ndim - 1 - axis_at))

    first = jax.random.permutation(own_key, blocks)[block_of(target)]
    far = (block_of(target) + blocks // 2) % blocks
    return jnp.where((block_of(source) == first) | (block_of(source) == far), factor * array, array)


def steps_of(stream_key, extent, pieces, least, top_value):
    def one(axis_at, parts):
        steps = jax.random.uniform(jax.random.fold_in(jax.random.fold_in(stream_key, 6), axis_at), (parts,), jnp.float32, least / len(pieces), top_value / len(pieces))
        return jnp.repeat(jnp.exp(steps), extent[axis_at] // parts).reshape((-1,) + (1,) * (len(extent) - axis_at - 1))

    gain = one(*pieces[0])
    for cut in pieces[1:]:
        gain = gain * one(*cut)
    return gain


def gaussian(own_key, extent, width, bound, cuts=(), kind=jnp.bfloat16):
    array = jax.random.normal(own_key, extent, jnp.float32) * width
    if len(cuts) > 0:
        array = steps_of(own_key, extent, cuts, -0.22, 0.18) * array
    return jnp.clip(array, min=-bound, max=bound).astype(kind)


def gaussian_with(key, dims, scale, most, cuts, heavy, held_as=jnp.bfloat16):
    entries = scale * jax.random.normal(key, dims, jnp.float32)
    if cuts:
        entries = entries * steps_of(key, dims, cuts, -0.22, 0.18)
    return jnp.clip(spiked(entries, jax.random.fold_in(key, 3), *heavy), -most, most).astype(held_as)


def setup_inputs(seed: int = 0) -> dict:
    key_list = jax.random.split(jax.random.key(seed), 26)
    return {
        "inputs": gaussian(key_list[0], (DOCS, SEQ_LEN, D), 1.0, 6.0, ((0, 4), (1, 8))),
        "lengths": draw_lengths(jax.random.fold_in(key_list[25], 71), 0),
        "cotangent": gaussian_with(key_list[2], (DOCS, SEQ_LEN, D), 1.0, 6.0, ((0, 4), (1, 8)), (1, 2, 8, 2.0)),
        "local_query": gaussian(key_list[3], (D, D), D ** -0.5, 0.21875),
        "local_query_bias": gaussian(key_list[4], (D,), 0.5, 3.0, (), jnp.float32),
        "local_key": gaussian(key_list[5], (D, D), D ** -0.5, 0.21875),
        "local_value": gaussian(key_list[6], (D, D), D ** -0.5, 0.21875),
        "local_value_bias": gaussian(key_list[7], (D,), 0.5, 3.0, (), jnp.float32),
        "local_output": gaussian(key_list[8], (D, D), (D // 16) ** -0.5, 0.875),
        "local_output_bias": gaussian(key_list[9], (D,), 0.5, 3.0, (), jnp.float32),
        "pooled_query": gaussian(key_list[10], (D, D), (2 * D) ** -0.5, 0.15625),
        "pooled_query_bias": gaussian(key_list[11], (D,), 0.5, 3.0, (), jnp.float32),
        "pooled_output": gaussian(key_list[12], (D, D), (D // 32) ** -0.5, 1.25),
        "pooled_output_bias": gaussian(key_list[13], (D,), 0.5, 3.0, (), jnp.float32),
        "conv_key": gaussian(key_list[14], (D, KER), 0.45, 2.5, (), jnp.float32),
        "conv_value": gaussian(key_list[15], (D, KER), 0.45, 2.5, (), jnp.float32),
        "conv_value_bias": gaussian(key_list[16], (D,), 0.5, 3.0, (), jnp.float32),
        "norm_gain": jnp.clip(1.0 + 0.1 * jax.random.normal(key_list[17], (D,), jnp.float32), 0.5, 1.5),
        "norm_shift": gaussian(key_list[18], (D,), 0.3, 1.75, (), jnp.float32),
        "expand_weight": gaussian(key_list[19], (D, FF), D ** -0.5, 0.21875),
        "expand_bias": gaussian(key_list[20], (FF,), 0.5, 3.0, (), jnp.float32),
        "reduce_weight": gaussian(key_list[21], (FF, D), FF ** -0.5, 0.109375),
        "reduce_bias": gaussian(key_list[22], (D,), 0.5, 3.0, (), jnp.float32),
        "final_gain": jnp.clip(1.0 + 0.1 * jax.random.normal(key_list[23], (D,), jnp.float32), 0.5, 1.5),
        "final_shift": gaussian(key_list[24], (D,), 0.3, 1.75, (), jnp.float32),
    }


NEGATIVE = -1e+30

@jax.custom_vjp
def low(v):
    return lax.optimization_barrier(v.astype(jnp.bfloat16)).astype(jnp.float32)

@jax.custom_vjp
def low_back(v):
    return v

def low_keep(v):
    return (low(v), None)

def low_pass(kept, grad):
    return (grad,)

def back_keep(v):
    return (v, None)

def back_low(kept, grad):
    return (low(grad),)
low.defvjp(low_keep, low_pass)
low_back.defvjp(back_keep, back_low)

def matmul(operand, matrix):
    return jnp.dot(operand, matrix, precision=lax.Precision.HIGHEST)

def widen(array_in):
    return array_in.astype(jnp.float32)

def add_pair(former, latter):
    return former + latter

def layer_norm(values, scales, offsets):
    centred = values - lax.optimization_barrier(jnp.mean(values, axis=-1, keepdims=True))
    spread = lax.optimization_barrier(jnp.mean(centred * centred, axis=-1, keepdims=True))
    return centred * lax.rsqrt(spread + 1e-05) * scales + offsets

def local_allowed(query_place, key_place, length):
    half_width = WIN // 2
    nearby = (key_place[None, :] >= query_place[:, None] - half_width) & (key_place[None, :] < query_place[:, None] + half_width)
    usable = (key_place >= 0) & (key_place < length)
    return nearby & usable[None, :] | (key_place[None, :] == query_place[:, None])

def pooled_allowed(centres, key_place, length):
    half_width = PWIN // 2
    nearby = (key_place[None, :] >= centres[:, None] - half_width) & (key_place[None, :] < centres[:, None] + half_width)
    usable = (key_place >= 0) & (key_place * STRIDE < length)
    return nearby & usable[None, :] | (key_place[None, :] == centres[:, None])

def attend(query_rows, key_rows, value_rows, allowed):
    row_count = query_rows.shape[0]
    query_heads = query_rows.reshape(row_count, HEADS, HD)
    key_heads = key_rows.reshape(key_rows.shape[0], HEADS, HD)
    value_heads = value_rows.reshape(value_rows.shape[0], HEADS, HD)
    raw_scores = low_back(jnp.einsum('qhd,khd->hqk', query_heads, key_heads, precision=lax.Precision.HIGHEST))
    scores = jnp.where(allowed[None], raw_scores * (1.0 / math.sqrt(HD)), NEGATIVE)
    weights = low(jax.nn.softmax(scores, axis=-1))
    mixture = jnp.einsum('hqk,khd->qhd', weights, value_heads, precision=lax.Precision.HIGHEST)
    return mixture.reshape(row_count, HEADS * HD)

def local_level(query_rows, key_rows, value_rows, length):
    row_count = query_rows.shape[0]
    block_rows = min(512, row_count)
    half_width = WIN // 2
    key_pad = jnp.pad(key_rows, ((half_width, half_width), (0, 0)))
    value_pad = jnp.pad(value_rows, ((half_width, half_width), (0, 0)))

    def one_block(block_index):
        first_row = block_index * block_rows
        query_place = first_row + jnp.arange(block_rows, dtype=jnp.int32)
        key_place = first_row - half_width + jnp.arange(block_rows + 2 * half_width, dtype=jnp.int32)
        allowed = local_allowed(query_place, key_place, length)
        return attend(lax.dynamic_slice_in_dim(query_rows, first_row, block_rows, 0), lax.dynamic_slice_in_dim(key_pad, first_row, block_rows + 2 * half_width, 0), lax.dynamic_slice_in_dim(value_pad, first_row, block_rows + 2 * half_width, 0), allowed)
    blocks = lax.map(jax.checkpoint(one_block), jnp.arange(row_count // block_rows, dtype=jnp.int32))
    return blocks.reshape(row_count, query_rows.shape[1])

def pooled_level(query_rows, key_rows, value_rows, length):
    row_count = query_rows.shape[0]
    block_rows = min(512, row_count)
    pooled_block = block_rows // STRIDE
    half_width = PWIN // 2
    key_pad = jnp.pad(key_rows, ((half_width, half_width), (0, 0)))
    value_pad = jnp.pad(value_rows, ((half_width, half_width), (0, 0)))

    def one_block(block_index):
        first_row = block_index * block_rows
        first_pooled = block_index * pooled_block
        centres = (first_row + jnp.arange(block_rows, dtype=jnp.int32)) // STRIDE
        key_place = first_pooled - half_width + jnp.arange(pooled_block + 2 * half_width, dtype=jnp.int32)
        allowed = pooled_allowed(centres, key_place, length)
        return attend(lax.dynamic_slice_in_dim(query_rows, first_row, block_rows, 0), lax.dynamic_slice_in_dim(key_pad, first_pooled, pooled_block + 2 * half_width, 0), lax.dynamic_slice_in_dim(value_pad, first_pooled, pooled_block + 2 * half_width, 0), allowed)
    blocks = lax.map(jax.checkpoint(one_block), jnp.arange(row_count // block_rows, dtype=jnp.int32))
    return blocks.reshape(row_count, query_rows.shape[1])

def pool(values, kernel):
    row_count, columns = values.shape
    padded = jnp.pad(values, ((KER // 2, STRIDE), (0, 0)))
    pooled = jnp.zeros((row_count // STRIDE, columns), jnp.float32)
    for tap_index in range(KER):
        pooled = pooled + lax.slice(padded, (tap_index, 0), (tap_index + row_count, columns), (STRIDE, 1)) * kernel[:, tap_index]
    return pooled

def layer_forward(rows_in, params, length):
    local_query, local_query_bias, local_key, local_value, local_value_bias, local_output, local_output_bias, pooled_query, pooled_query_bias, pooled_output, pooled_output_bias, conv_key, conv_value, conv_value_bias, norm_gain, norm_shift, expand_weight, expand_bias, reduce_weight, reduce_bias, final_gain, final_shift = params
    row_count = rows_in.shape[0]
    validity = (jnp.arange(row_count, dtype=jnp.int32) < length).astype(jnp.float32)[:, None]
    query_one = low(low_back(matmul(rows_in, local_query) + local_query_bias))
    key_one = low(low_back(matmul(rows_in, local_key)))
    value_one = low(low_back(matmul(rows_in, local_value) + local_value_bias))
    mixture_one = low(low_back(local_level(query_one, key_one, value_one, length)))
    first_branch = low_back(matmul(mixture_one, local_output) + local_output_bias)
    middle = rows_in + first_branch
    query_two = low(low_back(matmul(low(middle), pooled_query) + pooled_query_bias))
    pooled_keys = low(pool(validity * key_one, conv_key))
    pooled_values = low(pool(validity * value_one, conv_value) + conv_value_bias)
    mixture_two = low(low_back(pooled_level(query_two, pooled_keys, pooled_values, length)))
    second = low_back(matmul(mixture_two, pooled_output) + pooled_output_bias)
    normed = layer_norm(middle + second, norm_gain, norm_shift)
    hidden_pre = low_back(matmul(low(normed), expand_weight) + expand_bias)
    hidden = low(jax.nn.gelu(hidden_pre, approximate=False))
    branch = low_back(matmul(hidden, reduce_weight) + reduce_bias)
    return validity * layer_norm(normed + branch, final_gain, final_shift)

def reference(inputs, lengths, cotangent, local_query, local_query_bias, local_key, local_value, local_value_bias, local_output, local_output_bias, pooled_query, pooled_query_bias, pooled_output, pooled_output_bias, conv_key, conv_value, conv_value_bias, norm_gain, norm_shift, expand_weight, expand_bias, reduce_weight, reduce_bias, final_gain, final_shift):
    params = tuple(map(widen, (local_query, local_query_bias, local_key, local_value, local_value_bias, local_output, local_output_bias, pooled_query, pooled_query_bias, pooled_output, pooled_output_bias, conv_key, conv_value, conv_value_bias, norm_gain, norm_shift, expand_weight, expand_bias, reduce_weight, reduce_bias, final_gain, final_shift)))

    def one_document(totals, document_items):
        rows_in, length, grad_rows = document_items

        def forward(rows_float, weight_set):
            return layer_forward(rows_float, weight_set, length)
        result, pullback = jax.vjp(forward, rows_in.astype(jnp.float32), params)
        grad_input, grad_weights = pullback(grad_rows.astype(jnp.float32))
        totals = jax.tree.map(add_pair, totals, grad_weights)
        return (totals, (result.astype(jnp.bfloat16), grad_input.astype(jnp.bfloat16)))
    zero_grads = jax.tree.map(jnp.zeros_like, params)
    totals, (outputs, input_grad) = lax.scan(one_document, zero_grads, (inputs, lengths, cotangent))
    return (outputs, input_grad, totals[0], totals[1], totals[2], totals[3], totals[4], totals[5], totals[6], totals[7], totals[8], totals[9], totals[10], totals[11], totals[12], totals[13], totals[14], totals[15], totals[16], totals[17], totals[18], totals[19], totals[20], totals[21])
```

```python
import functools
import math

import jax
import jax.numpy as jnp
from jax import lax
from jax.experimental import pallas as pl
from jax.experimental.pallas import tpu as pltpu
from jax.sharding import PartitionSpec as P

HEADS = 12
HD = 64
WIN = 128
PWIN = 512
KER = 5
STRIDE = 4
HALF = WIN // 2
REACH = PWIN // 2
NEGATIVE = -1e30
SCALE = 1.0 / math.sqrt(HD)
EPSILON = 1e-05
LANES = 128
TILE = 128
ROWS = 128
CHUNK = 256
VMEM_BYTES = 58 * 1024 * 1024
F32 = jnp.float32
BF16 = jnp.bfloat16


def nn(left, right):
    return jnp.dot(left, right, preferred_element_type=F32)


def nt(left, right):
    return lax.dot_general(left, right, (((1,), (1,)), ((), ())), preferred_element_type=F32)


def tn(left, right):
    return lax.dot_general(left, right, (((0,), (0,)), ((), ())), preferred_element_type=F32)


def column_sum(block):
    return jnp.sum(block.astype(F32), axis=0, keepdims=True)


def call(body, grid, scalars, inputs, outputs, scratch=(), flops=0, moved=0, exps=0):
    def spec(block, index):
        if block is None:
            return pl.BlockSpec(memory_space=pltpu.VMEM)
        return pl.BlockSpec(block, index)

    return pl.pallas_call(
        body,
        grid_spec=pltpu.PrefetchScalarGridSpec(
            num_scalar_prefetch=len(scalars),
            grid=grid,
            in_specs=[spec(block, index) for _, block, index in inputs],
            out_specs=[spec(block, index) for _, _, block, index in outputs],
            scratch_shapes=list(scratch),
        ),
        out_shape=[jax.ShapeDtypeStruct(shape, dtype) for shape, dtype, _, _ in outputs],
        compiler_params=pltpu.CompilerParams(
            dimension_semantics=("arbitrary",) * len(grid), vmem_limit_bytes=VMEM_BYTES
        ),
        cost_estimate=pl.CostEstimate(flops=flops, bytes_accessed=moved, transcendentals=exps),
    )(*scalars, *[array for array, _, _ in inputs])


def whole(array):
    zeros = (0,) * array.ndim
    return (array, array.shape, lambda *_: zeros)


def by_doc(array):
    zeros = (0,) * (array.ndim - 1)
    return (array, (1,) + array.shape[1:], lambda doc, *_: (doc,) + zeros)


def out_doc(shape, dtype):
    zeros = (0,) * (len(shape) - 1)
    return (shape, dtype, (1,) + tuple(shape[1:]), lambda doc, *_: (doc,) + zeros)


def out_whole(shape, dtype):
    zeros = (0,) * len(shape)
    return (shape, dtype, shape, lambda *_: zeros)


def stack_heads(block):
    lane = lax.broadcasted_iota(jnp.int32, block.shape, 1)
    zero = jnp.zeros_like(block)
    return jnp.concatenate(
        [jnp.where(lane < HD, block, zero), jnp.where(lane < HD, zero, block)], axis=0
    )


def unstack(block):
    joined = jnp.concatenate([block[:HD, :TILE], block[HD:, TILE:]], axis=0)
    return joined.T


def positions(shape, dim):
    return lax.broadcasted_iota(jnp.int32, shape, dim)


def project_body(place, x, left, right, wq, bq, wk, wv, bv, ck, cv, bcv, q, kx, vx, pooled, rows):
    doc = pl.program_id(0)
    offset, length = place[0], place[1 + doc]
    own = x[0]
    q[0] = (nn(own, wq[...]) + bq[...]).astype(BF16)
    extended = jnp.concatenate([left[0], own, right[0]], axis=0)
    spot = offset - HALF + positions((extended.shape[0], 1), 0)
    valid = (spot >= 0) & (spot < length)
    count = pooled.shape[2]
    for which, (weight, bias, taps, out) in enumerate(((wk, None, ck, kx), (wv, bv, cv, vx))):
        value = nn(extended, weight[...])
        if bias is not None:
            value = value + bias[...]
        value = value.astype(BF16)
        out[0] = value
        masked = jnp.where(valid, value.astype(F32), 0.0)
        for group in range(value.shape[1] // LANES):
            lanes = slice(group * LANES, (group + 1) * LANES)
            rows[group] = masked[:, lanes]
            total = jnp.zeros((count, LANES), F32)
            for tap in range(KER):
                start = HALF - KER // 2 + tap
                read = rows[group, pl.ds(start, count, stride=STRIDE), :]
                total = total + read * taps[tap : tap + 1, lanes]
            if which == 1:
                total = total + bcv[:, lanes]
            pooled[0, which, :, lanes] = total.astype(BF16)


def project(place, x, left, right, wq, bq, wk, wv, bv, ck, cv, bcv):
    docs, rows, width = x.shape
    extended = rows + WIN
    return call(
        project_body,
        (docs,),
        (place,),
        [by_doc(x), by_doc(left), by_doc(right)]
        + [whole(a) for a in (wq, bq, wk, wv, bv, ck, cv, bcv)],
        [
            out_doc((docs, rows, width), BF16),
            out_doc((docs, extended, width), BF16),
            out_doc((docs, extended, width), BF16),
            out_doc((docs, 2, rows // STRIDE, width), BF16),
        ],
        [pltpu.VMEM((width // LANES, extended, LANES), F32)],
        flops=2 * docs * (rows + 2 * extended) * width * width,
        moved=10**7,
    )


def local_bias(tile, offset, length):
    shape = (TILE + WIN, TILE)
    key = positions(shape, 0)
    query = positions(shape, 1)
    spot = offset + tile * TILE - HALF + key
    allowed = (
        (key >= query) & (key < query + WIN) & (spot >= 0) & (spot < length)
    ) | (key == query + HALF)
    return jnp.where(allowed, 0.0, NEGATIVE)


def softmax_columns(scores):
    top = jnp.max(scores, axis=0, keepdims=True)
    grown = jnp.exp(scores - top)
    return grown * (1.0 / jnp.sum(grown, axis=0, keepdims=True))


def local_forward_body(
    place, q, kx, vx, x, wo, bo, wpq, bpq, mix, probs, middle, middle_low, q2
):
    doc = pl.program_id(0)
    offset, length = place[0], place[1 + doc]
    span = TILE + WIN
    for tile in range(q.shape[1] // TILE):
        half_bias = local_bias(tile, offset, length)
        bias = jnp.concatenate([half_bias, half_bias], axis=1)
        first = tile * TILE
        for pair in range(q.shape[2] // LANES):
            lanes = slice(pair * LANES, (pair + 1) * LANES)
            queries = stack_heads(q[0, first : first + TILE, lanes])
            scores = nt(kx[0, first : first + span, lanes], queries) * SCALE + bias
            chance = softmax_columns(scores)
            probs[0, pair, tile] = chance
            turned = vx[0, first : first + span, lanes].T
            mixed = nn(turned, chance.astype(BF16))
            mix[0, first : first + TILE, lanes] = unstack(mixed).astype(BF16)
    total = x[0].astype(F32) + (nn(mix[0], wo[...]) + bo[...])
    middle[0] = total
    low = total.astype(BF16)
    middle_low[0] = low
    q2[0] = (nn(low, wpq[...]) + bpq[...]).astype(BF16)


def local_forward(place, q, kx, vx, x, wo, bo, wpq, bpq):
    docs, rows, width = q.shape
    pairs, tiles, span = width // LANES, rows // TILE, TILE + WIN
    return call(
        local_forward_body,
        (docs,),
        (place,),
        [by_doc(a) for a in (q, kx, vx, x)] + [whole(a) for a in (wo, bo, wpq, bpq)],
        [
            out_doc((docs, rows, width), BF16),
            out_doc((docs, pairs, tiles, span, 2 * TILE), F32),
            out_doc((docs, rows, width), F32),
            out_doc((docs, rows, width), BF16),
            out_doc((docs, rows, width), BF16),
        ],
        flops=docs * rows * width * (4 * width + 4 * 2 * span),
        moved=2 * 10**7,
        exps=docs * rows * HEADS * span,
    )


def attention_back(keys, values, queries, grads, chance):
    stacked_grads = stack_heads(grads)
    stacked_queries = stack_heads(queries)
    grad_chance = nt(values, stacked_grads)
    dots = jnp.sum(chance * grad_chance, axis=0, keepdims=True)
    grad_raw = (chance * (grad_chance - dots) * SCALE).astype(BF16)
    grad_keys = nn(grad_raw, stacked_queries)
    grad_values = nn(chance.astype(BF16), stacked_grads)
    grad_queries = unstack(nn(keys.T, grad_raw))
    return grad_queries, grad_keys, grad_values


def local_backward_body(
    place, q, kx, vx, probs, gq2, gsum, wpq, wo,
    dq, own, low_left, low_right, gmid, gfirst, vec, gmix, dk, dv,
):
    doc = pl.program_id(0)
    total = gsum[0] + nt(gq2[0], wpq[...])
    gmid[0] = total
    low = total.astype(BF16)
    gfirst[0] = low
    gmix[...] = nt(low, wo[...]).astype(BF16)

    @pl.when(doc == 0)
    def _():
        vec[...] = jnp.zeros_like(vec)

    vec[0:1] += column_sum(gq2[0])
    vec[1:2] += column_sum(low)
    rows = q.shape[1]
    span = TILE + WIN
    dk[...] = jnp.zeros_like(dk)
    dv[...] = jnp.zeros_like(dv)
    for tile in range(rows // TILE):
        first = tile * TILE
        for pair in range(q.shape[2] // LANES):
            lanes = slice(pair * LANES, (pair + 1) * LANES)
            grad_q, grad_k, grad_v = attention_back(
                kx[0, first : first + span, lanes],
                vx[0, first : first + span, lanes],
                q[0, first : first + TILE, lanes],
                gmix[first : first + TILE, lanes],
                probs[0, pair, tile],
            )
            dq[0, first : first + TILE, lanes] = grad_q.astype(BF16)
            dk[first : first + span, lanes] += grad_k
            dv[first : first + span, lanes] += grad_v
    for which, part in enumerate((dk, dv)):
        own[0, which] = part[HALF : HALF + rows]
        low_left[0, which] = part[:HALF].astype(BF16)
        low_right[0, which] = part[HALF + rows :].astype(BF16)


def local_backward(place, q, kx, vx, probs, gq2, gsum, wpq, wo):
    docs, rows, width = q.shape
    span = TILE + WIN
    return call(
        local_backward_body,
        (docs,),
        (place,),
        [by_doc(a) for a in (q, kx, vx, probs, gq2, gsum)] + [whole(wpq), whole(wo)],
        [
            out_doc((docs, rows, width), BF16),
            out_doc((docs, 2, rows, width), F32),
            out_doc((docs, 2, HALF, width), BF16),
            out_doc((docs, 2, HALF, width), BF16),
            out_doc((docs, rows, width), F32),
            out_doc((docs, rows, width), BF16),
            out_whole((8, width), F32),
        ],
        [
            pltpu.VMEM((rows, width), BF16),
            pltpu.VMEM((rows + WIN, width), F32),
            pltpu.VMEM((rows + WIN, width), F32),
        ],
        flops=docs * rows * width * (4 * width + 8 * 2 * span),
        moved=2 * 10**7,
    )


def pooled_forward_body(place, slots, *refs, pieces):
    key_pieces = refs[:pieces]
    value_pieces = refs[pieces : 2 * pieces]
    q2, middle, wpo, bpo, keys, values, probs, mix, summed, bias = refs[2 * pieces :]
    doc, pair = pl.program_id(0), pl.program_id(1)
    offset, length, base = place[0], place[1 + doc], place[1 + pl.num_programs(0)]
    tiles = q2.shape[1] // TILE
    count = keys.shape[1]

    @pl.when(pair == 0)
    def _():
        for where, group, out in ((0, key_pieces, keys), (1, value_pieces, values)):
            at = 0
            for piece in group:
                size = piece.shape[2]
                for block in range(piece.shape[0]):
                    spot = pl.multiple_of(slots[where, at] * size, size)
                    out[0, pl.ds(spot, size), :] = piece[block, 0]
                    at += 1
        for tile in range(tiles):
            shape = (count, TILE)
            spot = base + positions(shape, 0)
            centre = offset // STRIDE + (tile * TILE + positions(shape, 1)) // STRIDE
            allowed = (
                (spot >= centre - REACH)
                & (spot < centre + REACH)
                & (spot >= 0)
                & (spot * STRIDE < length)
            ) | (spot == centre)
            bias[tile] = jnp.where(allowed, 0.0, NEGATIVE)

    lanes = pl.ds(pl.multiple_of(pair * LANES, LANES), LANES)
    pair_keys = keys[0, :, lanes]
    turned = values[0, :, lanes].T
    for tile in range(tiles):
        first = tile * TILE
        queries = stack_heads(q2[0, first : first + TILE, :])
        half_bias = bias[tile]
        scores = nt(pair_keys, queries) * SCALE + jnp.concatenate([half_bias, half_bias], axis=1)
        chance = softmax_columns(scores)
        probs[0, 0, tile] = chance
        mixed = nn(turned, chance.astype(BF16))
        mix[0, first : first + TILE, lanes] = unstack(mixed).astype(BF16)

    @pl.when(pair == pl.num_programs(1) - 1)
    def _():
        summed[0] = middle[0] + (nn(mix[0], wpo[...]) + bpo[...])


def pooled_forward(place, slots, key_pieces, value_pieces, q2, middle, wpo, bpo):
    docs, rows, width = q2.shape
    pairs, tiles = width // LANES, rows // TILE
    size = key_pieces[0].shape[2]
    count = size * slots.shape[1]

    def piece(array):
        return (array, (array.shape[0], 1, size, width), lambda doc, *_: (0, doc, 0, 0))

    return call(
        functools.partial(pooled_forward_body, pieces=len(key_pieces)),
        (docs, pairs),
        (place, slots),
        [piece(a) for a in key_pieces + value_pieces]
        + [
            (q2, (1, rows, LANES), lambda doc, pair, *_: (doc, 0, pair)),
            by_doc(middle),
            whole(wpo),
            whole(bpo),
        ],
        [
            out_doc((docs, count, width), BF16),
            out_doc((docs, count, width), BF16),
            (
                (docs, pairs, tiles, count, 2 * TILE),
                F32,
                (1, 1, tiles, count, 2 * TILE),
                lambda doc, pair, *_: (doc, pair, 0, 0, 0),
            ),
            out_doc((docs, rows, width), BF16),
            out_doc((docs, rows, width), F32),
        ],
        [pltpu.VMEM((tiles, count, TILE), F32)],
        flops=docs * rows * width * (2 * width + 4 * 2 * count),
        moved=3 * 10**7,
        exps=docs * rows * HEADS * count,
    )


def pooled_backward_body(places, q2, keys, values, probs, grads, dq, dk, dv):
    size = dk.shape[2]
    grad_keys = None
    for tile in range(q2.shape[1] // TILE):
        first = tile * TILE
        grad_q, grad_k, grad_v = attention_back(
            keys[0], values[0], q2[0, first : first + TILE], grads[0, first : first + TILE],
            probs[0, 0, tile],
        )
        dq[0, first : first + TILE] = grad_q.astype(BF16)
        if grad_keys is None:
            grad_keys, grad_values = grad_k, grad_v
        else:
            grad_keys, grad_values = grad_keys + grad_k, grad_values + grad_v
    for block in range(dk.shape[0]):
        part = slice(block * size, (block + 1) * size)
        dk[places[0, block], 0] = grad_keys[part].astype(BF16)
        dv[places[1, block], 0] = grad_values[part].astype(BF16)


def pooled_backward(places, q2, keys, values, probs, grads, size):
    docs, rows, width = q2.shape
    count = keys.shape[1]
    blocks = count // size
    tiles = rows // TILE

    def lanes_of(array):
        return (array, (1, array.shape[1], LANES), lambda doc, pair, *_: (doc, 0, pair))

    spread = (
        (blocks, docs, size, width),
        BF16,
        (blocks, 1, size, LANES),
        lambda doc, pair, *_: (0, doc, 0, pair),
    )
    return call(
        pooled_backward_body,
        (docs, width // LANES),
        (places,),
        [
            lanes_of(q2),
            lanes_of(keys),
            lanes_of(values),
            (
                probs,
                (1, 1, tiles, count, 2 * TILE),
                lambda doc, pair, *_: (doc, pair, 0, 0, 0),
            ),
            lanes_of(grads),
        ],
        [
            ((docs, rows, width), BF16, (1, rows, LANES), lambda doc, pair, *_: (doc, 0, pair)),
            spread,
            spread,
        ],
        flops=docs * rows * width * 8 * 2 * count,
        moved=2 * 10**7,
    )


def feed_body(
    place, summed, cotangent, we, be, wr, br, ng, ns, fg, fs, wpo,
    outputs, normed_low, hidden, grad_branch, grad_pre, grad_summed, grad_second, grad_mix,
    vec, vec_wide,
    normed, slope, work, unit,
):
    docs, rows = cotangent.shape[0], cotangent.shape[1]
    width = summed.shape[2]
    wide = we.shape[1]
    steps = rows // ROWS
    blocks = [(doc, step * ROWS, doc * rows + step * ROWS) for doc in range(docs) for step in range(steps)]

    def normal(value):
        centred = value - jnp.mean(value, axis=-1, keepdims=True)
        scale = lax.rsqrt(jnp.mean(centred * centred, axis=-1, keepdims=True) + EPSILON)
        return centred * scale, scale

    scales = []
    for doc, start, row in blocks:
        norm, scale = normal(summed[doc, start : start + ROWS])
        scales.append(scale)
        unit[row : row + ROWS] = norm
        full = norm * ng[...] + ns[...]
        normed[row : row + ROWS] = full
        normed_low[row : row + ROWS] = full.astype(BF16)

    def expand(index, _):
        part = pl.ds(pl.multiple_of(index * CHUNK, CHUNK), CHUNK)
        pre = nn(normed_low[...], we[:, part]) + be[:, part]
        cdf = 0.5 * (1.0 + lax.erf(pre * math.sqrt(0.5)))
        hidden[:, part] = (pre * cdf).astype(BF16)
        slope[:, part] = cdf + pre * (jnp.exp(pre * pre * -0.5) * (1.0 / math.sqrt(2.0 * math.pi)))
        return 0

    lax.fori_loop(0, wide // CHUNK, expand, 0)

    for start in range(0, width, CHUNK):
        part = slice(start, start + CHUNK)
        work[:, part] = normed[:, part] + (nn(hidden[...], wr[:, part]) + br[:, part])

    sums = [jnp.zeros((1, width), F32) for _ in range(6)]
    for doc, start, row in blocks:
        norm, scale = normal(work[row : row + ROWS])
        spot = place[0] + start + positions((ROWS, 1), 0)
        valid = (spot < place[1 + doc]).astype(F32)
        outputs[doc, start : start + ROWS] = (valid * (norm * fg[...] + fs[...])).astype(BF16)
        error = valid * cotangent[doc, start : start + ROWS].astype(F32)
        sums[0] += column_sum(error * norm)
        sums[1] += column_sum(error)
        scaled = error * fg[...]
        rest = (
            scaled
            - jnp.mean(scaled, axis=-1, keepdims=True)
            - norm * jnp.mean(scaled * norm, axis=-1, keepdims=True)
        ) * scale
        work[row : row + ROWS] = rest
        low = rest.astype(BF16)
        grad_branch[row : row + ROWS] = low
        sums[2] += column_sum(low)

    def reduce(index, _):
        part = pl.ds(pl.multiple_of(index * CHUNK, CHUNK), CHUNK)
        low = (nt(grad_branch[...], wr[part, :]) * slope[:, part]).astype(BF16)
        grad_pre[:, part] = low
        vec_wide[:, part] = column_sum(low)
        return 0

    lax.fori_loop(0, wide // CHUNK, reduce, 0)

    for start in range(0, width, CHUNK):
        part = slice(start, start + CHUNK)
        work[:, part] += nt(grad_pre[...], we[part, :])

    for (doc, start, row), scale in zip(blocks, scales):
        error = work[row : row + ROWS]
        norm = unit[row : row + ROWS]
        sums[3] += column_sum(error * norm)
        sums[4] += column_sum(error)
        scaled = error * ng[...]
        grad = (
            scaled
            - jnp.mean(scaled, axis=-1, keepdims=True)
            - norm * jnp.mean(scaled * norm, axis=-1, keepdims=True)
        ) * scale
        grad_summed[doc, start : start + ROWS] = grad
        low = grad.astype(BF16)
        grad_second[row : row + ROWS] = low
        sums[5] += column_sum(low)
        grad_mix[doc, start : start + ROWS] = nt(low, wpo[...]).astype(BF16)
    for index, value in enumerate(sums):
        vec[index : index + 1] = value
    vec[6:8] = jnp.zeros((2, width), F32)


def feed(place, summed, cotangent, we, be, wr, br, ng, ns, fg, fs, wpo):
    docs, rows, width = summed.shape
    wide = we.shape[1]
    tokens = docs * rows
    return call(
        feed_body,
        (1,),
        (place,),
        [whole(a) for a in (summed, cotangent, we, be, wr, br, ng, ns, fg, fs, wpo)],
        [
            out_whole((docs, rows, width), BF16),
            out_whole((tokens, width), BF16),
            out_whole((tokens, wide), BF16),
            out_whole((tokens, width), BF16),
            out_whole((tokens, wide), BF16),
            out_whole((docs, rows, width), F32),
            out_whole((tokens, width), BF16),
            out_whole((docs, rows, width), BF16),
            out_whole((8, width), F32),
            out_whole((1, wide), F32),
        ],
        [
            pltpu.VMEM((tokens, width), F32),
            pltpu.VMEM((tokens, wide), F32),
            pltpu.VMEM((tokens, width), F32),
            pltpu.VMEM((tokens, width), F32),
        ],
        flops=2 * tokens * width * (4 * wide + width),
        moved=3 * 10**7,
        exps=2 * tokens * wide,
    )


def input_body(
    place, own, from_left, from_right, gk_kept, gk_came, gv_kept, gv_came, gk_next, gv_next,
    kx, vx, ck, cv, dq, gmid, wq, wk, wv,
    gk, gv, dx, vec, rows_in, pooled, total,
):
    doc = pl.program_id(0)
    offset, length = place[0], place[1 + doc]
    rows = gk.shape[1]
    count = pooled.shape[0] - 8
    width = gk.shape[2]
    spot = offset - HALF + positions((rows + WIN, 1), 0)
    valid = (spot >= 0) & (spot < length)

    @pl.when(doc == 0)
    def _():
        vec[...] = jnp.zeros_like(vec)

    for which, (kept, came, after, ext, taps, out, row) in enumerate(
        (
            (gk_kept, gk_came, gk_next, kx, ck, gk, 0),
            (gv_kept, gv_came, gv_next, vx, cv, gv, KER),
        )
    ):
        pooled[:count] = kept[0].astype(F32) + came[0].astype(F32)
        pooled[count:] = jnp.broadcast_to(after[0].astype(F32), (8, width))
        masked = jnp.where(valid, ext[0].astype(F32), 0.0)
        for group in range(width // LANES):
            lanes = slice(group * LANES, (group + 1) * LANES)
            grown = pooled[:count, lanes]
            shifted = pooled[1 : count + 1, lanes]
            rows_in[group] = masked[:, lanes]
            for tap in range(KER):
                start = HALF - KER // 2 + tap
                read = rows_in[group, pl.ds(start, count, stride=STRIDE), :]
                vec[row + tap : row + tap + 1, lanes] += column_sum(grown * read)
            if which == 1:
                vec[2 * KER : 2 * KER + 1, lanes] += column_sum(grown)
            total[group] = own[0, which, :, lanes]
            total[group, :HALF] += from_left[0, which, :, lanes].astype(F32)
            total[group, rows - HALF :] += from_right[0, which, :, lanes].astype(F32)
            for phase, terms in enumerate(
                (
                    ((2, grown),),
                    ((3, grown),),
                    ((4, grown), (0, shifted)),
                    ((1, shifted),),
                )
            ):
                part = pl.ds(phase, count, stride=STRIDE)
                added = None
                for tap, values in terms:
                    term = values * taps[tap : tap + 1, lanes]
                    added = term if added is None else added + term
                inside = offset + phase + STRIDE * positions((count, 1), 0) < length
                total[group, part, :] = total[group, part, :] + jnp.where(inside, added, 0.0)
            out[0, :, lanes] = total[group].astype(BF16)
    vec[11:12] += column_sum(dq[0])
    vec[12:13] += column_sum(gv[0])
    dx[0] = (
        gmid[0] + nt(dq[0], wq[...]) + nt(gk[0], wk[...]) + nt(gv[0], wv[...])
    ).astype(BF16)


def input_gradients(
    place, own, from_left, from_right, pooled_grads, next_grads, kx, vx, ck, cv, dq, gmid, wq, wk, wv
):
    docs, rows, width = dq.shape
    return call(
        input_body,
        (docs,),
        (place,),
        [
            by_doc(a)
            for a in (own, from_left, from_right, *pooled_grads, *next_grads, kx, vx)
        ]
        + [whole(ck), whole(cv), by_doc(dq), by_doc(gmid), whole(wq), whole(wk), whole(wv)],
        [
            out_doc((docs, rows, width), BF16),
            out_doc((docs, rows, width), BF16),
            out_doc((docs, rows, width), BF16),
            out_whole((16, width), F32),
        ],
        [
            pltpu.VMEM((width // LANES, rows + WIN, LANES), F32),
            pltpu.VMEM((rows // STRIDE + 8, width), F32),
            pltpu.VMEM((width // LANES, rows, LANES), F32),
        ],
        flops=2 * docs * rows * width * 3 * width,
        moved=2 * 10**7,
    )


def scatter_body(bits, *refs, widths, splits):
    count = len(widths)
    lefts, rights, out = refs[: count * 2 : 2], refs[1 : count * 2 : 2], refs[count * 2]
    base = 0
    for left, right, (tall, wide) in zip(lefts, rights, widths):
        half = wide // 2
        piece = 384
        for block in range(0, tall, 768):
            turned = left[:, block : block + 768].T
            for part in range(half // piece):
                start = pl.multiple_of(bits[0] * half + part * piece, LANES)
                product = nn(turned, right[:, pl.ds(start, piece)])
                size = tall // splits // 2
                for step in range(768 // size):
                    row = block + step * size
                    owner, side = row // (2 * size), (row // size) % 2
                    index = [side ^ bits[1]]
                    for level in range(splits.bit_length() - 1):
                        index.append(((owner >> level) & 1) ^ bits[2 + level])
                    target = base + part * size
                    out[(*index, slice(target, target + size), slice(None))] = product[
                        step * size : (step + 1) * size
                    ].astype(BF16)
        base += (half // piece) * (tall // splits // 2)


def scatter_products(bits, pairs, splits):
    levels = splits.bit_length() - 1
    rows = sum(
        (right.shape[1] // 768) * (left.shape[1] // splits // 2) for left, right in pairs
    )
    shape = (2,) * (levels + 1) + (rows, 384)
    operands = [array for pair in pairs for array in pair]
    widths = tuple((left.shape[1], right.shape[1]) for left, right in pairs)
    (out,) = call(
        functools.partial(scatter_body, widths=widths, splits=splits),
        (1,),
        (bits,),
        [whole(a) for a in operands],
        [out_whole(shape, BF16)],
        flops=sum(left.shape[0] * tall * wide for (left, _), (tall, wide) in zip(pairs, widths)),
        moved=2 * sum(a.size for a in operands) + 2 * math.prod(shape),
    )
    return out


def swap(value, axis, bit):
    count = lax.axis_size(axis)
    return lax.ppermute(value, axis, [(i, i ^ (1 << bit)) for i in range(count)])


def shift(value, axis, by):
    count = lax.axis_size(axis)
    pairs = [(i, i + by) for i in range(count) if 0 <= i + by < count]
    return lax.ppermute(value, axis, pairs)


def reduce_products(bits_of, pairs, levels):
    send = scatter_products(bits_of(1), pairs, 1 << levels)
    came = swap(send, "batch", 0)
    kept = scatter_products(bits_of(0), pairs, 1 << levels)
    for axis, bit in [("batch", 1)] + [("seq", level) for level in range(levels)]:
        low = kept[1] + came[1] if came is not None else kept[1]
        kept = kept[0].astype(F32) + came[0].astype(F32)
        came = swap(low.astype(BF16), axis, bit)
    return kept + came.astype(F32)


def gather_quarters(quarter):
    low = quarter.astype(BF16)
    mine = lax.axis_index("batch")
    other = swap(low, "batch", 1)
    upper = (mine & 2) > 0
    both = jnp.stack([jnp.where(upper, other, low), jnp.where(upper, low, other)])
    across = swap(both, "batch", 0)
    odd = (mine & 1) > 0
    return jnp.stack([jnp.where(odd, across, both), jnp.where(odd, both, across)], axis=1).astype(F32)


def cut_square(quarters, start, size):
    block = quarters[:, :, start : start + size]
    return block.transpose(0, 2, 1, 3).reshape(2 * size, 768)


def cut_wide(quarters, start, size):
    block = quarters[:, :, start : start + 4 * size].reshape(2, 2, 4, size, 384)
    return block.transpose(0, 3, 1, 2, 4).reshape(2 * size, 3072)


def device_step(
    inputs, lengths, cotangent,
    local_query, local_query_bias, local_key, local_value, local_value_bias,
    local_output, local_output_bias, pooled_query, pooled_query_bias,
    pooled_output, pooled_output_bias, conv_key, conv_value, conv_value_bias,
    norm_gain, norm_shift, expand_weight, expand_bias, reduce_weight, reduce_bias,
    final_gain, final_shift,
):
    docs, rows, width = inputs.shape
    devices = lax.axis_size("seq")
    me = lax.axis_index("seq")
    half = lax.axis_index("batch")
    levels = devices.bit_length() - 1
    size = rows // STRIDE
    offset = me * rows
    reach = -(-REACH // size)
    gathered = devices <= 2 * reach
    base = jnp.where(gathered, 0, offset // STRIDE - reach * size)
    place = jnp.concatenate([offset[None], lengths, base[None]]).astype(jnp.int32)

    def line(vector):
        return vector[None]

    taps_key, taps_value = conv_key.T, conv_value.T

    left = shift(inputs[:, rows - HALF :], "seq", 1)
    right = shift(inputs[:, :HALF], "seq", -1)
    q, kx, vx, pooled = project(
        place, inputs, left, right, local_query, line(local_query_bias), local_key, local_value,
        line(local_value_bias), taps_key, taps_value, line(conv_value_bias),
    )

    own = [pooled[:, which][None] for which in range(2)]
    if gathered:
        orders = ([2, 1, 0], [0, 2, 1]) if levels == 3 else (list(range(levels)),) * 2
        pieces, slots = [], []
        for which in range(2):
            have, relative, got = own[which], [0], [own[which]]
            for bit in orders[which]:
                came = swap(have, "seq", bit)
                got.append(came)
                relative = relative + [r ^ (1 << bit) for r in relative]
                if bit != orders[which][-1]:
                    have = jnp.concatenate([have, came])
            pieces.append(got)
            slots.append(me ^ jnp.array(relative, jnp.int32))
        slots = jnp.stack(slots)
    else:
        pieces = [
            [own[which]]
            + [
                shift(own[which], "seq", sign * distance)
                for distance in range(1, reach + 1)
                for sign in (1, -1)
            ]
            for which in range(2)
        ]
        spots = [reach] + [
            reach - sign * distance for distance in range(1, reach + 1) for sign in (1, -1)
        ]
        slots = jnp.array([spots, spots], jnp.int32)

    mix_one, probs_one, middle, middle_low, q2 = local_forward(
        place, q, kx, vx, inputs, local_output, line(local_output_bias),
        pooled_query, line(pooled_query_bias),
    )
    keys, values, probs_two, mix_two, summed = pooled_forward(
        place, slots, pieces[0], pieces[1], q2, middle, pooled_output, line(pooled_output_bias)
    )
    (
        outputs, normed_low, hidden, grad_branch, grad_pre, grad_summed, grad_second, grad_mix_two,
        vec_feed, vec_wide,
    ) = feed(
        place, summed, cotangent, expand_weight, line(expand_bias), reduce_weight,
        line(reduce_bias), line(norm_gain), line(norm_shift), line(final_gain),
        line(final_shift), pooled_output,
    )

    fast = devices == 8 and width == 768 and lax.axis_size("batch") == 4
    bit_list = [half >> 1 & 1] + [me >> level & 1 for level in range(levels)]

    def bits_of(flip):
        return jnp.stack([(half & 1) ^ flip] + bit_list).astype(jnp.int32)

    flat = docs * rows

    def tokens(array):
        return array.reshape(flat, array.shape[-1])

    pairs_feed = [(normed_low, grad_pre), (hidden, grad_branch)]
    if fast:
        sum_feed = reduce_products(bits_of, pairs_feed, levels)

    if gathered:
        back = ([0, 1, 2], [1, 2, 0]) if levels == 3 else (list(range(levels)),) * 2
        places = []
        for which in range(2):
            relative = jnp.arange(devices, dtype=jnp.int32) ^ me
            index = 0
            for bit in back[which]:
                index = index * 2 + (relative >> bit & 1)
            places.append(index)
        places = jnp.stack(places)
    else:
        places = jnp.tile(jnp.arange(2 * reach + 1, dtype=jnp.int32)[None], (2, 1))
    grad_q2, grad_keys, grad_values = pooled_backward(
        places, q2, keys, values, probs_two, grad_mix_two, size
    )

    pooled_grads = []
    if gathered:
        for which, part in enumerate((grad_keys, grad_values)):
            kept = part.reshape((2,) * levels + part.shape[1:])
            came = swap(kept[1], "seq", back[which][0])
            kept = kept[0]
            for bit in back[which][1:]:
                low = (kept[1].astype(F32) + came[1].astype(F32)).astype(BF16)
                kept = kept[0].astype(F32) + came[0].astype(F32)
                came = swap(low, "seq", bit)
            pooled_grads += [kept, came]
    else:
        for part in (grad_keys, grad_values):
            total = part[reach].astype(F32)
            for distance in range(1, reach + 1):
                total = total + shift(part[reach - distance], "seq", -distance).astype(F32)
                total = total + shift(part[reach + distance], "seq", distance).astype(F32)
            pooled_grads += [total, jnp.zeros_like(part[reach])]

    dq, own_grads, low_left, low_right, grad_middle, grad_first, vec_local = local_backward(
        place, q, kx, vx, probs_one, grad_q2, grad_summed, pooled_query, local_output
    )
    from_left = shift(low_right, "seq", 1)
    from_right = shift(low_left, "seq", -1)
    pairs_middle = [
        (tokens(mix_two), grad_second),
        (tokens(middle_low), tokens(grad_q2)),
        (tokens(mix_one), tokens(grad_first)),
        (tokens(inputs), tokens(dq)),
    ]
    if fast:
        sum_middle = reduce_products(bits_of, pairs_middle, levels)

    heads = [
        (pooled_grads[2 * which][:, :1].astype(F32) + pooled_grads[2 * which + 1][:, :1].astype(F32))
        for which in range(2)
    ]
    after = shift(jnp.stack(heads).astype(BF16), "seq", -1)
    grad_k, grad_v, input_grad, vec_input = input_gradients(
        place, own_grads, from_left, from_right, pooled_grads, [after[0], after[1]], kx, vx,
        taps_key, taps_value, dq, grad_middle, local_query, local_key, local_value,
    )
    pairs_last = [(tokens(inputs), tokens(grad_k)), (tokens(inputs), tokens(grad_v))]

    if fast:
        sum_last = reduce_products(bits_of, pairs_last, levels)
        feed_quarters = gather_quarters(sum_feed)
        middle_quarters = gather_quarters(sum_middle)
        last_quarters = gather_quarters(sum_last)
        small = width // devices // 2
        grad_expand = cut_wide(feed_quarters, 0, small)
        grad_reduce = cut_square(feed_quarters, 4 * small, 4 * small)
        grad_po, grad_pq, grad_lo, grad_lq = [
            cut_square(middle_quarters, index * small, small) for index in range(4)
        ]
        grad_lk, grad_lv = [cut_square(last_quarters, index * small, small) for index in range(2)]
    else:

        def plain(pair):
            product = tn(*pair)
            part = lax.psum_scatter(product, "seq", scatter_dimension=0, tiled=True)
            return lax.psum(part.astype(BF16), "batch").astype(F32)

        grad_expand, grad_reduce = map(plain, pairs_feed)
        grad_po, grad_pq, grad_lo, grad_lq = map(plain, pairs_middle)
        grad_lk, grad_lv = map(plain, pairs_last)

    vectors = jnp.concatenate(
        [vec_feed, vec_local, vec_input, vec_wide.reshape(-1, width)], axis=0
    )
    vectors = lax.psum(vectors, ("seq", "batch"))
    share = width // devices
    mine = lax.dynamic_slice_in_dim(vectors, me * share, share, axis=1)
    wide = vectors[32:].reshape(-1)
    wide_share = wide.shape[0] // devices
    grad_eb = lax.dynamic_slice_in_dim(wide, me * wide_share, wide_share, axis=0)
    (fg, fs, rb, ng, ns, pob) = [mine[index] for index in range(6)]
    pqb, lob = mine[8], mine[9]
    grad_ck = mine[16 : 16 + KER].T
    grad_cv = mine[16 + KER : 16 + 2 * KER].T
    cvb, lqb, lvb = mine[26], mine[27], mine[28]
    return (
        outputs, input_grad,
        grad_lq, lqb, grad_lk, grad_lv, lvb, grad_lo, lob, grad_pq, pqb, grad_po, pob,
        grad_ck, grad_cv, cvb, ng, ns, grad_expand, grad_eb, grad_reduce, rb, fg, fs,
    )


def solution(mesh):
    vector = P("seq")
    matrix = P("seq", None)
    return jax.shard_map(
        device_step,
        mesh=mesh,
        in_specs=(P("batch", "seq", None), P("batch"), P("batch", "seq", None)) + (P(),) * 22,
        out_specs=(
            P("batch", "seq", None), P("batch", "seq", None),
            matrix, vector, matrix, matrix, vector, matrix, vector, matrix, vector, matrix, vector,
            matrix, matrix, vector, vector, vector, matrix, vector, matrix, vector, vector, vector,
        ),
        check_vma=False,
    )
```

```python
import functools
import math

import jax
import jax.numpy as jnp
from jax import lax
from jax.experimental import pallas as pl
from jax.experimental.pallas import tpu as pltpu
from jax.sharding import PartitionSpec as P

HEADS = 12
HD = 64
WIN = 128
PWIN = 512
KER = 5
STRIDE = 4
HALF = WIN // 2
REACH = PWIN // 2
NEGATIVE = -1e30
SCALE = 1.0 / math.sqrt(HD)
EPSILON = 1e-05
LANES = 128
TILE = 128
ROWS = 128
CHUNK = 256
F32 = jnp.float32
BF16 = jnp.bfloat16


def nn(left, right):
    return jnp.dot(left, right, preferred_element_type=F32)


def nt(left, right):
    return lax.dot_general(left, right, (((1,), (1,)), ((), ())), preferred_element_type=F32)


def tn(left, right):
    return lax.dot_general(left, right, (((0,), (0,)), ((), ())), preferred_element_type=F32)


def column_sum(block):
    return jnp.sum(block.astype(F32), axis=0, keepdims=True)


def call(body, grid, scalars, inputs, outputs, scratch=(), flops=0, moved=0, exps=0, spare=6):
    single = math.prod(grid) == 1
    used = spare * 2**20

    def spec(shape, dtype, block, index):
        nonlocal used
        fixed = single or tuple(block) == tuple(shape)
        used += math.prod(block) * jnp.dtype(dtype).itemsize * (1 if fixed else 2)
        mode = pl.Buffered(1) if fixed else None
        return pl.BlockSpec(block, index, pipeline_mode=mode)

    in_specs = [spec(a.shape, a.dtype, block, index) for a, block, index in inputs]
    out_specs = [spec(shape, dtype, block, index) for shape, dtype, block, index in outputs]
    for item in scratch:
        used += math.prod(item.shape) * jnp.dtype(item.dtype).itemsize
    return pl.pallas_call(
        body,
        grid_spec=pltpu.PrefetchScalarGridSpec(
            num_scalar_prefetch=len(scalars),
            grid=grid,
            in_specs=in_specs,
            out_specs=out_specs,
            scratch_shapes=list(scratch),
        ),
        out_shape=[jax.ShapeDtypeStruct(shape, dtype) for shape, dtype, _, _ in outputs],
        compiler_params=pltpu.CompilerParams(
            dimension_semantics=("arbitrary",) * len(grid), vmem_limit_bytes=used
        ),
        cost_estimate=pl.CostEstimate(flops=1000, bytes_accessed=1000, transcendentals=0),
    )(*scalars, *[array for array, _, _ in inputs])


def whole(array):
    zeros = (0,) * array.ndim
    return (array, array.shape, lambda *_: zeros)


def by_doc(array):
    zeros = (0,) * (array.ndim - 1)
    return (array, (1,) + array.shape[1:], lambda doc, *_: (doc,) + zeros)


def one_doc(array, doc):
    zeros = (0,) * (array.ndim - 1)
    return (array, (1,) + array.shape[1:], lambda *_: (doc,) + zeros)


def out_doc(shape, dtype):
    zeros = (0,) * (len(shape) - 1)
    return (shape, dtype, (1,) + tuple(shape[1:]), lambda doc, *_: (doc,) + zeros)


def out_whole(shape, dtype):
    zeros = (0,) * len(shape)
    return (shape, dtype, shape, lambda *_: zeros)


def sync(*values):
    return lax.optimization_barrier(values)


def stack_heads(block):
    lane = lax.broadcasted_iota(jnp.int32, block.shape, 1)
    zero = jnp.zeros_like(block)
    return jnp.concatenate(
        [jnp.where(lane < HD, block, zero), jnp.where(lane < HD, zero, block)], axis=0
    )


def unstack(block):
    joined = jnp.concatenate([block[:HD, :TILE], block[HD:, TILE:]], axis=0)
    return joined.T


def positions(shape, dim):
    return lax.broadcasted_iota(jnp.int32, shape, dim)


def project_body(place, x, left, right, wq, bq, wk, wv, bv, ck, cv, bcv, q, kx, vx, pooled, rows):
    doc = pl.program_id(0)
    offset, length = place[0], place[1 + doc]
    own = x[0]
    q[0] = (nn(own, wq[...]) + bq[...]).astype(BF16)
    extended = jnp.concatenate([left[0], own, right[0]], axis=0)
    spot = offset - HALF + positions((extended.shape[0], 1), 0)
    valid = (spot >= 0) & (spot < length)
    count = pooled.shape[2]
    for which, (weight, bias, taps, out) in enumerate(((wk, None, ck, kx), (wv, bv, cv, vx))):
        value = nn(extended, weight[...])
        if bias is not None:
            value = value + bias[...]
        value = value.astype(BF16)
        out[0] = value
        masked = jnp.where(valid, value.astype(F32), 0.0)
        for group in range(value.shape[1] // LANES):
            lanes = slice(group * LANES, (group + 1) * LANES)
            rows[group] = masked[:, lanes]
            total = jnp.zeros((count, LANES), F32)
            for tap in range(KER):
                start = HALF - KER // 2 + tap
                read = rows[group, pl.ds(start, count, stride=STRIDE), :]
                total = total + read * taps[tap : tap + 1, lanes]
            if which == 1:
                total = total + bcv[:, lanes]
            pooled[0, which, :, lanes] = total.astype(BF16)


def project(place, x, left, right, wq, bq, wk, wv, bv, ck, cv, bcv):
    docs, rows, width = x.shape
    extended = rows + WIN
    return call(
        project_body,
        (docs,),
        (place,),
        [by_doc(x), by_doc(left), by_doc(right)]
        + [whole(a) for a in (wq, bq, wk, wv, bv, ck, cv, bcv)],
        [
            out_doc((docs, rows, width), BF16),
            out_doc((docs, extended, width), BF16),
            out_doc((docs, extended, width), BF16),
            out_doc((docs, 2, rows // STRIDE, width), BF16),
        ],
        [pltpu.VMEM((width // LANES, extended, LANES), F32)],
        flops=2 * docs * (rows + 2 * extended) * width * width,
        moved=10**7,
    )


def local_bias(tile, offset, length):
    shape = (TILE + WIN, TILE)
    key = positions(shape, 0)
    query = positions(shape, 1)
    spot = offset + tile * TILE - HALF + key
    allowed = (
        (key >= query) & (key < query + WIN) & (spot >= 0) & (spot < length)
    ) | (key == query + HALF)
    return jnp.where(allowed, 0.0, NEGATIVE)


def softmax_columns(scores):
    top = jnp.max(scores, axis=0, keepdims=True)
    grown = jnp.exp(scores - top)
    return grown * (1.0 / jnp.sum(grown, axis=0, keepdims=True))


def local_forward_body(place, q, kx, vx, mix, probs, *, doc):
    offset, length = place[0], place[1 + doc]
    span = TILE + WIN
    for tile in range(q.shape[1] // TILE):
        half_bias = local_bias(tile, offset, length)
        bias = jnp.concatenate([half_bias, half_bias], axis=1)
        first = tile * TILE
        for pair in range(q.shape[2] // LANES):
            lanes = slice(pair * LANES, (pair + 1) * LANES)
            queries = stack_heads(q[0, first : first + TILE, lanes]) * SCALE
            scores = nt(kx[0, first : first + span, lanes], queries) + bias
            chance = softmax_columns(scores)
            probs[pair, tile] = chance
            turned = vx[0, first : first + span, lanes].T
            mixed = nn(turned, chance.astype(BF16))
            mix[first : first + TILE, lanes] = unstack(mixed).astype(BF16)


def local_forward(place, q, kx, vx, doc):
    _, rows, width = q.shape
    pairs, tiles, span = width // LANES, rows // TILE, TILE + WIN
    return call(
        functools.partial(local_forward_body, doc=doc),
        (1,),
        (place,),
        [one_doc(a, doc) for a in (q, kx, vx)],
        [
            out_whole((rows, width), BF16),
            out_whole((pairs, tiles, span, 2 * TILE), F32),
        ],
        flops=rows * width * 4 * 2 * span,
        moved=10**7,
        exps=rows * HEADS * span,
    )


def middle_body(place, x, wo, bo, wpq, bpq, *refs):
    docs, rows = x.shape[0], x.shape[1]
    mixes, (mix, middle, middle_low, q2) = refs[:docs], refs[docs:]
    for doc in range(docs):
        mix[doc] = mixes[doc][...]
    flat = docs * rows
    branch = nn(mix[...].reshape(flat, x.shape[2]), wo[...]) + bo[...]
    total = x[...].reshape(flat, x.shape[2]).astype(F32) + branch
    middle[...] = total.reshape(middle.shape)
    low = total.astype(BF16)
    middle_low[...] = low.reshape(middle_low.shape)
    q2[...] = (nn(low, wpq[...]) + bpq[...]).astype(BF16).reshape(q2.shape)


def middle_forward(place, x, wo, bo, wpq, bpq, mixes):
    docs, rows, width = x.shape
    return call(
        middle_body,
        (1,),
        (place,),
        [whole(a) for a in (x, wo, bo, wpq, bpq, *mixes)],
        [
            out_whole((docs, rows, width), BF16),
            out_whole((docs, rows, width), F32),
            out_whole((docs, rows, width), BF16),
            out_whole((docs, rows, width), BF16),
        ],
        flops=docs * rows * width * width * 4,
        moved=10**7,
    )


def attention_back(keys, values, queries, grads, chance):
    stacked_grads = stack_heads(grads)
    stacked_queries = stack_heads(queries)
    grad_chance = nt(values, stacked_grads * SCALE)
    dots = jnp.sum(chance * grad_chance, axis=0, keepdims=True)
    grad_raw = (chance * (grad_chance - dots)).astype(BF16)
    grad_keys = nn(grad_raw, stacked_queries)
    grad_values = nn(chance.astype(BF16), stacked_grads)
    grad_queries = unstack(nn(keys.T, grad_raw))
    return grad_queries, grad_keys, grad_values


def first_back_body(place, gq2, gsum, wpq, wo, gmid, gfirst, gmix, vec):
    docs, rows, width = gsum.shape
    flat = docs * rows
    grads = gq2[...].reshape(flat, width)
    total = gsum[...].reshape(flat, width) + nt(grads, wpq[...])
    gmid[...] = total.reshape(gmid.shape)
    low = total.astype(BF16)
    gfirst[...] = low
    gmix[...] = nt(low, wo[...]).astype(BF16).reshape(gmix.shape)
    vec[...] = jnp.zeros_like(vec)
    vec[0:1] = column_sum(grads)
    vec[1:2] = column_sum(low)


def first_backward(place, gq2, gsum, wpq, wo):
    docs, rows, width = gsum.shape
    return call(
        first_back_body,
        (1,),
        (place,),
        [whole(a) for a in (gq2, gsum, wpq, wo)],
        [
            out_whole((docs, rows, width), F32),
            out_whole((docs * rows, width), BF16),
            out_whole((docs, rows, width), BF16),
            out_whole((8, width), F32),
        ],
        flops=docs * rows * width * width * 4,
        moved=10**7,
    )


def local_backward_body(place, q, kx, vx, gmix, probs, *refs, doc):
    earlier = refs[: len(refs) - 6]
    dq, own, low_left, low_right, dk, dv = refs[len(refs) - 6 :]
    rows = q.shape[1]
    for old, new in zip(earlier, (dq, own, low_left, low_right)):
        new[:doc] = old[...]
    span = TILE + WIN
    dk[...] = jnp.zeros_like(dk)
    dv[...] = jnp.zeros_like(dv)
    for tile in range(rows // TILE):
        first = tile * TILE
        for pair in range(q.shape[2] // LANES):
            lanes = slice(pair * LANES, (pair + 1) * LANES)
            grad_q, grad_k, grad_v = attention_back(
                kx[0, first : first + span, lanes],
                vx[0, first : first + span, lanes],
                q[0, first : first + TILE, lanes],
                gmix[0, first : first + TILE, lanes],
                probs[pair, tile],
            )
            dq[doc, first : first + TILE, lanes] = grad_q.astype(BF16)
            dk[first : first + span, lanes] += grad_k
            dv[first : first + span, lanes] += grad_v
    for which, part in enumerate((dk, dv)):
        own[doc, which] = part[HALF : HALF + rows]
        low_left[doc, which] = part[:HALF].astype(BF16)
        low_right[doc, which] = part[HALF + rows :].astype(BF16)


def local_backward(place, q, kx, vx, gmix, probs, doc, earlier=()):
    _, rows, width = q.shape
    span = TILE + WIN
    return call(
        functools.partial(local_backward_body, doc=doc),
        (1,),
        (place,),
        [one_doc(a, doc) for a in (q, kx, vx, gmix)] + [whole(a) for a in (probs, *earlier)],
        [
            out_whole((doc + 1, rows, width), BF16),
            out_whole((doc + 1, 2, rows, width), F32),
            out_whole((doc + 1, 2, HALF, width), BF16),
            out_whole((doc + 1, 2, HALF, width), BF16),
        ],
        [
            pltpu.VMEM((rows + WIN, width), F32),
            pltpu.VMEM((rows + WIN, width), F32),
        ],
        flops=rows * width * 8 * 2 * span,
        moved=10**7,
    )


def pooled_forward_body(place, slots, *refs, pieces):
    key_pieces = refs[:pieces]
    value_pieces = refs[pieces : 2 * pieces]
    q2, middle, wpo, bpo, keys, values, probs, mix, summed, bias = refs[2 * pieces :]
    doc, pair = pl.program_id(0), pl.program_id(1)
    offset, length, base = place[0], place[1 + doc], place[1 + pl.num_programs(0)]
    tiles = q2.shape[1] // TILE
    count = keys.shape[1]

    @pl.when(pair == 0)
    def _():
        for where, group, out in ((0, key_pieces, keys), (1, value_pieces, values)):
            at = 0
            for piece in group:
                size = piece.shape[2]
                for block in range(piece.shape[0]):
                    spot = pl.multiple_of(slots[where, at] * size, size)
                    out[0, pl.ds(spot, size), :] = piece[block, 0]
                    at += 1
        for tile in range(tiles):
            shape = (count, TILE)
            spot = base + positions(shape, 0)
            centre = offset // STRIDE + (tile * TILE + positions(shape, 1)) // STRIDE
            allowed = (
                (spot >= centre - REACH)
                & (spot < centre + REACH)
                & (spot >= 0)
                & (spot * STRIDE < length)
            ) | (spot == centre)
            bias[tile] = jnp.where(allowed, 0.0, NEGATIVE)

    lanes = pl.ds(pl.multiple_of(pair * LANES, LANES), LANES)
    pair_keys = keys[0, :, lanes]
    turned = values[0, :, lanes].T
    for tile in range(tiles):
        first = tile * TILE
        queries = stack_heads(q2[0, first : first + TILE, :]) * SCALE
        half_bias = bias[tile]
        scores = nt(pair_keys, queries) + jnp.concatenate([half_bias, half_bias], axis=1)
        chance = softmax_columns(scores)
        probs[0, 0, tile] = chance
        mixed = nn(turned, chance.astype(BF16))
        mix[0, first : first + TILE, lanes] = unstack(mixed).astype(BF16)

    @pl.when(pair == pl.num_programs(1) - 1)
    def _():
        summed[0] = middle[0] + (nn(mix[0], wpo[...]) + bpo[...])


def pooled_forward(place, slots, key_pieces, value_pieces, q2, middle, wpo, bpo):
    docs, rows, width = q2.shape
    pairs, tiles = width // LANES, rows // TILE
    size = key_pieces[0].shape[2]
    count = size * slots.shape[1]

    def piece(array):
        return (array, (array.shape[0], 1, size, width), lambda doc, *_: (0, doc, 0, 0))

    return call(
        functools.partial(pooled_forward_body, pieces=len(key_pieces)),
        (docs, pairs),
        (place, slots),
        [piece(a) for a in key_pieces + value_pieces]
        + [
            (q2, (1, rows, LANES), lambda doc, pair, *_: (doc, 0, pair)),
            by_doc(middle),
            whole(wpo),
            whole(bpo),
        ],
        [
            out_doc((docs, count, width), BF16),
            out_doc((docs, count, width), BF16),
            (
                (docs, pairs, tiles, count, 2 * TILE),
                F32,
                (1, 1, tiles, count, 2 * TILE),
                lambda doc, pair, *_: (doc, pair, 0, 0, 0),
            ),
            out_doc((docs, rows, width), BF16),
            out_doc((docs, rows, width), F32),
        ],
        [pltpu.VMEM((tiles, count, TILE), F32)],
        flops=docs * rows * width * (2 * width + 4 * 2 * count),
        moved=3 * 10**7,
        exps=docs * rows * HEADS * count,
    )


def pooled_backward_body(
    places, token, q2, keys, values, probs, grads, dq, dk_kept, dk_sent, dv_kept, dv_sent, sums
):
    size = dk_kept.shape[2]
    total = None
    for tile in range(q2.shape[1] // TILE):
        first = tile * TILE
        grad_q, *added = attention_back(
            keys[0], values[0], q2[0, first : first + TILE], grads[0, first : first + TILE],
            probs[0, 0, tile],
        )
        dq[0, first : first + TILE] = grad_q.astype(BF16)
        total = added if total is None else [a + b for a, b in zip(total, added)]
    half = dk_kept.shape[0]
    for which, (kept, sent) in enumerate(((dk_kept, dk_sent), (dv_kept, dv_sent))):
        sums[...] = total[which]
        for block in range(half + sent.shape[0]):
            start = pl.multiple_of(places[which, block] * size, size)
            part = sums[pl.ds(start, size), :]
            if block < half:
                kept[block, 0] = part
            else:
                sent[block - half, 0] = part.astype(BF16)


def pooled_backward(places, token, q2, keys, values, probs, grads, size, kept):
    docs, rows, width = q2.shape
    count = keys.shape[1]
    blocks = count // size
    tiles = rows // TILE

    def lanes_of(array):
        return (array, (1, array.shape[1], LANES), lambda doc, pair, *_: (doc, 0, pair))

    def spread(number, dtype):
        return (
            (number, docs, size, width),
            dtype,
            (number, 1, size, LANES),
            lambda doc, pair, *_: (0, doc, 0, pair),
        )

    return call(
        pooled_backward_body,
        (docs, width // LANES),
        (places, token),
        [
            lanes_of(q2),
            lanes_of(keys),
            lanes_of(values),
            (
                probs,
                (1, 1, tiles, count, 2 * TILE),
                lambda doc, pair, *_: (doc, pair, 0, 0, 0),
            ),
            lanes_of(grads),
        ],
        [
            ((docs, rows, width), BF16, (1, rows, LANES), lambda doc, pair, *_: (doc, 0, pair)),
            spread(kept, F32),
            spread(blocks - kept, BF16),
            spread(kept, F32),
            spread(blocks - kept, BF16),
        ],
        [pltpu.VMEM((count, LANES), F32)],
        flops=docs * rows * width * 8 * 2 * count,
        moved=2 * 10**7,
    )


def feed_body(
    place, summed, cotangent, we, be, wr, br, ng, ns, fg, fs, wpo,
    outputs, normed_low, hidden, grad_branch, grad_pre, grad_summed, grad_second, grad_mix,
    vec, vec_wide,
    normed, slope, work, unit,
):
    docs, rows = cotangent.shape[0], cotangent.shape[1]
    width = summed.shape[2]
    wide = we.shape[1]
    steps = rows // ROWS
    blocks = [(doc, step * ROWS, doc * rows + step * ROWS) for doc in range(docs) for step in range(steps)]

    def normal(value):
        centred = value - jnp.mean(value, axis=-1, keepdims=True)
        scale = lax.rsqrt(jnp.mean(centred * centred, axis=-1, keepdims=True) + EPSILON)
        return centred * scale, scale

    scales = []
    for doc, start, row in blocks:
        norm, scale = normal(summed[doc, start : start + ROWS])
        scales.append(scale)
        unit[row : row + ROWS] = norm
        full = norm * ng[...] + ns[...]
        normed[row : row + ROWS] = full
        normed_low[row : row + ROWS] = full.astype(BF16)

    def expand(index, _):
        part = pl.ds(pl.multiple_of(index * CHUNK, CHUNK), CHUNK)
        pre = nn(normed_low[...], we[:, part]) + be[:, part]
        cdf = 0.5 * (1.0 + lax.erf(pre * math.sqrt(0.5)))
        hidden[:, part] = (pre * cdf).astype(BF16)
        slope[:, part] = cdf + pre * (jnp.exp(pre * pre * -0.5) * (1.0 / math.sqrt(2.0 * math.pi)))
        return 0

    lax.fori_loop(0, wide // CHUNK, expand, 0)

    for start in range(0, width, CHUNK):
        part = slice(start, start + CHUNK)
        work[:, part] = normed[:, part] + (nn(hidden[...], wr[:, part]) + br[:, part])

    sums = [jnp.zeros((1, width), F32) for _ in range(6)]
    for doc, start, row in blocks:
        norm, scale = normal(work[row : row + ROWS])
        spot = place[0] + start + positions((ROWS, 1), 0)
        valid = (spot < place[1 + doc]).astype(F32)
        outputs[doc, start : start + ROWS] = (valid * (norm * fg[...] + fs[...])).astype(BF16)
        error = valid * cotangent[doc, start : start + ROWS].astype(F32)
        sums[0] += column_sum(error * norm)
        sums[1] += column_sum(error)
        scaled = error * fg[...]
        rest = (
            scaled
            - jnp.mean(scaled, axis=-1, keepdims=True)
            - norm * jnp.mean(scaled * norm, axis=-1, keepdims=True)
        ) * scale
        work[row : row + ROWS] = rest
        low = rest.astype(BF16)
        grad_branch[row : row + ROWS] = low
        sums[2] += column_sum(low)

    def reduce(index, _):
        part = pl.ds(pl.multiple_of(index * CHUNK, CHUNK), CHUNK)
        low = (nt(grad_branch[...], wr[part, :]) * slope[:, part]).astype(BF16)
        grad_pre[:, part] = low
        vec_wide[:, part] = column_sum(low)
        return 0

    lax.fori_loop(0, wide // CHUNK, reduce, 0)

    for start in range(0, width, CHUNK):
        part = slice(start, start + CHUNK)
        work[:, part] += nt(grad_pre[...], we[part, :])

    for (doc, start, row), scale in zip(blocks, scales):
        error = work[row : row + ROWS]
        norm = unit[row : row + ROWS]
        sums[3] += column_sum(error * norm)
        sums[4] += column_sum(error)
        scaled = error * ng[...]
        grad = (
            scaled
            - jnp.mean(scaled, axis=-1, keepdims=True)
            - norm * jnp.mean(scaled * norm, axis=-1, keepdims=True)
        ) * scale
        grad_summed[doc, start : start + ROWS] = grad
        low = grad.astype(BF16)
        grad_second[row : row + ROWS] = low
        sums[5] += column_sum(low)
        grad_mix[doc, start : start + ROWS] = nt(low, wpo[...]).astype(BF16)
    for index, value in enumerate(sums):
        vec[index : index + 1] = value
    vec[6:8] = jnp.zeros((2, width), F32)


def feed(place, summed, cotangent, we, be, wr, br, ng, ns, fg, fs, wpo):
    docs, rows, width = summed.shape
    wide = we.shape[1]
    tokens = docs * rows
    return call(
        feed_body,
        (1,),
        (place,),
        [whole(a) for a in (summed, cotangent, we, be, wr, br, ng, ns, fg, fs, wpo)],
        [
            out_whole((docs, rows, width), BF16),
            out_whole((tokens, width), BF16),
            out_whole((tokens, wide), BF16),
            out_whole((tokens, width), BF16),
            out_whole((tokens, wide), BF16),
            out_whole((docs, rows, width), F32),
            out_whole((tokens, width), BF16),
            out_whole((docs, rows, width), BF16),
            out_whole((8, width), F32),
            out_whole((1, wide), F32),
        ],
        [
            pltpu.VMEM((tokens, width), F32),
            pltpu.VMEM((tokens, wide), F32),
            pltpu.VMEM((tokens, width), F32),
            pltpu.VMEM((tokens, width), F32),
        ],
        flops=2 * tokens * width * (4 * wide + width),
        moved=3 * 10**7,
        exps=2 * tokens * wide,
    )


def key_value_body(place, *refs, docs):
    (gk_kept, gk_came, gv_kept, gv_came, gk_next, gv_next, kx, vx, ck, cv) = refs[:10]
    own, from_left, from_right, dq = refs[10:14]
    gk, gv, vec, rows_in, pooled, total = refs[14:]
    offset = place[0]
    rows, width = gk.shape[0] // docs, gk.shape[1]
    count = rows // STRIDE
    vec[...] = jnp.zeros_like(vec)
    for doc in range(docs):
        length = place[1 + doc]
        spot = offset - HALF + positions((rows + WIN, 1), 0)
        valid = (spot >= 0) & (spot < length)
        first = doc * rows
        for which, (kept, came, after, ext, taps, out, row) in enumerate(
            (
                (gk_kept, gk_came, gk_next, kx, ck, gk, 0),
                (gv_kept, gv_came, gv_next, vx, cv, gv, KER),
            )
        ):
            pooled[:count] = kept[doc].astype(F32) + came[doc].astype(F32)
            pooled[count:] = jnp.broadcast_to(after[doc].astype(F32), (8, width))
            masked = jnp.where(valid, ext[doc].astype(F32), 0.0)
            for group in range(width // LANES):
                lanes = slice(group * LANES, (group + 1) * LANES)
                grown = pooled[:count, lanes]
                shifted = pooled[1 : count + 1, lanes]
                rows_in[group] = masked[:, lanes]
                for tap in range(KER):
                    start = HALF - KER // 2 + tap
                    read = rows_in[group, pl.ds(start, count, stride=STRIDE), :]
                    vec[row + tap : row + tap + 1, lanes] += column_sum(grown * read)
                if which == 1:
                    vec[2 * KER : 2 * KER + 1, lanes] += column_sum(grown)
                total[group] = own[doc, which, :, lanes]
                total[group, :HALF] += from_left[doc, which, :, lanes].astype(F32)
                total[group, rows - HALF :] += from_right[doc, which, :, lanes].astype(F32)
                for phase, terms in enumerate(
                    (
                        ((2, grown),),
                        ((3, grown),),
                        ((4, grown), (0, shifted)),
                        ((1, shifted),),
                    )
                ):
                    part = pl.ds(phase, count, stride=STRIDE)
                    added = None
                    for tap, values in terms:
                        term = values * taps[tap : tap + 1, lanes]
                        added = term if added is None else added + term
                    inside = offset + phase + STRIDE * positions((count, 1), 0) < length
                    total[group, part, :] = total[group, part, :] + jnp.where(inside, added, 0.0)
                out[first : first + rows, lanes] = total[group].astype(BF16)
        vec[11:12] += column_sum(dq[doc])
    vec[12:13] += column_sum(gv[...])


def key_value_gradients(place, pooled_grads, next_grads, kx, vx, ck, cv, own, left, right, dq):
    docs, rows, width = dq.shape
    return call(
        functools.partial(key_value_body, docs=docs),
        (1,),
        (place,),
        [
            whole(a)
            for a in (*pooled_grads, *next_grads, kx, vx, ck, cv, own, left, right, dq)
        ],
        [out_whole((docs * rows, width), BF16)] * 2 + [out_whole((16, width), F32)],
        [
            pltpu.VMEM((width // LANES, rows + WIN, LANES), F32),
            pltpu.VMEM((rows // STRIDE + 8, width), F32),
            pltpu.VMEM((width // LANES, rows, LANES), F32),
        ],
        flops=docs * rows * width * 40,
        moved=10**7,
    )


def input_body(place, dq, gk, gv, gmid, wq, wk, wv, dx):
    total = nt(dq[...], wq[...]) + nt(gk[...], wk[...]) + nt(gv[...], wv[...])
    dx[...] = (gmid[...] + total.reshape(gmid.shape)).astype(BF16)


def input_gradient(place, dq, gk, gv, gmid, wq, wk, wv):
    docs, rows, width = gmid.shape
    (dx,) = call(
        input_body,
        (1,),
        (place,),
        [whole(a) for a in (dq, gk, gv, gmid, wq, wk, wv)],
        [out_whole((docs, rows, width), BF16)],
        flops=2 * docs * rows * width * 3 * width,
        moved=10**7,
    )
    return dx


def scatter_body(bits, *refs, kinds, order, vectors, quartered):
    count = len(kinds)
    operands = [refs[2 * index : 2 * index + 2] for index in range(count)]
    extra = refs[2 * count : 2 * count + vectors]
    rest = refs[2 * count + vectors :]
    if quartered:
        results, (ordered, rounded, *small) = (rest[0], rest[0]), rest[1:]
    else:
        results, (ordered, rounded, *small) = rest[:2], rest[2:]
    core = bits[0]
    sides = 2 if ("batch", 1) in order else 1
    owners = 8

    def start_of(which, size):
        if quartered:
            return which * size
        return pl.multiple_of((which ^ core) * size, LANES)

    def place_tile(which, side, owner, target, size, value):
        index = []
        for at, (axis, bit) in enumerate(order):
            if axis == "batch":
                index += [side, which] if quartered else [side ^ bits[1 + at]]
            else:
                index.append(((owner >> bit) & 1) ^ bits[1 + at])
        results[which][(*index, slice(target, target + size), slice(None))] = value

    base = 0
    for (left, right), kind in zip(operands, kinds):
        tall = left.shape[1]
        turned = left[...].T
        if kind == "wide":
            half = right.shape[1] // 2
            size = tall // owners // sides
            for which in range(2):
                start = start_of(which, half)
                for part in range(half // 768):
                    rounded[...] = nn(turned, right[:, pl.ds(start + part * 768, 768)]).astype(BF16)
                    for column in range(2):
                        target = base + (2 * part + column) * size
                        for owner in range(owners):
                            for side in range(sides):
                                row = (owner * sides + side) * size
                                value = rounded[row : row + size, column * 384 : column * 384 + 384]
                                place_tile(which, side, owner, target, size, value)
            base += half // 384 * size
        elif kind == "tall":
            ordered[...] = turned
            size = tall // 2 // sides
            for part in range(right.shape[1] // 768):
                product = nn(ordered[...], right[:, part * 768 : part * 768 + 768])
                rounded[...] = product.astype(BF16)
                for column in range(2):
                    owner = 2 * part + column
                    for side in range(sides):
                        for which in range(2):
                            row = start_of(which, 384) + side * size
                            value = rounded[pl.ds(row, size), column * 384 : column * 384 + 384]
                            place_tile(which, side, owner, base, size, value)
            base += size
        else:
            size = tall // owners // sides
            if quartered:
                columns = right[...]
            else:
                columns = jnp.concatenate(
                    [right[:, pl.ds(start_of(which, 384), 384)] for which in range(2)], axis=1
                )
            rounded[...] = nn(turned, columns).astype(BF16)
            for which in range(2):
                for owner in range(owners):
                    for side in range(sides):
                        row = (owner * sides + side) * size
                        value = rounded[row : row + size, which * 384 : which * 384 + 384]
                        place_tile(which, side, owner, base, size, value)
            base += size
    if vectors:
        (block,) = small
        vec_feed, vec_first, vec_input, vec_wide = extra
        for owner in range(owners):
            lanes = slice(owner * 96, owner * 96 + 96)
            block[0, owner] = jnp.zeros(block.shape[2:], F32)
            block[1, owner] = jnp.zeros(block.shape[2:], F32)
            block[0, owner, 0:8, 0:96] = vec_feed[:, lanes]
            block[0, owner, 0:8, LANES : LANES + 96] = vec_first[:, lanes]
            block[1, owner, 0:16, 0:96] = vec_input[:, lanes]
            for part in range(4):
                at = owner * 384 + part * 96
                block[0, owner, 8 + part : 9 + part, 0:96] = vec_wide[:, at : at + 96]
        for owner in range(owners):
            for which in range(2):
                place_tile(which, 0, owner, base, 16, block[which ^ core, owner].astype(BF16))


def scatter_products(bits, order, items, extra=(), quartered=False):
    sides = 2 if ("batch", 1) in order else 1
    rows = 0
    for kind, left, right in items:
        if kind == "wide":
            rows += right.shape[1] // 768 * (left.shape[1] // 8 // sides)
        elif kind == "tall":
            rows += 384 // sides
        else:
            rows += 96 // sides
    rows += 16 if extra else 0
    shape = (2,) * (len(order) + quartered) + (rows, 384)
    operands = [array for _, left, right in items for array in (left, right)]
    return call(
        functools.partial(
            scatter_body,
            kinds=tuple(kind for kind, _, _ in items),
            order=tuple(order),
            vectors=len(extra),
            quartered=quartered,
        ),
        (1,),
        (bits,),
        [whole(a) for a in (*operands, *extra)],
        [out_whole(shape, BF16)] * (1 if quartered else 2),
        [pltpu.VMEM((768, operands[0].shape[0]), BF16), pltpu.VMEM((768, 768), BF16)]
        + ([pltpu.VMEM((2, 8, 16, 384), F32)] if extra else []),
        flops=sum(2 * left.shape[0] * left.shape[1] * right.shape[1] for _, left, right in items),
        moved=2 * sum(a.size for a in operands) + 4 * math.prod(shape),
    )


def swap(value, axis, bit):
    count = lax.axis_size(axis)
    return lax.ppermute(value, axis, [(i, i ^ (1 << bit)) for i in range(count)])


def shift(value, axis, by):
    count = lax.axis_size(axis)
    pairs = [(i, i + by) for i in range(count) if 0 <= i + by < count]
    return lax.ppermute(value, axis, pairs)


def fold(kept, came):
    low = (kept[1].astype(F32) + came[1].astype(F32)).astype(BF16)
    return low, kept[0].astype(F32) + came[0].astype(F32)


def total_of(terms, *index):
    total = None
    for term in terms:
        value = term[index].astype(F32)
        total = value if total is None else total + value
    return total


def advance(terms, hop):
    came = swap(total_of(terms, 1).astype(BF16), *hop)
    return [term[0] for term in terms], came


def cut(quarters, start, size):
    return quarters[:, :, start : start + size]


def device_step(
    inputs, lengths, cotangent,
    local_query, local_query_bias, local_key, local_value, local_value_bias,
    local_output, local_output_bias, pooled_query, pooled_query_bias,
    pooled_output, pooled_output_bias, conv_key, conv_value, conv_value_bias,
    norm_gain, norm_shift, expand_weight, expand_bias, reduce_weight, reduce_bias,
    final_gain, final_shift,
):
    docs, rows, width = inputs.shape
    devices = lax.axis_size("seq")
    me = lax.axis_index("seq")
    mine = lax.axis_index("batch")
    levels = devices.bit_length() - 1
    size = rows // STRIDE
    flat = docs * rows
    offset = me * rows
    reach = -(-REACH // size)
    gathered = devices <= 2 * reach
    fast = devices == 8 and width == 768 and lax.axis_size("batch") == 4
    base = jnp.where(gathered, 0, offset // STRIDE - reach * size)
    place = jnp.concatenate([offset[None], lengths, base[None]]).astype(jnp.int32)

    def line(vector):
        return vector[None]

    def tokens(array):
        return array.reshape(flat, array.shape[-1])

    taps_key, taps_value = conv_key.T, conv_value.T

    left = shift(inputs[:, rows - HALF :], "seq", 1)
    right = shift(inputs[:, :HALF], "seq", -1)
    q, kx, vx, pooled = project(
        place, inputs, left, right, local_query, line(local_query_bias), local_key, local_value,
        line(local_value_bias), taps_key, taps_value, line(conv_value_bias),
    )
    own = [pooled[:, which][None] for which in range(2)]

    mixes, probs_one = [], []

    def local_step(doc, token):
        mix, probs = local_forward(token, q, kx, vx, doc)
        mixes.append(mix)
        probs_one.append(probs)
        return mix

    if gathered:
        orders = ([2, 1, 0], [0, 2, 1]) if levels == 3 else (list(range(levels)),) * 2
        have = own
        pieces = [[own[0]], [own[1]]]
        relative = [[0], [0]]
        token = place
        for stage in range(levels):
            came = [swap(have[which], "seq", orders[which][stage]) for which in range(2)]
            if stage < docs:
                done = local_step(stage, token)
            else:
                mix_one, middle, middle_low, q2 = middle_forward(
                    token, inputs, local_output, line(local_output_bias), pooled_query,
                    line(pooled_query_bias), mixes,
                )
                done = q2
            came[0], came[1], done, token = sync(came[0], came[1], done, token)
            if stage < docs:
                mixes[stage] = done
            else:
                q2 = done
            for which in range(2):
                pieces[which].append(came[which])
                relative[which] += [r ^ (1 << orders[which][stage]) for r in relative[which]]
                if stage < levels - 1:
                    have[which] = jnp.concatenate([have[which], came[which]])
        slots = jnp.stack([me ^ jnp.array(r, jnp.int32) for r in relative])
    else:
        pieces = [
            [own[which]]
            + [
                shift(own[which], "seq", sign * distance)
                for distance in range(1, reach + 1)
                for sign in (1, -1)
            ]
            for which in range(2)
        ]
        spots = [reach] + [
            reach - sign * distance for distance in range(1, reach + 1) for sign in (1, -1)
        ]
        slots = jnp.array([spots, spots], jnp.int32)
        token = place
        for doc in range(docs):
            local_step(doc, token)
        mix_one, middle, middle_low, q2 = middle_forward(
            token, inputs, local_output, line(local_output_bias), pooled_query,
            line(pooled_query_bias), mixes,
        )

    keys, values, probs_two, mix_two, summed = pooled_forward(
        token, slots, pieces[0], pieces[1], q2, middle, pooled_output, line(pooled_output_bias)
    )
    (
        outputs, normed_low, hidden, grad_branch, grad_pre, grad_summed, grad_second, grad_mix_two,
        vec_feed, vec_wide,
    ) = feed(
        token, summed, cotangent, expand_weight, line(expand_bias), reduce_weight,
        line(reduce_bias), line(norm_gain), line(norm_shift), line(final_gain),
        line(final_shift), pooled_output,
    )

    order_first = [("batch", 1)] + [("seq", level) for level in range(levels)]
    order_last = order_first[1:]

    def bits_of(order):
        ids = [mine & 1] + [(mine if axis == "batch" else me) >> bit & 1 for axis, bit in order]
        return jnp.stack(ids).astype(jnp.int32)

    if fast:
        (feed_blocks,) = scatter_products(
            bits_of(order_first),
            order_first,
            [
                ("wide", normed_low, grad_pre),
                ("tall", grad_branch, hidden),
                ("square", tokens(mix_two), grad_second),
            ],
            quartered=True,
        )
        feed_blocks, grad_mix_two, token = sync(feed_blocks, grad_mix_two, token)
        feed_rows = feed_blocks.shape[-2]
        feed_mine = lax.psum_scatter(
            feed_blocks.reshape(4 * devices * feed_rows, 384),
            "batch",
            scatter_dimension=0,
            tiled=True,
        ).reshape((2,) * levels + (feed_rows, 384))

    blocks = devices if gathered else 2 * reach + 1
    if gathered:
        back = ([0, 1, 2], [1, 2, 0]) if levels == 3 else (list(range(levels)),) * 2
        places = []
        for which in range(2):
            spots = []
            for block in range(devices):
                relative = 0
                for at, bit in enumerate(back[which]):
                    relative |= (block >> (levels - 1 - at) & 1) << bit
                spots.append(relative)
            places.append(me ^ jnp.array(spots, jnp.int32))
        places = jnp.stack(places)
        half_blocks = devices // 2
    else:
        middle_first = [reach] + [spot for spot in range(blocks) if spot != reach]
        places = jnp.array([middle_first, middle_first], jnp.int32)
        half_blocks = 1
    grad_q2, dk_kept, dk_sent, dv_kept, dv_sent = pooled_backward(
        places, token, q2, keys, values, probs_two, grad_mix_two, size, half_blocks
    )
    back_parts = ()

    def back_step(doc, token, earlier):
        return local_backward(token, q, kx, vx, grad_mix_one, probs_one[doc], doc, earlier)

    grad_middle, grad_first, grad_mix_one, vec_first = first_backward(
        token, grad_q2, grad_summed, pooled_query, local_output
    )
    if gathered:
        kept = [part.reshape((2,) * (levels - 1) + part.shape[1:]) for part in (dk_kept, dv_kept)]
        sent = [part.reshape((2,) * (levels - 1) + part.shape[1:]) for part in (dk_sent, dv_sent)]
        for stage in range(levels):
            came = [swap(sent[which], "seq", back[which][stage]) for which in range(2)]
            if stage < docs:
                back_parts = list(back_step(stage, token, back_parts))
                came[0], came[1], back_parts[0], token = sync(
                    came[0], came[1], back_parts[0], token
                )
            if stage < levels - 1:
                for which in range(2):
                    sent[which], kept[which] = fold(kept[which], came[which])
        pooled_grads = [kept[0], came[0], kept[1], came[1]]
    else:
        pooled_grads = []
        for kept, sent in ((dk_kept, dk_sent), (dv_kept, dv_sent)):
            total = kept[0]
            for distance in range(1, reach + 1):
                total = total + shift(sent[reach - distance], "seq", -distance).astype(F32)
                total = total + shift(sent[reach + distance - 1], "seq", distance).astype(F32)
            pooled_grads += [total, jnp.zeros_like(total)]
        for doc in range(docs):
            back_parts = back_step(doc, token, back_parts)
    dq, own_grads, low_left, low_right = back_parts
    from_left = shift(low_right, "seq", 1)
    from_right = shift(low_left, "seq", -1)
    if fast:
        middle_kept, middle_sent = scatter_products(
            bits_of(order_first) + 0 * token[0],
            order_first,
            [
                ("square", tokens(middle_low), tokens(grad_q2)),
                ("square", tokens(mix_one), grad_first),
                ("square", tokens(inputs), tokens(dq)),
            ],
        )
        pooled_grads[1], pooled_grads[3], middle_sent, from_left, from_right, token = sync(
            pooled_grads[1], pooled_grads[3], middle_sent, from_left, from_right, token
        )
    heads = [
        pooled_grads[2 * which][:, :1].astype(F32) + pooled_grads[2 * which + 1][:, :1].astype(F32)
        for which in range(2)
    ]
    after = shift(jnp.stack(heads).astype(BF16), "seq", -1)
    if fast:
        middle_came = swap(middle_sent, "batch", 0)
        after, middle_came, token = sync(after, middle_came, token)
        middle_terms, middle_came = advance([middle_kept, middle_came], order_first[0])
        feed_terms, feed_came = advance([feed_mine], order_first[1])
    grad_k, grad_v, vec_input = key_value_gradients(
        token, pooled_grads, [after[0], after[1]], kx, vx, taps_key, taps_value,
        own_grads, from_left, from_right, dq,
    )
    if fast:
        last_kept, last_sent = scatter_products(
            bits_of(order_last),
            order_last,
            [("square", tokens(inputs), grad_k), ("square", tokens(inputs), grad_v)],
            (vec_feed, vec_first, vec_input, vec_wide),
        )
        last_sent, middle_came, token = sync(last_sent, middle_came, token)
        last_came = swap(last_sent, "batch", 0)
    input_grad = input_gradient(
        token, tokens(dq), grad_k, grad_v, grad_middle, local_query, local_key, local_value
    )

    if fast:
        upper = (mine & 2) > 0
        odd = (mine & 1) > 0

        def pair_up(flag, low, other):
            return jnp.stack([jnp.where(flag, other, low), jnp.where(flag, low, other)])

        input_grad, last_came, feed_came = sync(input_grad, last_came, feed_came)
        cut_at = middle_kept.shape[-2]

        def joined(axis):
            left_part = total_of(middle_terms + [middle_came], 1)
            right_part = total_of(last_terms, 1)
            return jnp.concatenate([left_part, right_part], axis=-2).astype(BF16)

        last_terms = [last_kept, last_came]
        came = swap(joined(0), "seq", 0)
        feed_terms, feed_came = advance(feed_terms + [feed_came], order_first[2])
        came, feed_came = sync(came, feed_came)
        middle_terms = [term[0] for term in middle_terms + [middle_came]] + [
            came[..., :cut_at, :]
        ]
        last_terms = [term[0] for term in last_terms] + [came[..., cut_at:, :]]
        for hop in range(1, levels):
            send = jnp.concatenate(
                [total_of(middle_terms, 1), total_of(last_terms, 1)], axis=-2
            ).astype(BF16)
            came = swap(send, "seq", hop)
            if hop == 1:
                feed_terms, feed_came = advance(feed_terms + [feed_came], order_first[3])
                came, feed_came = sync(came, feed_came)
            if hop == 2:
                feed_low = total_of(feed_terms + [feed_came], Ellipsis).astype(BF16)
                feed_other = swap(feed_low, "batch", 1)
                came, feed_other = sync(came, feed_other)
            middle_terms = [term[0] for term in middle_terms] + [came[..., :cut_at, :]]
            last_terms = [term[0] for term in last_terms] + [came[..., cut_at:, :]]
        final = jnp.concatenate(
            [total_of(middle_terms, Ellipsis), total_of(last_terms, Ellipsis)], axis=-2
        ).astype(BF16)
        other = swap(final, "batch", 1)
        feed_both = pair_up(upper, feed_low, feed_other)
        feed_across = swap(feed_both, "batch", 0)
        other, feed_across = sync(other, feed_across)
        middle_both = pair_up(upper, final[:cut_at], other[:cut_at]).reshape(2 * cut_at, 384)
        last_half = (final[cut_at:].astype(F32) + other[cut_at:].astype(F32)).astype(BF16)
        both = jnp.concatenate([middle_both, last_half])
        across = swap(both, "batch", 0)
        full_feed = pair_up(odd, feed_both, feed_across)
        full = pair_up(odd, both, across)
        full_middle = full[:, : 2 * cut_at].reshape(2, 2, cut_at, 384)
        last = full[:, 2 * cut_at :]
        small = width // devices // 2

        wide = cut(full_feed, 0, 4 * small).reshape(2, 2, 4, small, 384)
        grad_expand = wide.transpose(1, 3, 0, 2, 4).reshape(2 * small, 8 * 384).astype(F32)
        tall = cut(full_feed, 4 * small, 192).reshape(768, 384)
        grad_reduce = tall.T.astype(F32)

        def square(quarters, start):
            block = cut(quarters, start, small).transpose(1, 2, 0, 3)
            return block.reshape(2 * small, 768).astype(F32)

        grad_po = square(full_feed, 4 * small + 192)
        grad_pq, grad_lo, grad_lq = [square(full_middle, index * small) for index in range(3)]
        grad_lk, grad_lv = [
            last[:, index * 96 : index * 96 + 96].transpose(1, 0, 2).reshape(96, 768).astype(F32)
            for index in range(2)
        ]
        lines = last[:, 192:208].astype(F32)
        vec_low, vec_high = lines[0, :, :96], lines[1, :, :96]
        (fg, fs, rb, ng, ns, pob) = [vec_low[index] for index in range(6)]
        pqb, lob = lines[0, 0, LANES : LANES + 96], lines[0, 1, LANES : LANES + 96]
        grad_eb = vec_low[8:12].reshape(-1)
    else:

        def plain(left_array, right_array):
            product = tn(left_array, right_array)
            part = lax.psum_scatter(product, "seq", scatter_dimension=0, tiled=True)
            return lax.psum(part.astype(BF16), "batch").astype(F32)

        grad_expand = plain(normed_low, grad_pre)
        grad_reduce = plain(hidden, grad_branch)
        grad_po = plain(tokens(mix_two), grad_second)
        grad_pq = plain(tokens(middle_low), tokens(grad_q2))
        grad_lo = plain(tokens(mix_one), grad_first)
        grad_lq = plain(tokens(inputs), tokens(dq))
        grad_lk = plain(tokens(inputs), grad_k)
        grad_lv = plain(tokens(inputs), grad_v)
        vectors = jnp.concatenate(
            [vec_feed, vec_first, vec_input, vec_wide.reshape(-1, width)], axis=0
        )
        vectors = lax.psum(vectors, ("seq", "batch"))
        share = width // devices
        part = lax.dynamic_slice_in_dim(vectors, me * share, share, axis=1)
        wide = vectors[32:].reshape(-1)
        wide_share = wide.shape[0] // devices
        grad_eb = lax.dynamic_slice_in_dim(wide, me * wide_share, wide_share, axis=0)
        (fg, fs, rb, ng, ns, pob) = [part[index] for index in range(6)]
        pqb, lob = part[8], part[9]
        vec_high = part[16:32]
    grad_ck = vec_high[:KER].T
    grad_cv = vec_high[KER : 2 * KER].T
    cvb, lqb, lvb = vec_high[10], vec_high[11], vec_high[12]
    return (
        outputs, input_grad,
        grad_lq, lqb, grad_lk, grad_lv, lvb, grad_lo, lob, grad_pq, pqb, grad_po, pob,
        grad_ck, grad_cv, cvb, ng, ns, grad_expand, grad_eb, grad_reduce, rb, fg, fs,
    )


def solution(mesh):
    vector = P("seq")
    matrix = P("seq", None)
    return jax.shard_map(
        device_step,
        mesh=mesh,
        in_specs=(P("batch", "seq", None), P("batch"), P("batch", "seq", None)) + (P(),) * 22,
        out_specs=(
            P("batch", "seq", None), P("batch", "seq", None),
            matrix, vector, matrix, matrix, vector, matrix, vector, matrix, vector, matrix, vector,
            matrix, matrix, vector, vector, vector, matrix, vector, matrix, vector, vector, vector,
        ),
        check_vma=False,
    )
```

```python
import functools
import math

import jax
import jax.numpy as jnp
from jax import lax
from jax.experimental import pallas as pl
from jax.experimental.pallas import tpu as pltpu
from jax.sharding import PartitionSpec as P

HEADS = 12
HD = 64
WIN = 128
PWIN = 512
KER = 5
STRIDE = 4
HALF = WIN // 2
REACH = PWIN // 2
NEGATIVE = -1e30
SCALE = 1.0 / math.sqrt(HD)
EPSILON = 1e-05
LANES = 128
TILE = 128
ROWS = 128
CHUNK = 256
F32 = jnp.float32
BF16 = jnp.bfloat16


def nn(left, right):
    return jnp.dot(left, right, preferred_element_type=F32)


def nt(left, right):
    return lax.dot_general(left, right, (((1,), (1,)), ((), ())), preferred_element_type=F32)


def tn(left, right):
    return lax.dot_general(left, right, (((0,), (0,)), ((), ())), preferred_element_type=F32)


def column_sum(block):
    return jnp.sum(block.astype(F32), axis=0, keepdims=True)


def call(body, grid, scalars, inputs, outputs, scratch=(), spare=8):
    used = spare * 2**20
    arrays, in_specs, out_specs, shapes = [], [], [], []

    def spec(shape, dtype, block, index):
        nonlocal used
        if block is None:
            return pl.BlockSpec(memory_space=pltpu.VMEM)
        if block == "raw":
            return pl.BlockSpec(memory_space=pl.ANY)
        used += 2 * math.prod(block) * jnp.dtype(dtype).itemsize
        return pl.BlockSpec(block, index)

    for array, block, index in inputs:
        in_specs.append(spec(array.shape, array.dtype, block, index))
        if block is not None:
            array = pltpu.with_memory_space_constraint(array, pltpu.HBM)
        arrays.append(array)
    for shape, dtype, block, index in outputs:
        out_specs.append(spec(shape, dtype, block, index))
        plain = block is None
        shapes.append((jax.ShapeDtypeStruct if plain else pltpu.HBM)(shape, dtype))
    for item in scratch:
        if hasattr(item, "shape") and item.memory_space == pltpu.VMEM:
            used += math.prod(item.shape) * jnp.dtype(item.dtype).itemsize
    return pl.pallas_call(
        body,
        grid_spec=pltpu.PrefetchScalarGridSpec(
            num_scalar_prefetch=len(scalars),
            grid=grid,
            in_specs=in_specs,
            out_specs=out_specs,
            scratch_shapes=list(scratch),
        ),
        out_shape=shapes,
        compiler_params=pltpu.CompilerParams(
            dimension_semantics=("arbitrary",) * len(grid), vmem_limit_bytes=used
        ),
        cost_estimate=pl.CostEstimate(flops=1000, bytes_accessed=1000, transcendentals=0),
    )(*scalars, *arrays)


def raw(array):
    return (array, "raw", None)


def out_raw(shape, dtype):
    return (shape, dtype, "raw", None)


def whole(array):
    return (array, None, None)


def out_whole(shape, dtype):
    return (shape, dtype, None, None)


def sync(*values):
    return lax.optimization_barrier(values)


def stack_heads(block):
    lane = lax.broadcasted_iota(jnp.int32, block.shape, 1)
    zero = jnp.zeros_like(block)
    return jnp.concatenate(
        [jnp.where(lane < HD, block, zero), jnp.where(lane < HD, zero, block)], axis=0
    )


def unstack(block):
    joined = jnp.concatenate([block[:HD, :TILE], block[HD:, TILE:]], axis=0)
    return joined.T


def positions(shape, dim):
    return lax.broadcasted_iota(jnp.int32, shape, dim)


def project_body(place, x, wq, bq, wk, wv, bv, q, k, v):
    docs, rows, width = x.shape
    flat = x[...].reshape(docs * rows, width)
    q[...] = (nn(flat, wq[...]) + bq[...]).astype(BF16).reshape(q.shape)
    k[...] = nn(flat, wk[...]).astype(BF16).reshape(k.shape)
    v[...] = (nn(flat, wv[...]) + bv[...]).astype(BF16).reshape(v.shape)


def project(place, x, wq, bq, wk, wv, bv):
    return call(
        project_body,
        (1,),
        (place,),
        [whole(a) for a in (x, wq, bq, wk, wv, bv)],
        [out_whole(x.shape, BF16)] * 3,
    )


def pool_body(place, left, right, k, v, wk, wv, bv, ck, cv, bcv, kx, vx, pooled, rows):
    offset = place[0]
    docs, own_rows, width = k.shape
    rims = jnp.concatenate(
        [part[doc] for doc in range(docs) for part in (left, right)], axis=0
    )
    size = own_rows + WIN
    count = pooled.shape[2]
    spot = offset - HALF + positions((size, 1), 0)
    for which, (weight, bias, taps, own, out) in enumerate(
        ((wk, None, ck, k, kx), (wv, bv, cv, v, vx))
    ):
        value = nn(rims, weight[...])
        if bias is not None:
            value = value + bias[...]
        value = value.astype(BF16)
        for doc in range(docs):
            at = doc * WIN
            out[doc, :HALF] = value[at : at + HALF]
            out[doc, HALF : HALF + own_rows] = own[doc]
            out[doc, HALF + own_rows :] = value[at + HALF : at + WIN]
            valid = (spot >= 0) & (spot < place[1 + doc])
            for group in range(width // LANES):
                lanes = slice(group * LANES, (group + 1) * LANES)
                rows[group] = jnp.where(valid, out[doc, :, lanes].astype(F32), 0.0)
                total = jnp.zeros((count, LANES), F32)
                for tap in range(KER):
                    start = HALF - KER // 2 + tap
                    read = rows[group, pl.ds(start, count, stride=STRIDE), :]
                    total = total + read * taps[tap : tap + 1, lanes]
                if which == 1:
                    total = total + bcv[:, lanes]
                pooled[which, doc, :, lanes] = total.astype(BF16)


def pool(place, left, right, k, v, wk, wv, bv, ck, cv, bcv):
    docs, rows, width = k.shape
    extended = rows + WIN
    return call(
        pool_body,
        (1,),
        (place,),
        [whole(a) for a in (left, right, k, v, wk, wv, bv, ck, cv, bcv)],
        [
            out_whole((docs, extended, width), BF16),
            out_whole((docs, extended, width), BF16),
            out_whole((2, docs, rows // STRIDE, width), BF16),
        ],
        [pltpu.VMEM((width // LANES, extended, LANES), F32)],
    )


def local_bias(tile, offset, length):
    shape = (TILE + WIN, TILE)
    key = positions(shape, 0)
    query = positions(shape, 1)
    spot = offset + tile * TILE - HALF + key
    allowed = (
        (key >= query) & (key < query + WIN) & (spot >= 0) & (spot < length)
    ) | (key == query + HALF)
    return jnp.where(allowed, 0.0, NEGATIVE)


def softmax_columns(scores):
    top = jnp.max(scores, axis=0, keepdims=True)
    grown = jnp.exp(scores - top)
    return grown * (1.0 / jnp.sum(grown, axis=0, keepdims=True))


def local_forward_body(place, q, kx, vx, mix, probs, *, doc):
    offset, length = place[0], place[1 + doc]
    span = TILE + WIN
    for tile in range(q.shape[1] // TILE):
        half_bias = local_bias(tile, offset, length)
        bias = jnp.concatenate([half_bias, half_bias], axis=1)
        first = tile * TILE
        for pair in range(q.shape[2] // LANES):
            lanes = slice(pair * LANES, (pair + 1) * LANES)
            queries = stack_heads(q[doc, first : first + TILE, lanes]) * SCALE
            scores = nt(kx[doc, first : first + span, lanes], queries) + bias
            chance = softmax_columns(scores)
            probs[pair, tile] = chance
            turned = vx[doc, first : first + span, lanes].T
            mixed = nn(turned, chance.astype(BF16))
            mix[first : first + TILE, lanes] = unstack(mixed).astype(BF16)


def local_forward(place, q, kx, vx, doc):
    _, rows, width = q.shape
    pairs, tiles, span = width // LANES, rows // TILE, TILE + WIN
    return call(
        functools.partial(local_forward_body, doc=doc),
        (1,),
        (place,),
        [whole(a) for a in (q, kx, vx)],
        [
            out_whole((rows, width), BF16),
            out_whole((pairs, tiles, span, 2 * TILE), F32),
        ],
    )


def middle_body(place, x, wo, bo, wpq, bpq, *refs):
    docs, rows = x.shape[0], x.shape[1]
    mixes, (mix, middle, middle_low, q2) = refs[:docs], refs[docs:]
    for doc in range(docs):
        mix[doc] = mixes[doc][...]
    flat = docs * rows
    branch = nn(mix[...].reshape(flat, x.shape[2]), wo[...]) + bo[...]
    total = x[...].reshape(flat, x.shape[2]).astype(F32) + branch
    middle[...] = total.reshape(middle.shape)
    low = total.astype(BF16)
    middle_low[...] = low.reshape(middle_low.shape)
    q2[...] = (nn(low, wpq[...]) + bpq[...]).astype(BF16).reshape(q2.shape)


def middle_forward(place, x, wo, bo, wpq, bpq, mixes):
    docs, rows, width = x.shape
    return call(
        middle_body,
        (1,),
        (place,),
        [whole(a) for a in (x, wo, bo, wpq, bpq, *mixes)],
        [
            out_whole((docs, rows, width), BF16),
            out_whole((docs, rows, width), F32),
            out_whole((docs, rows, width), BF16),
            out_whole((docs, rows, width), BF16),
        ],
    )


def attention_back(keys, values, queries, grads, chance):
    stacked_grads = stack_heads(grads)
    stacked_queries = stack_heads(queries)
    grad_chance = nt(values, stacked_grads * SCALE)
    dots = jnp.sum(chance * grad_chance, axis=0, keepdims=True)
    grad_raw = (chance * (grad_chance - dots)).astype(BF16)
    grad_keys = nn(grad_raw, stacked_queries)
    grad_values = nn(chance.astype(BF16), stacked_grads)
    grad_queries = unstack(nn(keys.T, grad_raw))
    return grad_queries, grad_keys, grad_values


def first_back_body(place, gq2, gsum, wpq, wo, gmid, gfirst, gmix, vec):
    docs, rows, width = gsum.shape
    flat = docs * rows
    grads = gq2[...].reshape(flat, width)
    total = gsum[...].reshape(flat, width) + nt(grads, wpq[...])
    gmid[...] = total.reshape(gmid.shape)
    low = total.astype(BF16)
    gfirst[...] = low
    gmix[...] = nt(low, wo[...]).astype(BF16).reshape(gmix.shape)
    vec[...] = jnp.zeros_like(vec)
    vec[0:1] = column_sum(grads)
    vec[1:2] = column_sum(low)


def first_backward(place, gq2, gsum, wpq, wo):
    docs, rows, width = gsum.shape
    return call(
        first_back_body,
        (1,),
        (place,),
        [whole(a) for a in (gq2, gsum, wpq, wo)],
        [
            out_whole((docs, rows, width), F32),
            out_whole((docs * rows, width), BF16),
            out_whole((docs, rows, width), BF16),
            out_whole((8, width), F32),
        ],
    )


def local_backward_body(place, q, kx, vx, gmix, probs, *refs, doc):
    earlier = refs[: len(refs) - 6]
    dq, own, low_left, low_right, dk, dv = refs[len(refs) - 6 :]
    rows = q.shape[1]
    for old, new in zip(earlier, (dq, own, low_left, low_right)):
        new[:doc] = old[...]
    span = TILE + WIN
    dk[...] = jnp.zeros_like(dk)
    dv[...] = jnp.zeros_like(dv)
    for tile in range(rows // TILE):
        first = tile * TILE
        for pair in range(q.shape[2] // LANES):
            lanes = slice(pair * LANES, (pair + 1) * LANES)
            grad_q, grad_k, grad_v = attention_back(
                kx[doc, first : first + span, lanes],
                vx[doc, first : first + span, lanes],
                q[doc, first : first + TILE, lanes],
                gmix[doc, first : first + TILE, lanes],
                probs[pair, tile],
            )
            dq[doc, first : first + TILE, lanes] = grad_q.astype(BF16)
            dk[first : first + span, lanes] += grad_k
            dv[first : first + span, lanes] += grad_v
    for which, part in enumerate((dk, dv)):
        own[doc, which] = part[HALF : HALF + rows]
        low_left[doc, which] = part[:HALF].astype(BF16)
        low_right[doc, which] = part[HALF + rows :].astype(BF16)


def local_backward(place, q, kx, vx, gmix, probs, doc, earlier=()):
    _, rows, width = q.shape
    span = TILE + WIN
    return call(
        functools.partial(local_backward_body, doc=doc),
        (1,),
        (place,),
        [whole(a) for a in (q, kx, vx, gmix, probs, *earlier)],
        [
            out_whole((doc + 1, rows, width), BF16),
            out_whole((doc + 1, 2, rows, width), F32),
            out_whole((doc + 1, 2, HALF, width), BF16),
            out_whole((doc + 1, 2, HALF, width), BF16),
        ],
        [
            pltpu.VMEM((rows + WIN, width), F32),
            pltpu.VMEM((rows + WIN, width), F32),
        ],
    )


def pooled_forward_body(place, slots, *refs, pieces):
    key_pieces = refs[:pieces]
    value_pieces = refs[pieces : 2 * pieces]
    (
        q2, middle, wpo, bpo, we, wr,
        keys_out, values_out, probs, mix, summed, we_near, wr_near,
        keys, values, bias, sems,
    ) = refs[2 * pieces :]
    doc, pair = pl.program_id(0), pl.program_id(1)
    fetches = [
        pltpu.make_async_copy(we, we_near, sems.at[0]),
        pltpu.make_async_copy(wr, wr_near, sems.at[1]),
    ]
    last = (pair == pl.num_programs(1) - 1) & (doc == pl.num_programs(0) - 1)
    leaves = [
        pltpu.make_async_copy(keys.at[each], keys_out.at[each], sems.at[2 + each])
        for each in range(keys.shape[0])
    ] + [
        pltpu.make_async_copy(
            values.at[each], values_out.at[each], sems.at[2 + keys.shape[0] + each]
        )
        for each in range(keys.shape[0])
    ]

    @pl.when((pair == 0) & (doc == 0))
    def _():
        for fetch in fetches:
            fetch.start()

    offset, length, base = place[0], place[1 + doc], place[1 + pl.num_programs(0)]
    tiles = q2.shape[1] // TILE
    count = keys.shape[1]

    @pl.when(pair == 0)
    def _():
        for where, group, out in ((0, key_pieces, keys), (1, value_pieces, values)):
            at = 0
            for piece in group:
                size = piece.shape[2]
                for block in range(piece.shape[0]):
                    spot = pl.multiple_of(slots[where, at] * size, size)
                    out[doc, pl.ds(spot, size), :] = piece[block, doc]
                    at += 1
        for tile in range(tiles):
            shape = (count, TILE)
            spot = base + positions(shape, 0)
            centre = offset // STRIDE + (tile * TILE + positions(shape, 1)) // STRIDE
            allowed = (
                (spot >= centre - REACH)
                & (spot < centre + REACH)
                & (spot >= 0)
                & (spot * STRIDE < length)
            ) | (spot == centre)
            bias[tile] = jnp.where(allowed, 0.0, NEGATIVE)
        for each in range(keys.shape[0]):

            @pl.when(doc == each)
            def _():
                leaves[each].start()
                leaves[keys.shape[0] + each].start()

    lanes = pl.ds(pl.multiple_of(pair * LANES, LANES), LANES)
    pair_keys = keys[doc, :, lanes]
    turned = values[doc, :, lanes].T
    for tile in range(tiles):
        first = tile * TILE
        queries = stack_heads(q2[doc, first : first + TILE, lanes]) * SCALE
        half_bias = bias[tile]
        scores = nt(pair_keys, queries) + jnp.concatenate([half_bias, half_bias], axis=1)
        chance = softmax_columns(scores)
        probs[0, 0, tile] = chance
        mixed = nn(turned, chance.astype(BF16))
        mix[doc, first : first + TILE, lanes] = unstack(mixed).astype(BF16)

    @pl.when(last)
    def _():
        for copy in fetches + leaves:
            copy.wait()
        flat = (mix.shape[0] * mix.shape[1], mix.shape[2])
        second = nn(mix[...].reshape(flat), wpo[...]) + bpo[...]
        summed[...] = middle[...] + second.reshape(summed.shape)


def pooled_forward(place, slots, key_pieces, value_pieces, q2, middle, wpo, bpo, we, wr):
    docs, rows, width = q2.shape
    pairs, tiles = width // LANES, rows // TILE
    size = key_pieces[0].shape[2]
    count = size * slots.shape[1]

    return call(
        functools.partial(pooled_forward_body, pieces=len(key_pieces)),
        (docs, pairs),
        (place, slots),
        [whole(a) for a in (*key_pieces, *value_pieces, q2, middle, wpo, bpo)]
        + [raw(we), raw(wr)],
        [
            out_raw((docs, count, width), BF16),
            out_raw((docs, count, width), BF16),
            (
                (docs, pairs, tiles, count, 2 * TILE),
                F32,
                (1, 1, tiles, count, 2 * TILE),
                lambda doc, pair, *_: (doc, pair, 0, 0, 0),
            ),
            out_whole((docs, rows, width), BF16),
            out_whole((docs, rows, width), F32),
            out_whole(we.shape, BF16),
            out_whole(wr.shape, BF16),
        ],
        [
            pltpu.VMEM((docs, count, width), BF16),
            pltpu.VMEM((docs, count, width), BF16),
            pltpu.VMEM((tiles, count, TILE), F32),
            pltpu.SemaphoreType.DMA((2 + 2 * docs,)),
        ],
    )


def pooled_backward_body(
    places, token, q2, keys, values, probs, grads, dq, dk_kept, dk_sent, dv_kept, dv_sent, sums
):
    doc, pair = pl.program_id(0), pl.program_id(1)
    lanes = pl.ds(pl.multiple_of(pair * LANES, LANES), LANES)
    size = dk_kept.shape[2]
    total = None
    for tile in range(probs.shape[2]):
        first = tile * TILE
        grad_q, *added = attention_back(
            keys[0],
            values[0],
            q2[0, first : first + TILE],
            grads[0, first : first + TILE],
            probs[0, 0, tile],
        )
        dq[doc, first : first + TILE, lanes] = grad_q.astype(BF16)
        total = added if total is None else [a + b for a, b in zip(total, added)]
    half = dk_kept.shape[0]
    rows = keys.shape[1]
    for which, (kept, sent) in enumerate(((dk_kept, dk_sent), (dv_kept, dv_sent))):
        sums[:rows] = total[which]
        sums[rows:] = jnp.zeros((8, LANES), F32)
        for block in range(half + sent.shape[0]):
            start = pl.multiple_of(places[which, block] * (size - 8), size - 8)
            part = sums[pl.ds(start, size), :]
            if block < half:
                kept[block, doc, :, lanes] = part
            else:
                sent[block - half, doc, :, lanes] = part.astype(BF16)


def pooled_backward(places, token, q2, keys, values, probs, grads, size, kept):
    docs, rows, width = q2.shape
    count = keys.shape[1]
    blocks = count // size
    tiles = rows // TILE

    def lanes_of(array):
        return (array, (1, array.shape[1], LANES), lambda doc, pair, *_: (doc, 0, pair))

    return call(
        pooled_backward_body,
        (docs, width // LANES),
        (places, token),
        [
            lanes_of(q2),
            lanes_of(keys),
            lanes_of(values),
            (
                probs,
                (1, 1, tiles, count, 2 * TILE),
                lambda doc, pair, *_: (doc, pair, 0, 0, 0),
            ),
            lanes_of(grads),
        ],
        [
            out_whole((docs, rows, width), BF16),
            out_whole((kept, docs, size + 8, width), F32),
            out_whole((blocks - kept, docs, size + 8, width), BF16),
            out_whole((kept, docs, size + 8, width), F32),
            out_whole((blocks - kept, docs, size + 8, width), BF16),
        ],
        [pltpu.VMEM((count + 8, LANES), F32)],
    )


def feed_body(
    place, summed, cotangent, we, be, wr, br, ng, ns, fg, fs, wpo,
    outputs_far, normed_low, hidden, grad_branch, grad_pre, grad_summed_far, grad_second,
    grad_mix_far, vec, vec_wide,
    normed, slope, work, unit, outputs, grad_mix, sems,
):
    docs, rows = cotangent.shape[0], cotangent.shape[1]
    width = summed.shape[2]
    wide = we.shape[1]
    steps = rows // ROWS
    blocks = [
        (doc, step * ROWS, doc * rows + step * ROWS)
        for doc in range(docs)
        for step in range(steps)
    ]
    leaving = []

    def leave(source, target, doc, start, row):
        copy = pltpu.make_async_copy(
            source.at[pl.ds(row, ROWS)],
            target.at[doc, pl.ds(start, ROWS)],
            sems.at[len(leaving)],
        )
        copy.start()
        leaving.append(copy)


    def normal(value):
        centred = value - jnp.mean(value, axis=-1, keepdims=True)
        scale = lax.rsqrt(jnp.mean(centred * centred, axis=-1, keepdims=True) + EPSILON)
        return centred * scale, scale

    scales = []
    for doc, start, row in blocks:
        norm, scale = normal(summed[doc, start : start + ROWS])
        scales.append(scale)
        unit[row : row + ROWS] = norm
        full = norm * ng[...] + ns[...]
        normed[row : row + ROWS] = full
        normed_low[row : row + ROWS] = full.astype(BF16)

    def expand(index, _):
        part = pl.ds(pl.multiple_of(index * CHUNK, CHUNK), CHUNK)
        pre = nn(normed_low[...], we[:, part]) + be[:, part]
        cdf = 0.5 * (1.0 + lax.erf(pre * math.sqrt(0.5)))
        hidden[:, part] = (pre * cdf).astype(BF16)
        slope[:, part] = cdf + pre * (jnp.exp(pre * pre * -0.5) * (1.0 / math.sqrt(2.0 * math.pi)))
        return 0

    lax.fori_loop(0, wide // CHUNK, expand, 0)

    for start in range(0, width, CHUNK):
        part = slice(start, start + CHUNK)
        work[:, part] = normed[:, part] + (nn(hidden[...], wr[:, part]) + br[:, part])

    sums = [jnp.zeros((1, width), F32) for _ in range(6)]
    for doc, start, row in blocks:
        norm, scale = normal(work[row : row + ROWS])
        spot = place[0] + start + positions((ROWS, 1), 0)
        valid = (spot < place[1 + doc]).astype(F32)
        outputs[row : row + ROWS] = (valid * (norm * fg[...] + fs[...])).astype(BF16)
        leave(outputs, outputs_far, doc, start, row)
        error = valid * cotangent[doc, start : start + ROWS].astype(F32)
        sums[0] += column_sum(error * norm)
        sums[1] += column_sum(error)
        scaled = error * fg[...]
        rest = (
            scaled
            - jnp.mean(scaled, axis=-1, keepdims=True)
            - norm * jnp.mean(scaled * norm, axis=-1, keepdims=True)
        ) * scale
        work[row : row + ROWS] = rest
        low = rest.astype(BF16)
        grad_branch[row : row + ROWS] = low
        sums[2] += column_sum(low)

    def reduce(index, _):
        part = pl.ds(pl.multiple_of(index * CHUNK, CHUNK), CHUNK)
        low = (nt(grad_branch[...], wr[part, :]) * slope[:, part]).astype(BF16)
        grad_pre[:, part] = low
        vec_wide[:, part] = column_sum(low)
        return 0

    lax.fori_loop(0, wide // CHUNK, reduce, 0)

    for start in range(0, width, CHUNK):
        part = slice(start, start + CHUNK)
        work[:, part] += nt(grad_pre[...], we[part, :])

    for (doc, start, row), scale in zip(blocks, scales):
        error = work[row : row + ROWS]
        norm = unit[row : row + ROWS]
        sums[3] += column_sum(error * norm)
        sums[4] += column_sum(error)
        scaled = error * ng[...]
        grad = (
            scaled
            - jnp.mean(scaled, axis=-1, keepdims=True)
            - norm * jnp.mean(scaled * norm, axis=-1, keepdims=True)
        ) * scale
        unit[row : row + ROWS] = grad
        leave(unit, grad_summed_far, doc, start, row)
        low = grad.astype(BF16)
        grad_second[row : row + ROWS] = low
        sums[5] += column_sum(low)
        grad_mix[row : row + ROWS] = nt(low, wpo[...]).astype(BF16)
        leave(grad_mix, grad_mix_far, doc, start, row)
    for index, value in enumerate(sums):
        vec[index : index + 1] = value
    vec[6:8] = jnp.zeros((2, width), F32)
    for copy in leaving:
        copy.wait()


def feed(place, summed, cotangent, we, be, wr, br, ng, ns, fg, fs, wpo):
    docs, rows, width = summed.shape
    wide = we.shape[1]
    tokens = docs * rows
    return call(
        feed_body,
        (1,),
        (place,),
        [whole(a) for a in (summed, cotangent, we, be, wr, br, ng, ns, fg, fs, wpo)],
        [
            out_raw((docs, rows, width), BF16),
            out_whole((tokens, width), BF16),
            out_whole((tokens, wide), BF16),
            out_whole((tokens, width), BF16),
            out_whole((tokens, wide), BF16),
            out_raw((docs, rows, width), F32),
            out_whole((tokens, width), BF16),
            out_raw((docs, rows, width), BF16),
            out_whole((8, width), F32),
            out_whole((1, wide), F32),
        ],
        [
            pltpu.VMEM((tokens, width), F32),
            pltpu.VMEM((tokens, wide), F32),
            pltpu.VMEM((tokens, width), F32),
            pltpu.VMEM((tokens, width), F32),
            pltpu.VMEM((tokens, width), BF16),
            pltpu.VMEM((tokens, width), BF16),
            pltpu.SemaphoreType.DMA((3 * tokens // ROWS,)),
        ],
    )


def key_value_body(place, *refs, docs):
    gk_kept, gk_came, gv_kept, gv_came, kx, vx, ck, cv = refs[:8]
    own, from_left, from_right, dq = refs[8:12]
    gk, gv, vec, rows_in, pooled, total = refs[12:]
    offset = place[0]
    rows, width = gk.shape[0] // docs, gk.shape[1]
    count = rows // STRIDE
    vec[...] = jnp.zeros_like(vec)
    for doc in range(docs):
        length = place[1 + doc]
        spot = offset - HALF + positions((rows + WIN, 1), 0)
        valid = (spot >= 0) & (spot < length)
        first = doc * rows
        for which, (kept, came, ext, taps, out, row) in enumerate(
            (
                (gk_kept, gk_came, kx, ck, gk, 0),
                (gv_kept, gv_came, vx, cv, gv, KER),
            )
        ):
            pooled[...] = kept[doc].astype(F32) + came[doc].astype(F32)
            masked = jnp.where(valid, ext[doc].astype(F32), 0.0)
            for group in range(width // LANES):
                lanes = slice(group * LANES, (group + 1) * LANES)
                grown = pooled[:count, lanes]
                shifted = pooled[1 : count + 1, lanes]
                rows_in[group] = masked[:, lanes]
                for tap in range(KER):
                    start = HALF - KER // 2 + tap
                    read = rows_in[group, pl.ds(start, count, stride=STRIDE), :]
                    vec[row + tap : row + tap + 1, lanes] += column_sum(grown * read)
                if which == 1:
                    vec[2 * KER : 2 * KER + 1, lanes] += column_sum(grown)
                total[group] = own[doc, which, :, lanes]
                total[group, :HALF] += from_left[doc, which, :, lanes].astype(F32)
                total[group, rows - HALF :] += from_right[doc, which, :, lanes].astype(F32)
                for phase, terms in enumerate(
                    (
                        ((2, grown),),
                        ((3, grown),),
                        ((4, grown), (0, shifted)),
                        ((1, shifted),),
                    )
                ):
                    part = pl.ds(phase, count, stride=STRIDE)
                    added = None
                    for tap, values in terms:
                        term = values * taps[tap : tap + 1, lanes]
                        added = term if added is None else added + term
                    inside = offset + phase + STRIDE * positions((count, 1), 0) < length
                    total[group, part, :] = total[group, part, :] + jnp.where(inside, added, 0.0)
                out[first : first + rows, lanes] = total[group].astype(BF16)
        vec[11:12] += column_sum(dq[doc])
    vec[12:13] += column_sum(gv[...])


def key_value_gradients(place, pooled_grads, kx, vx, ck, cv, own, left, right, dq):
    docs, rows, width = dq.shape
    return call(
        functools.partial(key_value_body, docs=docs),
        (1,),
        (place,),
        [
            whole(a)
            for a in (*pooled_grads, kx, vx, ck, cv, own, left, right, dq)
        ],
        [out_whole((docs * rows, width), BF16)] * 2 + [out_whole((16, width), F32)],
        [
            pltpu.VMEM((width // LANES, rows + WIN, LANES), F32),
            pltpu.VMEM((rows // STRIDE + 8, width), F32),
            pltpu.VMEM((width // LANES, rows, LANES), F32),
        ],
    )


def input_body(place, dq, gk, gv, gmid, wq, wk, wv, dx):
    total = nt(dq[...], wq[...]) + nt(gk[...], wk[...]) + nt(gv[...], wv[...])
    dx[...] = (gmid[...] + total.reshape(gmid.shape)).astype(BF16)


def input_gradient(place, dq, gk, gv, gmid, wq, wk, wv):
    docs, rows, width = gmid.shape
    (dx,) = call(
        input_body,
        (1,),
        (place,),
        [whole(a) for a in (dq, gk, gv, gmid, wq, wk, wv)],
        [out_whole((docs, rows, width), BF16)],
    )
    return dx


def scatter_body(bits, *refs, kinds, order, vectors, quartered):
    count = len(kinds)
    operands = [refs[2 * index : 2 * index + 2] for index in range(count)]
    extra = refs[2 * count : 2 * count + vectors]
    rest = refs[2 * count + vectors :]
    if quartered:
        results, (ordered, rounded, *small) = (rest[0], rest[0]), rest[1:]
    else:
        results, (ordered, rounded, *small) = rest[:2], rest[2:]
    core = bits[0]
    sides = 2 if ("batch", 1) in order else 1
    owners = 8

    def start_of(which, size):
        if quartered:
            return which * size
        return pl.multiple_of((which ^ core) * size, LANES)

    def place_tile(which, side, owner, target, size, value):
        index = []
        for at, (axis, bit) in enumerate(order):
            if axis == "batch":
                index += [side, which] if quartered else [side ^ bits[1 + at]]
            else:
                index.append(((owner >> bit) & 1) ^ bits[1 + at])
        results[which][(*index, slice(target, target + size), slice(None))] = value

    base = 0
    for (left, right), kind in zip(operands, kinds):
        tall = left.shape[1]
        turned = left[...].T
        if kind == "wide":
            half = right.shape[1] // 2
            size = tall // owners // sides
            for which in range(2):
                start = start_of(which, half)
                for part in range(half // 768):
                    rounded[...] = nn(turned, right[:, pl.ds(start + part * 768, 768)]).astype(BF16)
                    for column in range(2):
                        target = base + (2 * part + column) * size
                        for owner in range(owners):
                            for side in range(sides):
                                row = (owner * sides + side) * size
                                value = rounded[row : row + size, column * 384 : column * 384 + 384]
                                place_tile(which, side, owner, target, size, value)
            base += half // 384 * size
        elif kind == "tall":
            ordered[...] = turned
            size = tall // 2 // sides
            for part in range(right.shape[1] // 768):
                product = nn(ordered[...], right[:, part * 768 : part * 768 + 768])
                rounded[...] = product.astype(BF16)
                for column in range(2):
                    owner = 2 * part + column
                    for side in range(sides):
                        for which in range(2):
                            row = start_of(which, 384) + side * size
                            value = rounded[pl.ds(row, size), column * 384 : column * 384 + 384]
                            place_tile(which, side, owner, base, size, value)
            base += size
        else:
            size = tall // owners // sides
            if quartered:
                columns = right[...]
            else:
                columns = jnp.concatenate(
                    [right[:, pl.ds(start_of(which, 384), 384)] for which in range(2)], axis=1
                )
            rounded[...] = nn(turned, columns).astype(BF16)
            for which in range(2):
                for owner in range(owners):
                    for side in range(sides):
                        row = (owner * sides + side) * size
                        value = rounded[row : row + size, which * 384 : which * 384 + 384]
                        place_tile(which, side, owner, base, size, value)
            base += size
    if vectors:
        (block,) = small
        vec_feed, vec_first, vec_input, vec_wide = extra
        for owner in range(owners):
            lanes = slice(owner * 96, owner * 96 + 96)
            block[0, owner] = jnp.zeros(block.shape[2:], F32)
            block[1, owner] = jnp.zeros(block.shape[2:], F32)
            block[0, owner, 0:8, 0:96] = vec_feed[:, lanes]
            block[0, owner, 0:8, LANES : LANES + 96] = vec_first[:, lanes]
            block[1, owner, 0:16, 0:96] = vec_input[:, lanes]
            for part in range(4):
                at = owner * 384 + part * 96
                block[0, owner, 8 + part : 9 + part, 0:96] = vec_wide[:, at : at + 96]
        for owner in range(owners):
            for which in range(2):
                place_tile(which, 0, owner, base, 16, block[which ^ core, owner].astype(BF16))


def scatter_products(bits, order, items, extra=(), quartered=False):
    sides = 2 if ("batch", 1) in order else 1
    rows = 0
    for kind, left, right in items:
        if kind == "wide":
            rows += right.shape[1] // 768 * (left.shape[1] // 8 // sides)
        elif kind == "tall":
            rows += 384 // sides
        else:
            rows += 96 // sides
    rows += 16 if extra else 0
    shape = (2,) * (len(order) + quartered) + (rows, 384)
    operands = [array for _, left, right in items for array in (left, right)]
    return call(
        functools.partial(
            scatter_body,
            kinds=tuple(kind for kind, _, _ in items),
            order=tuple(order),
            vectors=len(extra),
            quartered=quartered,
        ),
        (1,),
        (bits,),
        [whole(a) for a in (*operands, *extra)],
        [out_whole(shape, BF16)] * (1 if quartered else 2),
        [pltpu.VMEM((768, operands[0].shape[0]), BF16), pltpu.VMEM((768, 768), BF16)]
        + ([pltpu.VMEM((2, 8, 16, 384), F32)] if extra else []),
    )


def quarter_products_body(bits, *refs, kinds, levels):
    count = len(kinds)
    operands = [refs[2 * index : 2 * index + 2] for index in range(count)]
    out, turned, rounded, sems = refs[2 * count :]
    sides, cores, owners = 2, 2, 1 << levels
    pending = [[], []]
    turn = 0

    def product(left, right):
        nonlocal turn
        slot = turn % 2
        turn += 1
        for copy in pending[slot]:
            copy.wait()
        pending[slot] = []
        rounded[slot] = nn(left, right).astype(BF16)
        return slot

    def leave(slot, source, side, which, owner, base, size):
        digits = [((owner >> level) & 1) ^ bits[level] for level in range(levels)]
        target = out.at[(side, which, *digits, pl.ds(base, size))]
        copy = pltpu.make_async_copy(source, target, sems.at[slot, len(pending[slot])])
        copy.start()
        pending[slot].append(copy)

    def by_rows(slot, which, base, columns):
        size = 768 // owners // sides
        for owner in range(owners):
            for side in range(sides):
                row = (owner * sides + side) * size
                source = rounded.at[slot, pl.ds(row, size), pl.ds(columns, 384)]
                leave(slot, source, side, which, owner, base, size)

    base = 0
    for (left, right), kind in zip(operands, kinds):
        turned[...] = left[...].T
        if kind == "wide":
            for which in range(cores):
                for part in range(2):
                    start = which * 1536 + part * 768
                    slot = product(turned[...], right[:, start : start + 768])
                    for column in range(2):
                        by_rows(slot, which, base + (2 * part + column) * 48, column * 384)
            base += 192
        elif kind == "tall":
            for part in range(4):
                slot = product(turned[...], right[:, part * 768 : part * 768 + 768])
                for column in range(2):
                    for which in range(cores):
                        for side in range(sides):
                            row = (which * sides + side) * 192
                            source = rounded.at[slot, pl.ds(row, 192), pl.ds(column * 384, 384)]
                            leave(slot, source, side, which, 2 * part + column, base, 192)
            base += 192
        else:
            slot = product(turned[...], right[...])
            for which in range(cores):
                by_rows(slot, which, base, which * 384)
            base += 48
    for group in pending:
        for copy in group:
            copy.wait()


def quarter_products(bits, items, levels):
    rows = sum(48 if kind == "square" else 192 for kind, _, _ in items)
    operands = [array for _, left, right in items for array in (left, right)]
    (out,) = call(
        functools.partial(
            quarter_products_body, kinds=tuple(kind for kind, _, _ in items), levels=levels
        ),
        (1,),
        (bits,),
        [whole(a) for a in operands],
        [out_raw((2, 2) + (2,) * levels + (rows, 384), BF16)],
        [
            pltpu.VMEM((768, operands[0].shape[0]), BF16),
            pltpu.VMEM((2, 768, 768), BF16),
            pltpu.SemaphoreType.DMA((2, 32)),
        ],
    )
    return out


def swap(value, axis, bit):
    count = lax.axis_size(axis)
    return lax.ppermute(value, axis, [(i, i ^ (1 << bit)) for i in range(count)])


def shift(value, axis, by):
    count = lax.axis_size(axis)
    pairs = [(i, i + by) for i in range(count) if 0 <= i + by < count]
    return lax.ppermute(value, axis, pairs)


def fold(kept, came):
    low = (kept[1].astype(F32) + came[1].astype(F32)).astype(BF16)
    return low, kept[0].astype(F32) + came[0].astype(F32)


def total_of(terms, *index):
    total = None
    for term in terms:
        value = term[index].astype(F32)
        total = value if total is None else total + value
    return total


def advance(terms, hop):
    came = swap(total_of(terms, 1).astype(BF16), *hop)
    return [term[0] for term in terms], came


def cut(quarters, start, size):
    return quarters[:, :, start : start + size]


def device_step(
    inputs, lengths, cotangent,
    local_query, local_query_bias, local_key, local_value, local_value_bias,
    local_output, local_output_bias, pooled_query, pooled_query_bias,
    pooled_output, pooled_output_bias, conv_key, conv_value, conv_value_bias,
    norm_gain, norm_shift, expand_weight, expand_bias, reduce_weight, reduce_bias,
    final_gain, final_shift,
):
    docs, rows, width = inputs.shape
    devices = lax.axis_size("seq")
    me = lax.axis_index("seq")
    mine = lax.axis_index("batch")
    levels = devices.bit_length() - 1
    size = rows // STRIDE
    flat = docs * rows
    offset = me * rows
    reach = -(-REACH // size)
    gathered = devices <= 2 * reach
    fast = devices == 8 and width == 768 and lax.axis_size("batch") == 4
    base = jnp.where(gathered, 0, offset // STRIDE - reach * size)
    place = jnp.concatenate([offset[None], lengths, base[None]]).astype(jnp.int32)

    def line(vector):
        return vector[None]

    def tokens(array):
        return array.reshape(flat, array.shape[-1])

    taps_key, taps_value = conv_key.T, conv_value.T

    left = shift(inputs[:, rows - HALF :], "seq", 1)
    right = shift(inputs[:, :HALF], "seq", -1)
    q, k_own, v_own = project(
        place, inputs, local_query, line(local_query_bias), local_key, local_value,
        line(local_value_bias),
    )
    left, right, k_own = sync(left, right, k_own)
    kx, vx, pooled = pool(
        place, left, right, k_own, v_own, local_key, local_value, line(local_value_bias),
        taps_key, taps_value, line(conv_value_bias),
    )
    own = [pooled[which][None] for which in range(2)]

    mixes, probs_one = [], []

    def local_step(doc, token):
        mix, probs = local_forward(token, q, kx, vx, doc)
        mixes.append(mix)
        probs_one.append(probs)
        return mix

    if gathered:
        orders = ([2, 1, 0], [0, 2, 1]) if levels == 3 else (list(range(levels)),) * 2
        have = own
        pieces = [[own[0]], [own[1]]]
        relative = [[0], [0]]
        token = place
        for stage in range(levels):
            came = [swap(have[which], "seq", orders[which][stage]) for which in range(2)]
            if stage < docs:
                done = local_step(stage, token)
            else:
                mix_one, middle, middle_low, q2 = middle_forward(
                    token, inputs, local_output, line(local_output_bias), pooled_query,
                    line(pooled_query_bias), mixes,
                )
                done = q2
            came[0], came[1], done, token = sync(came[0], came[1], done, token)
            if stage < docs:
                mixes[stage] = done
            else:
                q2 = done
            for which in range(2):
                pieces[which].append(came[which])
                relative[which] += [r ^ (1 << orders[which][stage]) for r in relative[which]]
                if stage < levels - 1:
                    have[which] = jnp.concatenate([have[which], came[which]])
        slots = jnp.stack([me ^ jnp.array(r, jnp.int32) for r in relative])
    else:
        pieces = [
            [own[which]]
            + [
                shift(own[which], "seq", sign * distance)
                for distance in range(1, reach + 1)
                for sign in (1, -1)
            ]
            for which in range(2)
        ]
        spots = [reach] + [
            reach - sign * distance for distance in range(1, reach + 1) for sign in (1, -1)
        ]
        slots = jnp.array([spots, spots], jnp.int32)
        token = place
        for doc in range(docs):
            local_step(doc, token)
        mix_one, middle, middle_low, q2 = middle_forward(
            token, inputs, local_output, line(local_output_bias), pooled_query,
            line(pooled_query_bias), mixes,
        )

    keys, values, probs_two, mix_two, summed, expand_near, reduce_near = pooled_forward(
        token, slots, pieces[0], pieces[1], q2, middle, pooled_output, line(pooled_output_bias),
        expand_weight, reduce_weight,
    )
    (
        outputs, normed_low, hidden, grad_branch, grad_pre, grad_summed, grad_second, grad_mix_two,
        vec_feed, vec_wide,
    ) = feed(
        token, summed, cotangent, expand_near, line(expand_bias), reduce_near,
        line(reduce_bias), line(norm_gain), line(norm_shift), line(final_gain),
        line(final_shift), pooled_output,
    )

    order_first = [("batch", 1)] + [("seq", level) for level in range(levels)]
    order_last = order_first[1:]

    def bits_of(order):
        ids = [mine & 1] + [(mine if axis == "batch" else me) >> bit & 1 for axis, bit in order]
        return jnp.stack(ids).astype(jnp.int32)

    seq_bits = jnp.stack([me >> level & 1 for level in range(levels)]).astype(jnp.int32)

    def over_batch(blocks):
        part = blocks.shape[2:]
        flat_blocks = blocks.reshape(-1, blocks.shape[-1])
        mine_part = lax.psum_scatter(flat_blocks, "batch", scatter_dimension=0, tiled=True)
        return mine_part.reshape(part)

    if fast:
        feed_blocks = quarter_products(
            seq_bits,
            [
                ("wide", normed_low, grad_pre),
                ("tall", grad_branch, hidden),
                ("square", tokens(mix_two), grad_second),
            ],
            levels,
        )
        feed_blocks, grad_mix_two, token = sync(feed_blocks, grad_mix_two, token)
        feed_part = over_batch(feed_blocks)

    blocks = devices if gathered else 2 * reach + 1
    if gathered:
        back = ([0, 1, 2], [1, 2, 0]) if levels == 3 else (list(range(levels)),) * 2
        places = []
        for which in range(2):
            spots = []
            for block in range(devices):
                relative = 0
                for at, bit in enumerate(back[which]):
                    relative |= (block >> (levels - 1 - at) & 1) << bit
                spots.append(relative)
            places.append(me ^ jnp.array(spots, jnp.int32))
        places = jnp.stack(places)
        half_blocks = devices // 2
    else:
        middle_first = [reach] + [spot for spot in range(blocks) if spot != reach]
        places = jnp.array([middle_first, middle_first], jnp.int32)
        half_blocks = 1
    grad_q2, dk_kept, dk_sent, dv_kept, dv_sent = pooled_backward(
        places, token, q2, keys, values, probs_two, grad_mix_two, size, half_blocks
    )
    grad_middle, grad_first, grad_mix_one, vec_first = first_backward(
        token, grad_q2, grad_summed, pooled_query, local_output
    )
    back_parts = ()

    def back_step(doc, token):
        return local_backward(
            token, q, kx, vx, grad_mix_one, probs_one[doc], doc, back_parts
        )

    if gathered:
        kept = [part.reshape((2,) * (levels - 1) + part.shape[1:]) for part in (dk_kept, dv_kept)]
        sent = [part.reshape((2,) * (levels - 1) + part.shape[1:]) for part in (dk_sent, dv_sent)]
        for stage in range(levels):
            came = [swap(sent[which], "seq", back[which][stage]) for which in range(2)]
            if stage < docs:
                back_parts = list(back_step(stage, token))
            if stage == docs - 1:
                from_left = shift(back_parts[3], "seq", 1)
                from_right = shift(back_parts[2], "seq", -1)
            if fast and stage == 0:
                came[0], came[1], back_parts[0], token = sync(
                    came[0], came[1], back_parts[0], token
                )
            if fast and stage == 1:
                middle_kept, middle_sent = scatter_products(
                    bits_of(order_first) + 0 * token[0],
                    order_first,
                    [
                        ("square", tokens(middle_low), tokens(grad_q2)),
                        ("square", tokens(mix_one), grad_first),
                        ("square", tokens(inputs), tokens(back_parts[0])),
                    ],
                )
                came[0], came[1], from_left, from_right, middle_sent, token = sync(
                    came[0], came[1], from_left, from_right, middle_sent, token
                )
            if fast and stage == 2:
                middle_came = swap(middle_sent, "batch", 0)
                came[0], came[1], middle_came, token = sync(
                    came[0], came[1], middle_came, token
                )
            if stage < levels - 1:
                for which in range(2):
                    sent[which], kept[which] = fold(kept[which], came[which])
        pooled_grads = [kept[0], came[0], kept[1], came[1]]
    else:
        pooled_grads = []
        for kept, sent in ((dk_kept, dk_sent), (dv_kept, dv_sent)):
            total = kept[0]
            for distance in range(1, reach + 1):
                total = total + shift(sent[reach - distance], "seq", -distance).astype(F32)
                total = total + shift(sent[reach + distance - 1], "seq", distance).astype(F32)
            after = shift(total[:, :1].astype(BF16), "seq", -1).astype(F32)
            total = jnp.concatenate([total[:, :size], jnp.tile(after, (1, 8, 1))], axis=1)
            pooled_grads += [total, jnp.zeros_like(total)]
        for doc in range(docs):
            back_parts = back_step(doc, token)
        from_left = shift(back_parts[3], "seq", 1)
        from_right = shift(back_parts[2], "seq", -1)
    dq, own_grads = back_parts[:2]
    if fast:
        middle_terms = [middle_kept, middle_came]
        middle_far = swap(total_of(middle_terms, 1, slice(None), 1).astype(BF16), "batch", 1)
    grad_k, grad_v, vec_input = key_value_gradients(
        token, pooled_grads, kx, vx, taps_key, taps_value,
        own_grads, from_left, from_right, dq,
    )
    if fast:
        last_kept, last_sent = scatter_products(
            bits_of(order_last),
            order_last,
            [("square", tokens(inputs), grad_k), ("square", tokens(inputs), grad_v)],
            (vec_feed, vec_first, vec_input, vec_wide),
        )
        last_sent, middle_far, token = sync(last_sent, middle_far, token)
        last_came = swap(last_sent, "batch", 0)
        middle_near = swap(total_of(middle_terms, 1, slice(None), 0).astype(BF16), "batch", 1)
    input_grad = input_gradient(
        token, tokens(dq), grad_k, grad_v, grad_middle, local_query, local_key, local_value
    )

    if fast:
        upper = (mine & 2) > 0
        odd = (mine & 1) > 0
        cut_feed = feed_part.shape[-2] // 2
        one = [feed_part[..., :cut_feed, :]]
        two = [feed_part[..., cut_feed:, :]]

        def pair_up(flag, low, other):
            return jnp.stack([jnp.where(flag, other, low), jnp.where(flag, low, other)])

        def advance_second(terms, hop):
            came = swap(total_of(terms, slice(None), 1).astype(BF16), *hop)
            return [term[:, 0] for term in terms], came

        one, one_came = advance(one, ("seq", 0))
        two, two_came = advance_second(two, ("seq", 1))
        input_grad, last_came, middle_near, one_came, two_came = sync(
            input_grad, last_came, middle_near, one_came, two_came
        )
        last_terms, last_came = advance([last_kept, last_came], ("seq", 0))
        middle_came = swap(
            total_of([term[0, :, 1] for term in middle_terms] + [middle_far], Ellipsis).astype(BF16),
            "seq",
            1,
        )
        middle_terms = [term[0, :, 0] for term in middle_terms] + [middle_near]
        one, one_came = advance(one + [one_came], ("seq", 1))
        two, two_came = advance(two + [two_came], ("seq", 0))
        last_came, middle_came, one_came, two_came = sync(
            last_came, middle_came, one_came, two_came
        )

        last_terms, last_came = advance(last_terms + [last_came], ("seq", 1))
        one, two = one + [one_came], two + [two_came]
        feed_came = swap(
            jnp.concatenate([total_of(one, 1), total_of(two, 1)]).astype(BF16), "seq", 2
        )
        middle_terms, middle_came = advance(middle_terms + [middle_came], ("seq", 0))
        last_came, middle_came, feed_came = sync(last_came, middle_came, feed_came)

        last_terms, last_came = advance(last_terms + [last_came], ("seq", 2))
        middle_terms, middle_came = advance(middle_terms + [middle_came], ("seq", 2))
        feed_low = (
            jnp.concatenate([total_of(one, 0), total_of(two, 0)]) + feed_came.astype(F32)
        ).astype(BF16)
        feed_other = swap(feed_low, "batch", 1)
        last_came, middle_came, feed_other = sync(last_came, middle_came, feed_other)
        last_low = total_of(last_terms + [last_came], Ellipsis).astype(BF16)
        middle_sum = total_of(middle_terms + [middle_came], Ellipsis).astype(BF16)
        cut_at = middle_sum.shape[0]
        other = swap(jnp.concatenate([middle_sum, last_low]), "batch", 1)
        feed_both = pair_up(upper, feed_low, feed_other)
        feed_across = swap(feed_both, "batch", 0)
        other, feed_across = sync(other, feed_across)
        middle_both = pair_up(upper, middle_sum, other[:cut_at]).reshape(2 * cut_at, 384)
        last_half = (last_low.astype(F32) + other[cut_at:].astype(F32)).astype(BF16)
        both = jnp.concatenate([middle_both, last_half])
        across = swap(both, "batch", 0)
        full_feed = pair_up(odd, feed_both, feed_across)
        full = pair_up(odd, both, across)
        full_middle = full[:, : 2 * cut_at].reshape(2, 2, cut_at, 384)
        last = full[:, 2 * cut_at :]
        small = width // devices // 2

        wide = cut(full_feed, 0, 4 * small).reshape(2, 2, 4, small, 384)
        grad_expand = wide.transpose(1, 3, 0, 2, 4).reshape(2 * small, 8 * 384).astype(F32)
        tall = cut(full_feed, 4 * small, 192).reshape(768, 384)
        grad_reduce = tall.T.astype(F32)

        def square(quarters, start):
            block = cut(quarters, start, small).transpose(1, 2, 0, 3)
            return block.reshape(2 * small, 768).astype(F32)

        grad_po = square(full_feed, 4 * small + 192)
        grad_pq, grad_lo, grad_lq = [square(full_middle, index * small) for index in range(3)]
        grad_lk, grad_lv = [
            last[:, index * 96 : index * 96 + 96].transpose(1, 0, 2).reshape(96, 768).astype(F32)
            for index in range(2)
        ]
        lines = last[:, 192:208].astype(F32)
        vec_low, vec_high = lines[0, :, :96], lines[1, :, :96]
        (fg, fs, rb, ng, ns, pob) = [vec_low[index] for index in range(6)]
        pqb, lob = lines[0, 0, LANES : LANES + 96], lines[0, 1, LANES : LANES + 96]
        grad_eb = vec_low[8:12].reshape(-1)
    else:

        def plain(left_array, right_array):
            product = tn(left_array, right_array)
            part = lax.psum_scatter(product, "seq", scatter_dimension=0, tiled=True)
            return lax.psum(part.astype(BF16), "batch").astype(F32)

        grad_expand = plain(normed_low, grad_pre)
        grad_reduce = plain(hidden, grad_branch)
        grad_po = plain(tokens(mix_two), grad_second)
        grad_pq = plain(tokens(middle_low), tokens(grad_q2))
        grad_lo = plain(tokens(mix_one), grad_first)
        grad_lq = plain(tokens(inputs), tokens(dq))
        grad_lk = plain(tokens(inputs), grad_k)
        grad_lv = plain(tokens(inputs), grad_v)
        vectors = jnp.concatenate(
            [vec_feed, vec_first, vec_input, vec_wide.reshape(-1, width)], axis=0
        )
        vectors = lax.psum(vectors, ("seq", "batch"))
        share = width // devices
        part = lax.dynamic_slice_in_dim(vectors, me * share, share, axis=1)
        wide = vectors[32:].reshape(-1)
        wide_share = wide.shape[0] // devices
        grad_eb = lax.dynamic_slice_in_dim(wide, me * wide_share, wide_share, axis=0)
        (fg, fs, rb, ng, ns, pob) = [part[index] for index in range(6)]
        pqb, lob = part[8], part[9]
        vec_high = part[16:32]
    grad_ck = vec_high[:KER].T
    grad_cv = vec_high[KER : 2 * KER].T
    cvb, lqb, lvb = vec_high[10], vec_high[11], vec_high[12]
    return (
        outputs, input_grad,
        grad_lq, lqb, grad_lk, grad_lv, lvb, grad_lo, lob, grad_pq, pqb, grad_po, pob,
        grad_ck, grad_cv, cvb, ng, ns, grad_expand, grad_eb, grad_reduce, rb, fg, fs,
    )


def solution(mesh):
    vector = P("seq")
    matrix = P("seq", None)
    return jax.shard_map(
        device_step,
        mesh=mesh,
        in_specs=(P("batch", "seq", None), P("batch"), P("batch", "seq", None)) + (P(),) * 22,
        out_specs=(
            P("batch", "seq", None), P("batch", "seq", None),
            matrix, vector, matrix, matrix, vector, matrix, vector, matrix, vector, matrix, vector,
            matrix, matrix, vector, vector, vector, matrix, vector, matrix, vector, vector, vector,
        ),
        check_vma=False,
    )
```

```python
import functools
import math

import jax
import jax.numpy as jnp
from jax import lax
from jax.experimental import pallas as pl
from jax.experimental.pallas import tpu as pltpu
from jax.sharding import PartitionSpec as P

HEADS = 12
HD = 64
WIN = 128
PWIN = 512
KER = 5
STRIDE = 4
HALF = WIN // 2
REACH = PWIN // 2
NEGATIVE = -1e30
SCALE = 1.0 / math.sqrt(HD)
EPSILON = 1e-05
LANES = 128
TILE = 128
ROWS = 128
CHUNK = 768
PAIRS = 2
F32 = jnp.float32
BF16 = jnp.bfloat16


def nn(left, right):
    return jnp.dot(left, right, preferred_element_type=F32)


def nt(left, right):
    return lax.dot_general(left, right, (((1,), (1,)), ((), ())), preferred_element_type=F32)


def tn(left, right):
    return lax.dot_general(left, right, (((0,), (0,)), ((), ())), preferred_element_type=F32)


def column_sum(block):
    return jnp.sum(block.astype(F32), axis=0, keepdims=True)


def call(body, grid, scalars, inputs, outputs, scratch=(), spare=8):
    used = spare * 2**20
    arrays, in_specs, out_specs, shapes = [], [], [], []

    def spec(shape, dtype, block, index):
        nonlocal used
        if block is None:
            return pl.BlockSpec(memory_space=pltpu.VMEM)
        if block == "raw":
            return pl.BlockSpec(memory_space=pl.ANY)
        used += 2 * math.prod(block) * jnp.dtype(dtype).itemsize
        return pl.BlockSpec(block, index)

    for array, block, index in inputs:
        in_specs.append(spec(array.shape, array.dtype, block, index))
        if block is not None:
            array = pltpu.with_memory_space_constraint(array, pltpu.HBM)
        arrays.append(array)
    for shape, dtype, block, index in outputs:
        out_specs.append(spec(shape, dtype, block, index))
        plain = block is None
        shapes.append((jax.ShapeDtypeStruct if plain else pltpu.HBM)(shape, dtype))
    for item in scratch:
        if hasattr(item, "shape") and item.memory_space == pltpu.VMEM:
            used += math.prod(item.shape) * jnp.dtype(item.dtype).itemsize
    return pl.pallas_call(
        body,
        grid_spec=pltpu.PrefetchScalarGridSpec(
            num_scalar_prefetch=len(scalars),
            grid=grid,
            in_specs=in_specs,
            out_specs=out_specs,
            scratch_shapes=list(scratch),
        ),
        out_shape=shapes,
        compiler_params=pltpu.CompilerParams(
            dimension_semantics=("arbitrary",) * len(grid), vmem_limit_bytes=used
        ),
        cost_estimate=pl.CostEstimate(flops=1000, bytes_accessed=1000, transcendentals=0),
    )(*scalars, *arrays)


def raw(array):
    return (array, "raw", None)


def out_raw(shape, dtype):
    return (shape, dtype, "raw", None)


def whole(array):
    return (array, None, None)


def out_whole(shape, dtype):
    return (shape, dtype, None, None)


def sync(*values):
    return lax.optimization_barrier(values)


def stack_heads(block):
    lane = lax.broadcasted_iota(jnp.int32, block.shape, 1)
    zero = jnp.zeros_like(block)
    return jnp.concatenate(
        [jnp.where(lane < HD, block, zero), jnp.where(lane < HD, zero, block)], axis=0
    )


def unstack(block):
    half = block.shape[1] // 2
    joined = jnp.concatenate([block[:HD, :half], block[HD:, half:]], axis=0)
    return joined.T


def positions(shape, dim):
    return lax.broadcasted_iota(jnp.int32, shape, dim)


def project_body(place, x_far, wq_far, bq, wk_far, wv_far, bv, q, k, v, wk, wv, x, wq, sems):
    docs, rows, width = x.shape
    fetches = [
        pltpu.make_async_copy(far, near, sems.at[index])
        for index, (far, near) in enumerate(
            ((x_far, x), (wq_far, wq), (wk_far, wk), (wv_far, wv))
        )
    ]
    for fetch in fetches:
        fetch.start()
    fetches[0].wait()
    flat = x[...].reshape(docs * rows, width)
    fetches[1].wait()
    q[...] = (nn(flat, wq[...]) + bq[...]).astype(BF16).reshape(q.shape)
    fetches[2].wait()
    k[...] = nn(flat, wk[...]).astype(BF16).reshape(k.shape)
    fetches[3].wait()
    v[...] = (nn(flat, wv[...]) + bv[...]).astype(BF16).reshape(v.shape)


def project(place, x, wq, bq, wk, wv, bv):
    return call(
        project_body,
        (1,),
        (place,),
        [raw(x), raw(wq), whole(bq), raw(wk), raw(wv), whole(bv)],
        [out_whole(x.shape, BF16)] * 3 + [out_whole(wk.shape, BF16)] * 2,
        [
            pltpu.VMEM(x.shape, BF16),
            pltpu.VMEM(wq.shape, BF16),
            pltpu.SemaphoreType.DMA((4,)),
        ],
    )


def pool_body(place, left, right, k, v, wk, wv, bv, ck, cv, bcv, kx, vx, pooled, rows):
    offset = place[0]
    docs, own_rows, width = k.shape
    rims = jnp.concatenate(
        [part[doc] for doc in range(docs) for part in (left, right)], axis=0
    )
    size = own_rows + WIN
    count = pooled.shape[2]
    spot = offset - HALF + positions((size, 1), 0)
    for which, (weight, bias, taps, own, out) in enumerate(
        ((wk, None, ck, k, kx), (wv, bv, cv, v, vx))
    ):
        value = nn(rims, weight[...])
        if bias is not None:
            value = value + bias[...]
        value = value.astype(BF16)
        for doc in range(docs):
            at = doc * WIN
            out[doc, :HALF] = value[at : at + HALF]
            out[doc, HALF : HALF + own_rows] = own[doc]
            out[doc, HALF + own_rows :] = value[at + HALF : at + WIN]
            valid = (spot >= 0) & (spot < place[1 + doc])
            for group in range(width // LANES):
                lanes = slice(group * LANES, (group + 1) * LANES)
                rows[group] = jnp.where(valid, out[doc, :, lanes].astype(F32), 0.0)
                total = jnp.zeros((count, LANES), F32)
                for tap in range(KER):
                    start = HALF - KER // 2 + tap
                    read = rows[group, pl.ds(start, count, stride=STRIDE), :]
                    total = total + read * taps[tap : tap + 1, lanes]
                if which == 1:
                    total = total + bcv[:, lanes]
                pooled[which, doc, :, lanes] = total.astype(BF16)


def pool(place, left, right, k, v, wk, wv, bv, ck, cv, bcv):
    docs, rows, width = k.shape
    extended = rows + WIN
    return call(
        pool_body,
        (1,),
        (place,),
        [whole(a) for a in (left, right, k, v, wk, wv, bv, ck, cv, bcv)],
        [
            out_whole((docs, extended, width), BF16),
            out_whole((docs, extended, width), BF16),
            out_whole((2, docs, rows // STRIDE, width), BF16),
        ],
        [pltpu.VMEM((width // LANES, extended, LANES), F32)],
    )


def local_bias(tile, offset, length):
    shape = (TILE + WIN, TILE)
    key = positions(shape, 0)
    query = positions(shape, 1)
    spot = offset + tile * TILE - HALF + key
    allowed = (
        (key >= query) & (key < query + WIN) & (spot >= 0) & (spot < length)
    ) | (key == query + HALF)
    return jnp.where(allowed, 0.0, NEGATIVE)


def softmax_columns(scores):
    top = jnp.max(scores, axis=0, keepdims=True)
    grown = jnp.exp(scores - top)
    return grown * (1.0 / jnp.sum(grown, axis=0, keepdims=True))


def local_forward_body(place, q, kx, vx, mix, probs, *, doc):
    offset, length = place[0], place[1 + doc]
    span = TILE + WIN
    for tile in range(q.shape[1] // TILE):
        half_bias = local_bias(tile, offset, length)
        bias = jnp.concatenate([half_bias, half_bias], axis=1)
        first = tile * TILE
        for pair in range(q.shape[2] // LANES):
            lanes = slice(pair * LANES, (pair + 1) * LANES)
            queries = stack_heads(q[doc, first : first + TILE, lanes]) * SCALE
            scores = nt(kx[doc, first : first + span, lanes], queries) + bias
            chance = softmax_columns(scores)
            probs[pair, tile] = chance
            turned = vx[doc, first : first + span, lanes].T
            mixed = nn(turned, chance.astype(BF16))
            mix[first : first + TILE, lanes] = unstack(mixed).astype(BF16)


def local_forward(place, q, kx, vx, doc):
    _, rows, width = q.shape
    pairs, tiles, span = width // LANES, rows // TILE, TILE + WIN
    return call(
        functools.partial(local_forward_body, doc=doc),
        (1,),
        (place,),
        [whole(a) for a in (q, kx, vx)],
        [
            out_whole((rows, width), BF16),
            out_whole((pairs, tiles, span, 2 * TILE), F32),
        ],
    )


def middle_body(place, x, wo, bo, wpq, bpq, *refs):
    docs, rows = x.shape[0], x.shape[1]
    mixes, (mix, middle, middle_low, q2) = refs[:docs], refs[docs:]
    for doc in range(docs):
        mix[doc] = mixes[doc][...]
    flat = docs * rows
    branch = nn(mix[...].reshape(flat, x.shape[2]), wo[...]) + bo[...]
    total = x[...].reshape(flat, x.shape[2]).astype(F32) + branch
    middle[...] = total.reshape(middle.shape)
    low = total.astype(BF16)
    middle_low[...] = low.reshape(middle_low.shape)
    q2[...] = (nn(low, wpq[...]) + bpq[...]).astype(BF16).reshape(q2.shape)


def middle_forward(place, x, wo, bo, wpq, bpq, mixes):
    docs, rows, width = x.shape
    return call(
        middle_body,
        (1,),
        (place,),
        [whole(a) for a in (x, wo, bo, wpq, bpq, *mixes)],
        [
            out_whole((docs, rows, width), BF16),
            out_whole((docs, rows, width), F32),
            out_whole((docs, rows, width), BF16),
            out_whole((docs, rows, width), BF16),
        ],
    )


def attention_back(keys, values, queries, grads, chance):
    stacked_grads = stack_heads(grads)
    stacked_queries = stack_heads(queries)
    grad_chance = nt(values, stacked_grads * SCALE)
    dots = jnp.sum(chance * grad_chance, axis=0, keepdims=True)
    grad_raw = (chance * (grad_chance - dots)).astype(BF16)
    grad_keys = nn(grad_raw, stacked_queries)
    grad_values = nn(chance.astype(BF16), stacked_grads)
    grad_queries = unstack(nn(keys.T, grad_raw))
    return grad_queries, grad_keys, grad_values


def first_back_body(place, gq2, gsum, wpq, wo, gmid, gfirst, gmix, vec):
    docs, rows, width = gsum.shape
    flat = docs * rows
    grads = gq2[...].reshape(flat, width)
    total = gsum[...].reshape(flat, width) + nt(grads, wpq[...])
    gmid[...] = total.reshape(gmid.shape)
    low = total.astype(BF16)
    gfirst[...] = low
    gmix[...] = nt(low, wo[...]).astype(BF16).reshape(gmix.shape)
    vec[...] = jnp.zeros_like(vec)
    vec[0:1] = column_sum(grads)
    vec[1:2] = column_sum(low)


def first_backward(place, gq2, gsum, wpq, wo):
    docs, rows, width = gsum.shape
    return call(
        first_back_body,
        (1,),
        (place,),
        [whole(a) for a in (gq2, gsum, wpq, wo)],
        [
            out_whole((docs, rows, width), F32),
            out_whole((docs * rows, width), BF16),
            out_whole((docs, rows, width), BF16),
            out_whole((8, width), F32),
        ],
    )


def local_backward_body(place, q, kx, vx, gmix, probs, *refs, doc):
    earlier = refs[: len(refs) - 6]
    dq, own, low_left, low_right, dk, dv = refs[len(refs) - 6 :]
    rows = q.shape[1]
    for old, new in zip(earlier, (dq, own, low_left, low_right)):
        new[:doc] = old[...]
    span = TILE + WIN
    dk[...] = jnp.zeros_like(dk)
    dv[...] = jnp.zeros_like(dv)
    for tile in range(rows // TILE):
        first = tile * TILE
        for pair in range(q.shape[2] // LANES):
            lanes = slice(pair * LANES, (pair + 1) * LANES)
            grad_q, grad_k, grad_v = attention_back(
                kx[doc, first : first + span, lanes],
                vx[doc, first : first + span, lanes],
                q[doc, first : first + TILE, lanes],
                gmix[doc, first : first + TILE, lanes],
                probs[pair, tile],
            )
            dq[doc, first : first + TILE, lanes] = grad_q.astype(BF16)
            dk[first : first + span, lanes] += grad_k
            dv[first : first + span, lanes] += grad_v
    for which, part in enumerate((dk, dv)):
        own[doc, which] = part[HALF : HALF + rows]
        low_left[doc, which] = part[:HALF].astype(BF16)
        low_right[doc, which] = part[HALF + rows :].astype(BF16)


def local_backward(place, q, kx, vx, gmix, probs, doc, earlier=()):
    _, rows, width = q.shape
    span = TILE + WIN
    return call(
        functools.partial(local_backward_body, doc=doc),
        (1,),
        (place,),
        [whole(a) for a in (q, kx, vx, gmix, probs, *earlier)],
        [
            out_whole((doc + 1, rows, width), BF16),
            out_whole((doc + 1, 2, rows, width), F32),
            out_whole((doc + 1, 2, HALF, width), BF16),
            out_whole((doc + 1, 2, HALF, width), BF16),
        ],
        [
            pltpu.VMEM((rows + WIN, width), F32),
            pltpu.VMEM((rows + WIN, width), F32),
        ],
    )


def pooled_forward_body(place, slots, *refs, pieces):
    key_pieces = refs[:pieces]
    value_pieces = refs[pieces : 2 * pieces]
    (
        q2, middle, wpo, bpo, we, wr,
        keys_out, values_out, probs, mix, summed, we_near, wr_near,
        keys, values, bias, sems,
    ) = refs[2 * pieces :]
    doc, pair = pl.program_id(0), pl.program_id(1)
    fetches = [
        pltpu.make_async_copy(we, we_near, sems.at[0]),
        pltpu.make_async_copy(wr, wr_near, sems.at[1]),
    ]
    last = (pair == pl.num_programs(1) - 1) & (doc == pl.num_programs(0) - 1)
    leaves = [
        pltpu.make_async_copy(keys.at[each], keys_out.at[each], sems.at[2 + each])
        for each in range(keys.shape[0])
    ] + [
        pltpu.make_async_copy(
            values.at[each], values_out.at[each], sems.at[2 + keys.shape[0] + each]
        )
        for each in range(keys.shape[0])
    ]

    @pl.when((pair == 0) & (doc == 0))
    def _():
        for fetch in fetches:
            fetch.start()

    offset, length, base = place[0], place[1 + doc], place[1 + pl.num_programs(0)]
    count = keys.shape[1]

    @pl.when(pair == 0)
    def _():
        for where, group, out in ((0, key_pieces, keys), (1, value_pieces, values)):
            at = 0
            for piece in group:
                size = piece.shape[2]
                for block in range(piece.shape[0]):
                    spot = pl.multiple_of(slots[where, at] * size, size)
                    out[doc, pl.ds(spot, size), :] = piece[block, doc]
                    at += 1
        if True:
            shape = (count, q2.shape[1])
            spot = base + positions(shape, 0)
            centre = offset // STRIDE + positions(shape, 1) // STRIDE
            allowed = (
                (spot >= centre - REACH)
                & (spot < centre + REACH)
                & (spot >= 0)
                & (spot * STRIDE < length)
            ) | (spot == centre)
            bias[...] = jnp.where(allowed, 0.0, NEGATIVE)
        for each in range(keys.shape[0]):

            @pl.when(doc == each)
            def _():
                leaves[each].start()
                leaves[keys.shape[0] + each].start()

    for each in range(PAIRS):
        lanes = pl.ds(pl.multiple_of((pair * PAIRS + each) * LANES, LANES), LANES)
        queries = stack_heads(q2[doc, :, lanes]) * SCALE
        half_bias = bias[...]
        scores = nt(keys[doc, :, lanes], queries) + jnp.concatenate([half_bias, half_bias], axis=1)
        chance = softmax_columns(scores)
        probs[0, each] = chance
        mixed = nn(values[doc, :, lanes].T, chance.astype(BF16))
        mix[doc, :, lanes] = unstack(mixed).astype(BF16)

    @pl.when(last)
    def _():
        for copy in fetches + leaves:
            copy.wait()
        flat = (mix.shape[0] * mix.shape[1], mix.shape[2])
        second = nn(mix[...].reshape(flat), wpo[...]) + bpo[...]
        summed[...] = middle[...] + second.reshape(summed.shape)


def pooled_forward(place, slots, key_pieces, value_pieces, q2, middle, wpo, bpo, we, wr):
    docs, rows, width = q2.shape
    pairs, tiles = width // LANES, rows // TILE
    size = key_pieces[0].shape[2]
    count = size * slots.shape[1]

    return call(
        functools.partial(pooled_forward_body, pieces=len(key_pieces)),
        (docs, pairs // PAIRS),
        (place, slots),
        [whole(a) for a in (*key_pieces, *value_pieces, q2, middle, wpo, bpo)]
        + [raw(we), raw(wr)],
        [
            out_raw((docs, count, width), BF16),
            out_raw((docs, count, width), BF16),
            (
                (docs, pairs, count, 2 * rows),
                F32,
                (1, PAIRS, count, 2 * rows),
                lambda doc, pair, *_: (doc, pair, 0, 0),
            ),
            out_whole((docs, rows, width), BF16),
            out_whole((docs, rows, width), F32),
            out_whole(we.shape, BF16),
            out_whole(wr.shape, BF16),
        ],
        [
            pltpu.VMEM((docs, count, width), BF16),
            pltpu.VMEM((docs, count, width), BF16),
            pltpu.VMEM((count, rows), F32),
            pltpu.SemaphoreType.DMA((2 + 2 * docs,)),
        ],
    )


def pooled_backward_body(
    places, token, q2, keys, values, probs, grads, dq, dk_kept, dk_sent, dv_kept, dv_sent, sums
):
    doc, step = pl.program_id(0), pl.program_id(1)
    size = dk_kept.shape[2]
    half = dk_kept.shape[0]
    rows = keys.shape[1]
    for each in range(PAIRS):
        inner = slice(each * LANES, (each + 1) * LANES)
        lanes = pl.ds(pl.multiple_of((step * PAIRS + each) * LANES, LANES), LANES)
        grad_q, *total = attention_back(
            keys[0, :, inner], values[0, :, inner], q2[0, :, inner], grads[0, :, inner],
            probs[0, each],
        )
        dq[doc, :, lanes] = grad_q.astype(BF16)
        for which, (kept, sent) in enumerate(((dk_kept, dk_sent), (dv_kept, dv_sent))):
            sums[each, which, :rows] = total[which]
            sums[each, which, rows:] = jnp.zeros((8, LANES), F32)
            for block in range(half + sent.shape[0]):
                start = pl.multiple_of(places[which, block] * (size - 8), size - 8)
                part = sums[each, which, pl.ds(start, size), :]
                if block < half:
                    kept[block, doc, :, lanes] = part
                else:
                    sent[block - half, doc, :, lanes] = part.astype(BF16)


def pooled_backward(places, token, q2, keys, values, probs, grads, size, kept):
    docs, rows, width = q2.shape
    count = keys.shape[1]
    blocks = count // size
    tiles = rows // TILE

    def lanes_of(array):
        return (array, (1, array.shape[1], PAIRS * LANES), lambda doc, pair, *_: (doc, 0, pair))

    return call(
        pooled_backward_body,
        (docs, width // LANES // PAIRS),
        (places, token),
        [
            lanes_of(q2),
            lanes_of(keys),
            lanes_of(values),
            (
                probs,
                (1, PAIRS, count, 2 * rows),
                lambda doc, pair, *_: (doc, pair, 0, 0),
            ),
            lanes_of(grads),
        ],
        [
            out_whole((docs, rows, width), BF16),
            out_whole((kept, docs, size + 8, width), F32),
            out_whole((blocks - kept, docs, size + 8, width), BF16),
            out_whole((kept, docs, size + 8, width), F32),
            out_whole((blocks - kept, docs, size + 8, width), BF16),
        ],
        [pltpu.VMEM((PAIRS, 2, count + 8, LANES), F32)],
    )


def feed_body(
    place, summed, cotangent, we, be, wr, br, ng, ns, fg, fs, wpo,
    outputs_far, normed_low, hidden, grad_branch, grad_pre, grad_summed_far, grad_second,
    grad_mix_far, vec, vec_wide,
    normed, slope, work, unit, outputs, grad_mix, sems,
):
    docs, rows = cotangent.shape[0], cotangent.shape[1]
    width = summed.shape[2]
    wide = we.shape[1]
    steps = rows // ROWS
    blocks = [
        (doc, step * ROWS, doc * rows + step * ROWS)
        for doc in range(docs)
        for step in range(steps)
    ]
    leaving = []

    def leave(source, target, doc, start, row):
        copy = pltpu.make_async_copy(
            source.at[pl.ds(row, ROWS)],
            target.at[doc, pl.ds(start, ROWS)],
            sems.at[len(leaving)],
        )
        copy.start()
        leaving.append(copy)


    def normal(value):
        centred = value - jnp.mean(value, axis=-1, keepdims=True)
        scale = lax.rsqrt(jnp.mean(centred * centred, axis=-1, keepdims=True) + EPSILON)
        return centred * scale, scale

    scales = []
    for doc, start, row in blocks:
        norm, scale = normal(summed[doc, start : start + ROWS])
        scales.append(scale)
        unit[row : row + ROWS] = norm
        full = norm * ng[...] + ns[...]
        normed[row : row + ROWS] = full
        normed_low[row : row + ROWS] = full.astype(BF16)

    def expand(index, _):
        part = pl.ds(pl.multiple_of(index * CHUNK, CHUNK), CHUNK)
        pre = nn(normed_low[...], we[:, part]) + be[:, part]
        cdf = 0.5 * (1.0 + lax.erf(pre * math.sqrt(0.5)))
        hidden[:, part] = (pre * cdf).astype(BF16)
        slope[:, part] = cdf + pre * (jnp.exp(pre * pre * -0.5) * (1.0 / math.sqrt(2.0 * math.pi)))
        return 0

    lax.fori_loop(0, wide // CHUNK, expand, 0)

    for start in range(0, width, CHUNK):
        part = slice(start, start + CHUNK)
        work[:, part] = normed[:, part] + (nn(hidden[...], wr[:, part]) + br[:, part])

    sums = [jnp.zeros((1, width), F32) for _ in range(6)]
    for doc, start, row in blocks:
        norm, scale = normal(work[row : row + ROWS])
        spot = place[0] + start + positions((ROWS, 1), 0)
        valid = (spot < place[1 + doc]).astype(F32)
        outputs[row : row + ROWS] = (valid * (norm * fg[...] + fs[...])).astype(BF16)
        leave(outputs, outputs_far, doc, start, row)
        error = valid * cotangent[doc, start : start + ROWS].astype(F32)
        sums[0] += column_sum(error * norm)
        sums[1] += column_sum(error)
        scaled = error * fg[...]
        rest = (
            scaled
            - jnp.mean(scaled, axis=-1, keepdims=True)
            - norm * jnp.mean(scaled * norm, axis=-1, keepdims=True)
        ) * scale
        work[row : row + ROWS] = rest
        low = rest.astype(BF16)
        grad_branch[row : row + ROWS] = low
        sums[2] += column_sum(low)

    def reduce(index, _):
        part = pl.ds(pl.multiple_of(index * CHUNK, CHUNK), CHUNK)
        low = (nt(grad_branch[...], wr[part, :]) * slope[:, part]).astype(BF16)
        grad_pre[:, part] = low
        vec_wide[:, part] = column_sum(low)
        return 0

    lax.fori_loop(0, wide // CHUNK, reduce, 0)

    for start in range(0, width, CHUNK):
        part = slice(start, start + CHUNK)
        work[:, part] += nt(grad_pre[...], we[part, :])

    for (doc, start, row), scale in zip(blocks, scales):
        error = work[row : row + ROWS]
        norm = unit[row : row + ROWS]
        sums[3] += column_sum(error * norm)
        sums[4] += column_sum(error)
        scaled = error * ng[...]
        grad = (
            scaled
            - jnp.mean(scaled, axis=-1, keepdims=True)
            - norm * jnp.mean(scaled * norm, axis=-1, keepdims=True)
        ) * scale
        unit[row : row + ROWS] = grad
        leave(unit, grad_summed_far, doc, start, row)
        low = grad.astype(BF16)
        grad_second[row : row + ROWS] = low
        sums[5] += column_sum(low)
        grad_mix[row : row + ROWS] = nt(low, wpo[...]).astype(BF16)
        leave(grad_mix, grad_mix_far, doc, start, row)
    for index, value in enumerate(sums):
        vec[index : index + 1] = value
    vec[6:8] = jnp.zeros((2, width), F32)
    for copy in leaving:
        copy.wait()


def feed(place, summed, cotangent, we, be, wr, br, ng, ns, fg, fs, wpo):
    docs, rows, width = summed.shape
    wide = we.shape[1]
    tokens = docs * rows
    return call(
        feed_body,
        (1,),
        (place,),
        [whole(a) for a in (summed, cotangent, we, be, wr, br, ng, ns, fg, fs, wpo)],
        [
            out_raw((docs, rows, width), BF16),
            out_whole((tokens, width), BF16),
            out_whole((tokens, wide), BF16),
            out_whole((tokens, width), BF16),
            out_whole((tokens, wide), BF16),
            out_raw((docs, rows, width), F32),
            out_whole((tokens, width), BF16),
            out_raw((docs, rows, width), BF16),
            out_whole((8, width), F32),
            out_whole((1, wide), F32),
        ],
        [
            pltpu.VMEM((tokens, width), F32),
            pltpu.VMEM((tokens, wide), F32),
            pltpu.VMEM((tokens, width), F32),
            pltpu.VMEM((tokens, width), F32),
            pltpu.VMEM((tokens, width), BF16),
            pltpu.VMEM((tokens, width), BF16),
            pltpu.SemaphoreType.DMA((3 * tokens // ROWS,)),
        ],
    )


def key_value_body(place, *refs, docs):
    gk_kept, gk_came, gv_kept, gv_came, kx, vx, ck, cv = refs[:8]
    own, from_left, from_right, dq = refs[8:12]
    gk, gv, vec, rows_in, pooled, total = refs[12:]
    offset = place[0]
    rows, width = gk.shape[0] // docs, gk.shape[1]
    count = rows // STRIDE
    vec[...] = jnp.zeros_like(vec)
    for doc in range(docs):
        length = place[1 + doc]
        spot = offset - HALF + positions((rows + WIN, 1), 0)
        valid = (spot >= 0) & (spot < length)
        first = doc * rows
        for which, (kept, came, ext, taps, out, row) in enumerate(
            (
                (gk_kept, gk_came, kx, ck, gk, 0),
                (gv_kept, gv_came, vx, cv, gv, KER),
            )
        ):
            pooled[...] = kept[doc].astype(F32) + came[doc].astype(F32)
            masked = jnp.where(valid, ext[doc].astype(F32), 0.0)
            for group in range(width // LANES):
                lanes = slice(group * LANES, (group + 1) * LANES)
                grown = pooled[:count, lanes]
                shifted = pooled[1 : count + 1, lanes]
                rows_in[group] = masked[:, lanes]
                for tap in range(KER):
                    start = HALF - KER // 2 + tap
                    read = rows_in[group, pl.ds(start, count, stride=STRIDE), :]
                    vec[row + tap : row + tap + 1, lanes] += column_sum(grown * read)
                if which == 1:
                    vec[2 * KER : 2 * KER + 1, lanes] += column_sum(grown)
                total[group] = own[doc, which, :, lanes]
                total[group, :HALF] += from_left[doc, which, :, lanes].astype(F32)
                total[group, rows - HALF :] += from_right[doc, which, :, lanes].astype(F32)
                for phase, terms in enumerate(
                    (
                        ((2, grown),),
                        ((3, grown),),
                        ((4, grown), (0, shifted)),
                        ((1, shifted),),
                    )
                ):
                    part = pl.ds(phase, count, stride=STRIDE)
                    added = None
                    for tap, values in terms:
                        term = values * taps[tap : tap + 1, lanes]
                        added = term if added is None else added + term
                    inside = offset + phase + STRIDE * positions((count, 1), 0) < length
                    total[group, part, :] = total[group, part, :] + jnp.where(inside, added, 0.0)
                out[first : first + rows, lanes] = total[group].astype(BF16)
        vec[11:12] += column_sum(dq[doc])
    vec[12:13] += column_sum(gv[...])


def key_value_gradients(place, pooled_grads, kx, vx, ck, cv, own, left, right, dq):
    docs, rows, width = dq.shape
    return call(
        functools.partial(key_value_body, docs=docs),
        (1,),
        (place,),
        [
            whole(a)
            for a in (*pooled_grads, kx, vx, ck, cv, own, left, right, dq)
        ],
        [out_whole((docs * rows, width), BF16)] * 2 + [out_whole((16, width), F32)],
        [
            pltpu.VMEM((width // LANES, rows + WIN, LANES), F32),
            pltpu.VMEM((rows // STRIDE + 8, width), F32),
            pltpu.VMEM((width // LANES, rows, LANES), F32),
        ],
    )


def input_body(place, dq, gk, gv, gmid, wq, wk, wv, dx):
    total = nt(dq[...], wq[...]) + nt(gk[...], wk[...]) + nt(gv[...], wv[...])
    dx[...] = (gmid[...] + total.reshape(gmid.shape)).astype(BF16)


def input_gradient(place, dq, gk, gv, gmid, wq, wk, wv):
    docs, rows, width = gmid.shape
    (dx,) = call(
        input_body,
        (1,),
        (place,),
        [whole(a) for a in (dq, gk, gv, gmid, wq, wk, wv)],
        [out_whole((docs, rows, width), BF16)],
    )
    return dx


def scatter_body(bits, *refs, kinds, order, vectors, quartered):
    count = len(kinds)
    operands = [refs[2 * index : 2 * index + 2] for index in range(count)]
    extra = refs[2 * count : 2 * count + vectors]
    rest = refs[2 * count + vectors :]
    if quartered:
        results, (ordered, rounded, *small) = (rest[0], rest[0]), rest[1:]
    else:
        results, (ordered, rounded, *small) = rest[:2], rest[2:]
    core = bits[0]
    sides = 2 if ("batch", 1) in order else 1
    owners = 8

    def start_of(which, size):
        if quartered:
            return which * size
        return pl.multiple_of((which ^ core) * size, LANES)

    def place_tile(which, side, owner, target, size, value):
        index = []
        for at, (axis, bit) in enumerate(order):
            if axis == "batch":
                index += [side, which] if quartered else [side ^ bits[1 + at]]
            else:
                index.append(((owner >> bit) & 1) ^ bits[1 + at])
        results[which][(*index, slice(target, target + size), slice(None))] = value

    base = 0
    for (left, right), kind in zip(operands, kinds):
        tall = left.shape[1]
        turned = left[...].T
        if kind == "wide":
            half = right.shape[1] // 2
            size = tall // owners // sides
            for which in range(2):
                start = start_of(which, half)
                for part in range(half // 768):
                    rounded[...] = nn(turned, right[:, pl.ds(start + part * 768, 768)]).astype(BF16)
                    for column in range(2):
                        target = base + (2 * part + column) * size
                        for owner in range(owners):
                            for side in range(sides):
                                row = (owner * sides + side) * size
                                value = rounded[row : row + size, column * 384 : column * 384 + 384]
                                place_tile(which, side, owner, target, size, value)
            base += half // 384 * size
        elif kind == "tall":
            ordered[...] = turned
            size = tall // 2 // sides
            for part in range(right.shape[1] // 768):
                product = nn(ordered[...], right[:, part * 768 : part * 768 + 768])
                rounded[...] = product.astype(BF16)
                for column in range(2):
                    owner = 2 * part + column
                    for side in range(sides):
                        for which in range(2):
                            row = start_of(which, 384) + side * size
                            value = rounded[pl.ds(row, size), column * 384 : column * 384 + 384]
                            place_tile(which, side, owner, base, size, value)
            base += size
        else:
            size = tall // owners // sides
            if quartered:
                columns = right[...]
            else:
                columns = jnp.concatenate(
                    [right[:, pl.ds(start_of(which, 384), 384)] for which in range(2)], axis=1
                )
            rounded[...] = nn(turned, columns).astype(BF16)
            for which in range(2):
                for owner in range(owners):
                    for side in range(sides):
                        row = (owner * sides + side) * size
                        value = rounded[row : row + size, which * 384 : which * 384 + 384]
                        place_tile(which, side, owner, base, size, value)
            base += size
    if vectors:
        (block,) = small
        vec_feed, vec_first, vec_input, vec_wide = extra
        for owner in range(owners):
            lanes = slice(owner * 96, owner * 96 + 96)
            block[0, owner] = jnp.zeros(block.shape[2:], F32)
            block[1, owner] = jnp.zeros(block.shape[2:], F32)
            block[0, owner, 0:8, 0:96] = vec_feed[:, lanes]
            block[0, owner, 0:8, LANES : LANES + 96] = vec_first[:, lanes]
            block[1, owner, 0:16, 0:96] = vec_input[:, lanes]
            for part in range(4):
                at = owner * 384 + part * 96
                block[0, owner, 8 + part : 9 + part, 0:96] = vec_wide[:, at : at + 96]
        for owner in range(owners):
            for which in range(2):
                place_tile(which, 0, owner, base, 16, block[which ^ core, owner].astype(BF16))


def scatter_products(bits, order, items, extra=(), quartered=False):
    sides = 2 if ("batch", 1) in order else 1
    rows = 0
    for kind, left, right in items:
        if kind == "wide":
            rows += right.shape[1] // 768 * (left.shape[1] // 8 // sides)
        elif kind == "tall":
            rows += 384 // sides
        else:
            rows += 96 // sides
    rows += 16 if extra else 0
    shape = (2,) * (len(order) + quartered) + (rows, 384)
    operands = [array for _, left, right in items for array in (left, right)]
    return call(
        functools.partial(
            scatter_body,
            kinds=tuple(kind for kind, _, _ in items),
            order=tuple(order),
            vectors=len(extra),
            quartered=quartered,
        ),
        (1,),
        (bits,),
        [whole(a) for a in (*operands, *extra)],
        [out_whole(shape, BF16)] * (1 if quartered else 2),
        [pltpu.VMEM((768, operands[0].shape[0]), BF16), pltpu.VMEM((768, 768), BF16)]
        + ([pltpu.VMEM((2, 8, 16, 384), F32)] if extra else []),
    )


def quarter_products_body(bits, *refs, kinds, levels):
    count = len(kinds)
    operands = [refs[2 * index : 2 * index + 2] for index in range(count)]
    out, turned, rounded, sems = refs[2 * count :]
    sides, cores, owners = 2, 2, 1 << levels
    pending = [[], []]
    turn = 0

    def product(left, right):
        nonlocal turn
        slot = turn % 2
        turn += 1
        for copy in pending[slot]:
            copy.wait()
        pending[slot] = []
        rounded[slot] = nn(left, right).astype(BF16)
        return slot

    def leave(slot, source, side, which, owner, base, size):
        digits = [((owner >> level) & 1) ^ bits[level] for level in range(levels)]
        target = out.at[(side, which, *digits, pl.ds(base, size))]
        copy = pltpu.make_async_copy(source, target, sems.at[slot, len(pending[slot])])
        copy.start()
        pending[slot].append(copy)

    def by_rows(slot, which, base, columns):
        size = 768 // owners // sides
        for owner in range(owners):
            for side in range(sides):
                row = (owner * sides + side) * size
                source = rounded.at[slot, pl.ds(row, size), pl.ds(columns, 384)]
                leave(slot, source, side, which, owner, base, size)

    base = 0
    for (left, right), kind in zip(operands, kinds):
        turned[...] = left[...].T
        if kind == "wide":
            for which in range(cores):
                for part in range(2):
                    start = which * 1536 + part * 768
                    slot = product(turned[...], right[:, start : start + 768])
                    for column in range(2):
                        by_rows(slot, which, base + (2 * part + column) * 48, column * 384)
            base += 192
        elif kind == "tall":
            for part in range(4):
                slot = product(turned[...], right[:, part * 768 : part * 768 + 768])
                for column in range(2):
                    for which in range(cores):
                        for side in range(sides):
                            row = (which * sides + side) * 192
                            source = rounded.at[slot, pl.ds(row, 192), pl.ds(column * 384, 384)]
                            leave(slot, source, side, which, 2 * part + column, base, 192)
            base += 192
        else:
            slot = product(turned[...], right[...])
            for which in range(cores):
                by_rows(slot, which, base, which * 384)
            base += 48
    for group in pending:
        for copy in group:
            copy.wait()


def quarter_products(bits, items, levels):
    rows = sum(48 if kind == "square" else 192 for kind, _, _ in items)
    operands = [array for _, left, right in items for array in (left, right)]
    (out,) = call(
        functools.partial(
            quarter_products_body, kinds=tuple(kind for kind, _, _ in items), levels=levels
        ),
        (1,),
        (bits,),
        [whole(a) for a in operands],
        [out_raw((2, 2) + (2,) * levels + (rows, 384), BF16)],
        [
            pltpu.VMEM((768, operands[0].shape[0]), BF16),
            pltpu.VMEM((2, 768, 768), BF16),
            pltpu.SemaphoreType.DMA((2, 32)),
        ],
    )
    return out


def order_quarters(spots, low, other, across, quarters):
    odd, upper = spots[0], spots[1]
    quarters[odd, upper] = low[...]
    quarters[odd, 1 - upper] = other[...]
    quarters[1 - odd, upper] = across[0]
    quarters[1 - odd, 1 - upper] = across[1]


def join_square(quarters, start, out):
    for core in range(2):
        for side in range(2):
            block = quarters[core, side, start : start + 48]
            out[side * 48 : side * 48 + 48, core * 384 : core * 384 + 384] = block.astype(F32)


def collect_feed_body(spots, low, other, across, expand, reduce, pooled_out, quarters, tall):
    order_quarters(spots, low, other, across, quarters)
    for core in range(2):
        for side in range(2):
            rows = slice(side * 48, side * 48 + 48)
            for part in range(4):
                column = core * 1536 + part * 384
                block = quarters[core, side, part * 48 : part * 48 + 48]
                expand[rows, column : column + 384] = block.astype(F32)
            at = core * 384 + side * 192
            tall[at : at + 192] = quarters[core, side, 192:384].astype(F32)
    reduce[...] = tall[...].T
    join_square(quarters, 384, pooled_out)


def collect_feed(spots, low, other, across):
    return call(
        collect_feed_body,
        (1,),
        (spots,),
        [whole(low), whole(other), whole(across)],
        [out_whole((96, 3072), F32), out_whole((384, 768), F32), out_whole((96, 768), F32)],
        [pltpu.VMEM((2, 2) + low.shape, BF16), pltpu.VMEM((768, 384), F32)],
    )


def collect_last_body(spots, low, other, across, *refs, cut):
    pq, lo, lq, lk, lv, vectors, quarters = refs
    order_quarters(spots, low, other, across, quarters)
    for index, out in enumerate((pq, lo, lq)):
        join_square(quarters, index * 48, out)
    for core in range(2):
        half = quarters[core, 0, cut:].astype(F32) + quarters[core, 1, cut:].astype(F32)
        lk[:, core * 384 : core * 384 + 384] = half[:96]
        lv[:, core * 384 : core * 384 + 384] = half[96:192]
        vectors[core] = half[192:208]


def collect_last(spots, low, other, across, cut):
    return call(
        functools.partial(collect_last_body, cut=cut),
        (1,),
        (spots,),
        [whole(low), whole(other), whole(across)],
        [out_whole((96, 768), F32)] * 5 + [out_whole((2, 16, 384), F32)],
        [pltpu.VMEM((2, 2) + low.shape, BF16)],
    )


def swap(value, axis, bit):
    count = lax.axis_size(axis)
    return lax.ppermute(value, axis, [(i, i ^ (1 << bit)) for i in range(count)])


def shift(value, axis, by):
    count = lax.axis_size(axis)
    pairs = [(i, i + by) for i in range(count) if 0 <= i + by < count]
    return lax.ppermute(value, axis, pairs)


def fold(kept, came):
    low = (kept[1].astype(F32) + came[1].astype(F32)).astype(BF16)
    return low, kept[0].astype(F32) + came[0].astype(F32)


def total_of(terms, *index):
    total = None
    for term in terms:
        value = term[index].astype(F32)
        total = value if total is None else total + value
    return total


def advance(terms, hop):
    came = swap(total_of(terms, 1).astype(BF16), *hop)
    return [term[0] for term in terms], came


def cut(quarters, start, size):
    return quarters[:, :, start : start + size]


def device_step(
    inputs, lengths, cotangent,
    local_query, local_query_bias, local_key, local_value, local_value_bias,
    local_output, local_output_bias, pooled_query, pooled_query_bias,
    pooled_output, pooled_output_bias, conv_key, conv_value, conv_value_bias,
    norm_gain, norm_shift, expand_weight, expand_bias, reduce_weight, reduce_bias,
    final_gain, final_shift,
):
    docs, rows, width = inputs.shape
    devices = lax.axis_size("seq")
    me = lax.axis_index("seq")
    mine = lax.axis_index("batch")
    levels = devices.bit_length() - 1
    size = rows // STRIDE
    flat = docs * rows
    offset = me * rows
    reach = -(-REACH // size)
    gathered = devices <= 2 * reach
    fast = devices == 8 and width == 768 and lax.axis_size("batch") == 4
    base = jnp.where(gathered, 0, offset // STRIDE - reach * size)
    place = jnp.concatenate([offset[None], lengths, base[None]]).astype(jnp.int32)

    def line(vector):
        return vector[None]

    def tokens(array):
        return array.reshape(flat, array.shape[-1])

    taps_key, taps_value = conv_key.T, conv_value.T

    left = shift(inputs[:, rows - HALF :], "seq", 1)
    right = shift(inputs[:, :HALF], "seq", -1)
    q, k_own, v_own, key_near, value_near = project(
        place, inputs, local_query, line(local_query_bias), local_key, local_value,
        line(local_value_bias),
    )
    left, right, k_own = sync(left, right, k_own)
    kx, vx, pooled = pool(
        place, left, right, k_own, v_own, key_near, value_near, line(local_value_bias),
        taps_key, taps_value, line(conv_value_bias),
    )
    own = [pooled[which][None] for which in range(2)]

    mixes, probs_one = [], []

    def local_step(doc, token):
        mix, probs = local_forward(token, q, kx, vx, doc)
        mixes.append(mix)
        probs_one.append(probs)
        return mix

    if gathered:
        orders = ([2, 1, 0], [0, 2, 1]) if levels == 3 else (list(range(levels)),) * 2
        have = own
        pieces = [[own[0]], [own[1]]]
        relative = [[0], [0]]
        token = place
        for stage in range(levels):
            came = [swap(have[which], "seq", orders[which][stage]) for which in range(2)]
            if stage < docs:
                done = local_step(stage, token)
            else:
                mix_one, middle, middle_low, q2 = middle_forward(
                    token, inputs, local_output, line(local_output_bias), pooled_query,
                    line(pooled_query_bias), mixes,
                )
                done = q2
            came[0], came[1], done, token = sync(came[0], came[1], done, token)
            if stage < docs:
                mixes[stage] = done
            else:
                q2 = done
            for which in range(2):
                pieces[which].append(came[which])
                relative[which] += [r ^ (1 << orders[which][stage]) for r in relative[which]]
                if stage < levels - 1:
                    have[which] = jnp.concatenate([have[which], came[which]])
        slots = jnp.stack([me ^ jnp.array(r, jnp.int32) for r in relative])
    else:
        pieces = [
            [own[which]]
            + [
                shift(own[which], "seq", sign * distance)
                for distance in range(1, reach + 1)
                for sign in (1, -1)
            ]
            for which in range(2)
        ]
        spots = [reach] + [
            reach - sign * distance for distance in range(1, reach + 1) for sign in (1, -1)
        ]
        slots = jnp.array([spots, spots], jnp.int32)
        token = place
        for doc in range(docs):
            local_step(doc, token)
        mix_one, middle, middle_low, q2 = middle_forward(
            token, inputs, local_output, line(local_output_bias), pooled_query,
            line(pooled_query_bias), mixes,
        )

    keys, values, probs_two, mix_two, summed, expand_near, reduce_near = pooled_forward(
        token, slots, pieces[0], pieces[1], q2, middle, pooled_output, line(pooled_output_bias),
        expand_weight, reduce_weight,
    )
    (
        outputs, normed_low, hidden, grad_branch, grad_pre, grad_summed, grad_second, grad_mix_two,
        vec_feed, vec_wide,
    ) = feed(
        token, summed, cotangent, expand_near, line(expand_bias), reduce_near,
        line(reduce_bias), line(norm_gain), line(norm_shift), line(final_gain),
        line(final_shift), pooled_output,
    )

    order_first = [("batch", 1)] + [("seq", level) for level in range(levels)]
    order_last = order_first[1:]

    def bits_of(order):
        ids = [mine & 1] + [(mine if axis == "batch" else me) >> bit & 1 for axis, bit in order]
        return jnp.stack(ids).astype(jnp.int32)

    seq_bits = jnp.stack([me >> level & 1 for level in range(levels)]).astype(jnp.int32)

    def over_batch(blocks):
        part = blocks.shape[2:]
        flat_blocks = blocks.reshape(-1, blocks.shape[-1])
        mine_part = lax.psum_scatter(flat_blocks, "batch", scatter_dimension=0, tiled=True)
        return mine_part.reshape(part)

    if fast:
        feed_blocks = quarter_products(
            seq_bits,
            [
                ("wide", normed_low, grad_pre),
                ("tall", grad_branch, hidden),
                ("square", tokens(mix_two), grad_second),
            ],
            levels,
        )
        feed_blocks, grad_mix_two, token = sync(feed_blocks, grad_mix_two, token)
        feed_part = over_batch(feed_blocks)

    blocks = devices if gathered else 2 * reach + 1
    if gathered:
        back = ([0, 1, 2], [1, 2, 0]) if levels == 3 else (list(range(levels)),) * 2
        places = []
        for which in range(2):
            spots = []
            for block in range(devices):
                relative = 0
                for at, bit in enumerate(back[which]):
                    relative |= (block >> (levels - 1 - at) & 1) << bit
                spots.append(relative)
            places.append(me ^ jnp.array(spots, jnp.int32))
        places = jnp.stack(places)
        half_blocks = devices // 2
    else:
        middle_first = [reach] + [spot for spot in range(blocks) if spot != reach]
        places = jnp.array([middle_first, middle_first], jnp.int32)
        half_blocks = 1
    grad_q2, dk_kept, dk_sent, dv_kept, dv_sent = pooled_backward(
        places, token, q2, keys, values, probs_two, grad_mix_two, size, half_blocks
    )
    grad_middle, grad_first, grad_mix_one, vec_first = first_backward(
        token, grad_q2, grad_summed, pooled_query, local_output
    )
    back_parts = ()

    def back_step(doc, token):
        return local_backward(
            token, q, kx, vx, grad_mix_one, probs_one[doc], doc, back_parts
        )

    if gathered:
        kept = [part.reshape((2,) * (levels - 1) + part.shape[1:]) for part in (dk_kept, dv_kept)]
        sent = [part.reshape((2,) * (levels - 1) + part.shape[1:]) for part in (dk_sent, dv_sent)]
        for stage in range(levels):
            came = [swap(sent[which], "seq", back[which][stage]) for which in range(2)]
            if stage < docs:
                back_parts = list(back_step(stage, token))
            if stage == docs - 1:
                from_left = shift(back_parts[3], "seq", 1)
                from_right = shift(back_parts[2], "seq", -1)
            if fast and stage == 0:
                came[0], came[1], back_parts[0], token = sync(
                    came[0], came[1], back_parts[0], token
                )
            if fast and stage == 1:
                middle_kept, middle_sent = scatter_products(
                    bits_of(order_first) + 0 * token[0],
                    order_first,
                    [
                        ("square", tokens(middle_low), tokens(grad_q2)),
                        ("square", tokens(mix_one), grad_first),
                        ("square", tokens(inputs), tokens(back_parts[0])),
                    ],
                )
                came[0], came[1], from_left, from_right, middle_sent, token = sync(
                    came[0], came[1], from_left, from_right, middle_sent, token
                )
            if fast and stage == 2:
                middle_came = swap(middle_sent, "batch", 0)
                came[0], came[1], middle_came, token = sync(
                    came[0], came[1], middle_came, token
                )
            if stage < levels - 1:
                for which in range(2):
                    sent[which], kept[which] = fold(kept[which], came[which])
        pooled_grads = [kept[0], came[0], kept[1], came[1]]
    else:
        pooled_grads = []
        for kept, sent in ((dk_kept, dk_sent), (dv_kept, dv_sent)):
            total = kept[0]
            for distance in range(1, reach + 1):
                total = total + shift(sent[reach - distance], "seq", -distance).astype(F32)
                total = total + shift(sent[reach + distance - 1], "seq", distance).astype(F32)
            after = shift(total[:, :1].astype(BF16), "seq", -1).astype(F32)
            total = jnp.concatenate([total[:, :size], jnp.tile(after, (1, 8, 1))], axis=1)
            pooled_grads += [total, jnp.zeros_like(total)]
        for doc in range(docs):
            back_parts = back_step(doc, token)
        from_left = shift(back_parts[3], "seq", 1)
        from_right = shift(back_parts[2], "seq", -1)
    dq, own_grads = back_parts[:2]
    if fast:
        middle_terms = [middle_kept, middle_came]
        middle_far = swap(total_of(middle_terms, 1, slice(None), 1).astype(BF16), "batch", 1)
    grad_k, grad_v, vec_input = key_value_gradients(
        token, pooled_grads, kx, vx, taps_key, taps_value,
        own_grads, from_left, from_right, dq,
    )
    if fast:
        last_kept, last_sent = scatter_products(
            bits_of(order_last),
            order_last,
            [("square", tokens(inputs), grad_k), ("square", tokens(inputs), grad_v)],
            (vec_feed, vec_first, vec_input, vec_wide),
        )
        last_sent, middle_far, token = sync(last_sent, middle_far, token)
        last_came = swap(last_sent, "batch", 0)
        middle_near = swap(total_of(middle_terms, 1, slice(None), 0).astype(BF16), "batch", 1)
    input_grad = input_gradient(
        token, tokens(dq), grad_k, grad_v, grad_middle, local_query, local_key, local_value
    )

    if fast:
        cut_feed = feed_part.shape[-2] // 2
        one = [feed_part[..., :cut_feed, :]]
        two = [feed_part[..., cut_feed:, :]]

        def advance_second(terms, hop):
            came = swap(total_of(terms, slice(None), 1).astype(BF16), *hop)
            return [term[:, 0] for term in terms], came

        one, one_came = advance(one, ("seq", 0))
        two, two_came = advance_second(two, ("seq", 1))
        input_grad, last_came, middle_near, one_came, two_came = sync(
            input_grad, last_came, middle_near, one_came, two_came
        )
        last_terms, last_came = advance([last_kept, last_came], ("seq", 0))
        middle_came = swap(
            total_of([term[0, :, 1] for term in middle_terms] + [middle_far], Ellipsis).astype(BF16),
            "seq",
            1,
        )
        middle_terms = [term[0, :, 0] for term in middle_terms] + [middle_near]
        one, one_came = advance(one + [one_came], ("seq", 1))
        two, two_came = advance(two + [two_came], ("seq", 0))
        last_came, middle_came, one_came, two_came = sync(
            last_came, middle_came, one_came, two_came
        )

        last_terms, last_came = advance(last_terms + [last_came], ("seq", 1))
        one, two = one + [one_came], two + [two_came]
        feed_came = swap(
            jnp.concatenate([total_of(one, 1), total_of(two, 1)]).astype(BF16), "seq", 2
        )
        middle_terms, middle_came = advance(middle_terms + [middle_came], ("seq", 0))
        last_came, middle_came, feed_came = sync(last_came, middle_came, feed_came)

        last_terms, last_came = advance(last_terms + [last_came], ("seq", 2))
        middle_terms, middle_came = advance(middle_terms + [middle_came], ("seq", 2))
        feed_low = (
            jnp.concatenate([total_of(one, 0), total_of(two, 0)]) + feed_came.astype(F32)
        ).astype(BF16)
        feed_other = swap(feed_low, "batch", 1)
        last_came, middle_came, feed_other = sync(last_came, middle_came, feed_other)
        cut_at = middle_came.shape[0]
        low = jnp.concatenate(
            [
                total_of(middle_terms + [middle_came], Ellipsis),
                total_of(last_terms + [last_came], Ellipsis),
            ]
        ).astype(BF16)
        other = swap(low, "batch", 1)
        feed_across = swap(jnp.stack([feed_low, feed_other]), "batch", 0)
        low, other, feed_across = sync(low, other, feed_across)
        across = swap(jnp.stack([low, other]), "batch", 0)
        spots = jnp.stack([mine & 1, mine >> 1]).astype(jnp.int32)
        grad_expand, grad_reduce, grad_po = collect_feed(spots, feed_low, feed_other, feed_across)
        grad_pq, grad_lo, grad_lq, grad_lk, grad_lv, lines = collect_last(
            spots, low, other, across, cut_at
        )
        vec_low, vec_high = lines[0, :, :96], lines[1, :, :96]
        (fg, fs, rb, ng, ns, pob) = [vec_low[index] for index in range(6)]
        pqb, lob = lines[0, 0, LANES : LANES + 96], lines[0, 1, LANES : LANES + 96]
        grad_eb = vec_low[8:12].reshape(-1)
    else:

        def plain(left_array, right_array):
            product = tn(left_array, right_array)
            part = lax.psum_scatter(product, "seq", scatter_dimension=0, tiled=True)
            return lax.psum(part.astype(BF16), "batch").astype(F32)

        grad_expand = plain(normed_low, grad_pre)
        grad_reduce = plain(hidden, grad_branch)
        grad_po = plain(tokens(mix_two), grad_second)
        grad_pq = plain(tokens(middle_low), tokens(grad_q2))
        grad_lo = plain(tokens(mix_one), grad_first)
        grad_lq = plain(tokens(inputs), tokens(dq))
        grad_lk = plain(tokens(inputs), grad_k)
        grad_lv = plain(tokens(inputs), grad_v)
        vectors = jnp.concatenate(
            [vec_feed, vec_first, vec_input, vec_wide.reshape(-1, width)], axis=0
        )
        vectors = lax.psum(vectors, ("seq", "batch"))
        share = width // devices
        part = lax.dynamic_slice_in_dim(vectors, me * share, share, axis=1)
        wide = vectors[32:].reshape(-1)
        wide_share = wide.shape[0] // devices
        grad_eb = lax.dynamic_slice_in_dim(wide, me * wide_share, wide_share, axis=0)
        (fg, fs, rb, ng, ns, pob) = [part[index] for index in range(6)]
        pqb, lob = part[8], part[9]
        vec_high = part[16:32]
    grad_ck = vec_high[:KER].T
    grad_cv = vec_high[KER : 2 * KER].T
    cvb, lqb, lvb = vec_high[10], vec_high[11], vec_high[12]
    return (
        outputs, input_grad,
        grad_lq, lqb, grad_lk, grad_lv, lvb, grad_lo, lob, grad_pq, pqb, grad_po, pob,
        grad_ck, grad_cv, cvb, ng, ns, grad_expand, grad_eb, grad_reduce, rb, fg, fs,
    )


def solution(mesh):
    vector = P("seq")
    matrix = P("seq", None)
    return jax.shard_map(
        device_step,
        mesh=mesh,
        in_specs=(P("batch", "seq", None), P("batch"), P("batch", "seq", None)) + (P(),) * 22,
        out_specs=(
            P("batch", "seq", None), P("batch", "seq", None),
            matrix, vector, matrix, matrix, vector, matrix, vector, matrix, vector, matrix, vector,
            matrix, matrix, vector, vector, vector, matrix, vector, matrix, vector, vector, vector,
        ),
        check_vma=False,
    )
```

```python
import functools
import math

import jax
import jax.numpy as jnp
from jax import lax
from jax.experimental import pallas as pl
from jax.experimental.pallas import tpu as pltpu
from jax.sharding import PartitionSpec as P

HEADS = 12
HD = 64
WIN = 128
PWIN = 512
KER = 5
STRIDE = 4
HALF = WIN // 2
REACH = PWIN // 2
NEGATIVE = -1e30
SCALE = 1.0 / math.sqrt(HD)
EPSILON = 1e-05
LANES = 128
TILE = 128
ROWS = 128
CHUNK = 768
PAIRS = 2
F32 = jnp.float32
BF16 = jnp.bfloat16


def nn(left, right):
    return jnp.dot(left, right, preferred_element_type=F32)


def nt(left, right):
    return lax.dot_general(left, right, (((1,), (1,)), ((), ())), preferred_element_type=F32)


def tn(left, right):
    return lax.dot_general(left, right, (((0,), (0,)), ((), ())), preferred_element_type=F32)


def column_sum(block):
    return jnp.sum(block.astype(F32), axis=0, keepdims=True)


def call(body, grid, scalars, inputs, outputs, scratch=(), spare=8):
    used = spare * 2**20
    arrays, in_specs, out_specs, shapes = [], [], [], []

    def spec(shape, dtype, block, index):
        nonlocal used
        if block is None:
            return pl.BlockSpec(memory_space=pltpu.VMEM)
        if block == "raw":
            return pl.BlockSpec(memory_space=pl.ANY)
        used += 2 * math.prod(block) * jnp.dtype(dtype).itemsize
        return pl.BlockSpec(block, index)

    for array, block, index in inputs:
        in_specs.append(spec(array.shape, array.dtype, block, index))
        if block is not None:
            array = pltpu.with_memory_space_constraint(array, pltpu.HBM)
        arrays.append(array)
    for shape, dtype, block, index in outputs:
        out_specs.append(spec(shape, dtype, block, index))
        plain = block is None
        shapes.append((jax.ShapeDtypeStruct if plain else pltpu.HBM)(shape, dtype))
    for item in scratch:
        if hasattr(item, "shape") and item.memory_space == pltpu.VMEM:
            used += math.prod(item.shape) * jnp.dtype(item.dtype).itemsize
    return pl.pallas_call(
        body,
        grid_spec=pltpu.PrefetchScalarGridSpec(
            num_scalar_prefetch=len(scalars),
            grid=grid,
            in_specs=in_specs,
            out_specs=out_specs,
            scratch_shapes=list(scratch),
        ),
        out_shape=shapes,
        compiler_params=pltpu.CompilerParams(
            dimension_semantics=("arbitrary",) * len(grid), vmem_limit_bytes=used
        ),
        cost_estimate=pl.CostEstimate(flops=1000, bytes_accessed=1000, transcendentals=0),
    )(*scalars, *arrays)


def raw(array):
    return (array, "raw", None)


def out_raw(shape, dtype):
    return (shape, dtype, "raw", None)


def whole(array):
    return (array, None, None)


def out_whole(shape, dtype):
    return (shape, dtype, None, None)


def sync(*values):
    return lax.optimization_barrier(values)


def stack_heads(block):
    lane = lax.broadcasted_iota(jnp.int32, block.shape, 1)
    zero = jnp.zeros_like(block)
    return jnp.concatenate(
        [jnp.where(lane < HD, block, zero), jnp.where(lane < HD, zero, block)], axis=0
    )


def unstack(block):
    half = block.shape[1] // 2
    joined = jnp.concatenate([block[:HD, :half], block[HD:, half:]], axis=0)
    return joined.T


def positions(shape, dim):
    return lax.broadcasted_iota(jnp.int32, shape, dim)


def project_body(place, x_far, wq_far, bq, wk_far, wv_far, bv, q, k, v, wk, wv, x, wq, sems):
    docs, rows, width = x.shape
    fetches = [
        pltpu.make_async_copy(far, near, sems.at[index])
        for index, (far, near) in enumerate(
            ((x_far, x), (wq_far, wq), (wk_far, wk), (wv_far, wv))
        )
    ]
    for fetch in fetches:
        fetch.start()
    fetches[0].wait()
    flat = x[...].reshape(docs * rows, width)
    fetches[1].wait()
    q[...] = (nn(flat, wq[...]) + bq[...]).astype(BF16).reshape(q.shape)
    fetches[2].wait()
    k[...] = nn(flat, wk[...]).astype(BF16).reshape(k.shape)
    fetches[3].wait()
    v[...] = (nn(flat, wv[...]) + bv[...]).astype(BF16).reshape(v.shape)


def project(place, x, wq, bq, wk, wv, bv):
    return call(
        project_body,
        (1,),
        (place,),
        [raw(x), raw(wq), whole(bq), raw(wk), raw(wv), whole(bv)],
        [out_whole(x.shape, BF16)] * 3 + [out_whole(wk.shape, BF16)] * 2,
        [
            pltpu.VMEM(x.shape, BF16),
            pltpu.VMEM(wq.shape, BF16),
            pltpu.SemaphoreType.DMA((4,)),
        ],
    )


def pool_body(place, left, right, k, v, wk, wv, bv, ck, cv, bcv, kx, vx, pooled, rows):
    offset = place[0]
    docs, own_rows, width = k.shape
    rims = jnp.concatenate(
        [part[doc] for doc in range(docs) for part in (left, right)], axis=0
    )
    size = own_rows + WIN
    count = pooled.shape[2]
    spot = offset - HALF + positions((size, 1), 0)
    for which, (weight, bias, taps, own, out) in enumerate(
        ((wk, None, ck, k, kx), (wv, bv, cv, v, vx))
    ):
        value = nn(rims, weight[...])
        if bias is not None:
            value = value + bias[...]
        value = value.astype(BF16)
        for doc in range(docs):
            at = doc * WIN
            out[doc, :HALF] = value[at : at + HALF]
            out[doc, HALF : HALF + own_rows] = own[doc]
            out[doc, HALF + own_rows :] = value[at + HALF : at + WIN]
            valid = (spot >= 0) & (spot < place[1 + doc])
            for group in range(width // LANES):
                lanes = slice(group * LANES, (group + 1) * LANES)
                rows[group] = jnp.where(valid, out[doc, :, lanes].astype(F32), 0.0)
                total = jnp.zeros((count, LANES), F32)
                for tap in range(KER):
                    start = HALF - KER // 2 + tap
                    read = rows[group, pl.ds(start, count, stride=STRIDE), :]
                    total = total + read * taps[tap : tap + 1, lanes]
                if which == 1:
                    total = total + bcv[:, lanes]
                pooled[which, doc, :, lanes] = total.astype(BF16)


def pool(place, left, right, k, v, wk, wv, bv, ck, cv, bcv):
    docs, rows, width = k.shape
    extended = rows + WIN
    return call(
        pool_body,
        (1,),
        (place,),
        [whole(a) for a in (left, right, k, v, wk, wv, bv, ck, cv, bcv)],
        [
            out_whole((docs, extended, width), BF16),
            out_whole((docs, extended, width), BF16),
            out_whole((2, docs, rows // STRIDE, width), BF16),
        ],
        [pltpu.VMEM((width // LANES, extended, LANES), F32)],
    )


def local_bias(tile, offset, length):
    shape = (TILE + WIN, TILE)
    key = positions(shape, 0)
    query = positions(shape, 1)
    spot = offset + tile * TILE - HALF + key
    allowed = (
        (key >= query) & (key < query + WIN) & (spot >= 0) & (spot < length)
    ) | (key == query + HALF)
    return jnp.where(allowed, 0.0, NEGATIVE)


def softmax_columns(scores):
    top = jnp.max(scores, axis=0, keepdims=True)
    grown = jnp.exp(scores - top)
    return grown * (1.0 / jnp.sum(grown, axis=0, keepdims=True))


def local_forward_body(place, q, kx, vx, mix, probs, *, doc):
    offset, length = place[0], place[1 + doc]
    span = TILE + WIN
    for tile in range(q.shape[1] // TILE):
        half_bias = local_bias(tile, offset, length)
        bias = jnp.concatenate([half_bias, half_bias], axis=1)
        first = tile * TILE
        for pair in range(q.shape[2] // LANES):
            lanes = slice(pair * LANES, (pair + 1) * LANES)
            queries = stack_heads(q[doc, first : first + TILE, lanes]) * SCALE
            scores = nt(kx[doc, first : first + span, lanes], queries) + bias
            chance = softmax_columns(scores)
            probs[pair, tile] = chance
            turned = vx[doc, first : first + span, lanes].T
            mixed = nn(turned, chance.astype(BF16))
            mix[first : first + TILE, lanes] = unstack(mixed).astype(BF16)


def local_forward(place, q, kx, vx, doc):
    _, rows, width = q.shape
    pairs, tiles, span = width // LANES, rows // TILE, TILE + WIN
    return call(
        functools.partial(local_forward_body, doc=doc),
        (1,),
        (place,),
        [whole(a) for a in (q, kx, vx)],
        [
            out_whole((rows, width), BF16),
            out_whole((pairs, tiles, span, 2 * TILE), F32),
        ],
    )


def middle_body(place, x, wo, bo, wpq, bpq, *refs):
    docs, rows = x.shape[0], x.shape[1]
    mixes, (mix, middle, middle_low, q2) = refs[:docs], refs[docs:]
    for doc in range(docs):
        mix[doc] = mixes[doc][...]
    flat = docs * rows
    branch = nn(mix[...].reshape(flat, x.shape[2]), wo[...]) + bo[...]
    total = x[...].reshape(flat, x.shape[2]).astype(F32) + branch
    middle[...] = total.reshape(middle.shape)
    low = total.astype(BF16)
    middle_low[...] = low.reshape(middle_low.shape)
    q2[...] = (nn(low, wpq[...]) + bpq[...]).astype(BF16).reshape(q2.shape)


def middle_forward(place, x, wo, bo, wpq, bpq, mixes):
    docs, rows, width = x.shape
    return call(
        middle_body,
        (1,),
        (place,),
        [whole(a) for a in (x, wo, bo, wpq, bpq, *mixes)],
        [
            out_whole((docs, rows, width), BF16),
            out_whole((docs, rows, width), F32),
            out_whole((docs, rows, width), BF16),
            out_whole((docs, rows, width), BF16),
        ],
    )


def attention_back(keys, values, queries, grads, chance):
    stacked_grads = stack_heads(grads)
    stacked_queries = stack_heads(queries)
    grad_chance = nt(values, stacked_grads * SCALE)
    dots = jnp.sum(chance * grad_chance, axis=0, keepdims=True)
    grad_raw = (chance * (grad_chance - dots)).astype(BF16)
    grad_keys = nn(grad_raw, stacked_queries)
    grad_values = nn(chance.astype(BF16), stacked_grads)
    grad_queries = unstack(nn(keys.T, grad_raw))
    return grad_queries, grad_keys, grad_values


def first_back_body(place, gq2, gsum, wpq, wo, gmid, gfirst, gmix, vec):
    docs, rows, width = gsum.shape
    flat = docs * rows
    grads = gq2[...].reshape(flat, width)
    total = gsum[...].reshape(flat, width) + nt(grads, wpq[...])
    gmid[...] = total.reshape(gmid.shape)
    low = total.astype(BF16)
    gfirst[...] = low
    gmix[...] = nt(low, wo[...]).astype(BF16).reshape(gmix.shape)
    vec[...] = jnp.zeros_like(vec)
    vec[0:1] = column_sum(grads)
    vec[1:2] = column_sum(low)


def first_backward(place, gq2, gsum, wpq, wo):
    docs, rows, width = gsum.shape
    return call(
        first_back_body,
        (1,),
        (place,),
        [whole(a) for a in (gq2, gsum, wpq, wo)],
        [
            out_whole((docs, rows, width), F32),
            out_whole((docs * rows, width), BF16),
            out_whole((docs, rows, width), BF16),
            out_whole((8, width), F32),
        ],
    )


def local_backward_body(place, q, kx, vx, gmix, probs, *refs, doc):
    earlier = refs[: len(refs) - 6]
    dq, own, low_left, low_right, dk, dv = refs[len(refs) - 6 :]
    rows = q.shape[1]
    for old, new in zip(earlier, (dq, own, low_left, low_right)):
        new[:doc] = old[...]
    span = TILE + WIN
    dk[...] = jnp.zeros_like(dk)
    dv[...] = jnp.zeros_like(dv)
    for tile in range(rows // TILE):
        first = tile * TILE
        for pair in range(q.shape[2] // LANES):
            lanes = slice(pair * LANES, (pair + 1) * LANES)
            grad_q, grad_k, grad_v = attention_back(
                kx[doc, first : first + span, lanes],
                vx[doc, first : first + span, lanes],
                q[doc, first : first + TILE, lanes],
                gmix[doc, first : first + TILE, lanes],
                probs[pair, tile],
            )
            dq[doc, first : first + TILE, lanes] = grad_q.astype(BF16)
            dk[first : first + span, lanes] += grad_k
            dv[first : first + span, lanes] += grad_v
    for which, part in enumerate((dk, dv)):
        own[doc, which] = part[HALF : HALF + rows]
        low_left[doc, which] = part[:HALF].astype(BF16)
        low_right[doc, which] = part[HALF + rows :].astype(BF16)


def local_backward(place, q, kx, vx, gmix, probs, doc, earlier=()):
    _, rows, width = q.shape
    span = TILE + WIN
    return call(
        functools.partial(local_backward_body, doc=doc),
        (1,),
        (place,),
        [whole(a) for a in (q, kx, vx, gmix, probs, *earlier)],
        [
            out_whole((doc + 1, rows, width), BF16),
            out_whole((doc + 1, 2, rows, width), F32),
            out_whole((doc + 1, 2, HALF, width), BF16),
            out_whole((doc + 1, 2, HALF, width), BF16),
        ],
        [
            pltpu.VMEM((rows + WIN, width), F32),
            pltpu.VMEM((rows + WIN, width), F32),
        ],
    )


def pooled_forward_body(place, slots, *refs, pieces):
    key_pieces = refs[:pieces]
    value_pieces = refs[pieces : 2 * pieces]
    (
        q2, middle, wpo, bpo, we, wr,
        keys_out, values_out, probs, mix, summed, we_near, wr_near,
        keys, values, bias, sems,
    ) = refs[2 * pieces :]
    doc, pair = pl.program_id(0), pl.program_id(1)
    fetches = [
        pltpu.make_async_copy(we, we_near, sems.at[0]),
        pltpu.make_async_copy(wr, wr_near, sems.at[1]),
    ]
    last = (pair == pl.num_programs(1) - 1) & (doc == pl.num_programs(0) - 1)
    leaves = [
        pltpu.make_async_copy(keys.at[each], keys_out.at[each], sems.at[2 + each])
        for each in range(keys.shape[0])
    ] + [
        pltpu.make_async_copy(
            values.at[each], values_out.at[each], sems.at[2 + keys.shape[0] + each]
        )
        for each in range(keys.shape[0])
    ]

    @pl.when((pair == 0) & (doc == 0))
    def _():
        for fetch in fetches:
            fetch.start()

    offset, length, base = place[0], place[1 + doc], place[1 + pl.num_programs(0)]
    count = keys.shape[1]

    @pl.when(pair == 0)
    def _():
        for where, group, out in ((0, key_pieces, keys), (1, value_pieces, values)):
            at = 0
            for piece in group:
                size = piece.shape[2]
                for block in range(piece.shape[0]):
                    spot = pl.multiple_of(slots[where, at] * size, size)
                    out[doc, pl.ds(spot, size), :] = piece[block, doc]
                    at += 1
        if True:
            shape = (count, q2.shape[1])
            spot = base + positions(shape, 0)
            centre = offset // STRIDE + positions(shape, 1) // STRIDE
            allowed = (
                (spot >= centre - REACH)
                & (spot < centre + REACH)
                & (spot >= 0)
                & (spot * STRIDE < length)
            ) | (spot == centre)
            bias[...] = jnp.where(allowed, 0.0, NEGATIVE)
        for each in range(keys.shape[0]):

            @pl.when(doc == each)
            def _():
                leaves[each].start()
                leaves[keys.shape[0] + each].start()

    for each in range(PAIRS):
        lanes = pl.ds(pl.multiple_of((pair * PAIRS + each) * LANES, LANES), LANES)
        queries = stack_heads(q2[doc, :, lanes]) * SCALE
        half_bias = bias[...]
        scores = nt(keys[doc, :, lanes], queries) + jnp.concatenate([half_bias, half_bias], axis=1)
        chance = softmax_columns(scores)
        probs[0, each] = chance
        mixed = nn(values[doc, :, lanes].T, chance.astype(BF16))
        mix[doc, :, lanes] = unstack(mixed).astype(BF16)

    @pl.when(last)
    def _():
        for copy in fetches + leaves:
            copy.wait()
        flat = (mix.shape[0] * mix.shape[1], mix.shape[2])
        second = nn(mix[...].reshape(flat), wpo[...]) + bpo[...]
        summed[...] = middle[...] + second.reshape(summed.shape)


def pooled_forward(place, slots, key_pieces, value_pieces, q2, middle, wpo, bpo, we, wr):
    docs, rows, width = q2.shape
    pairs, tiles = width // LANES, rows // TILE
    size = key_pieces[0].shape[2]
    count = size * slots.shape[1]

    return call(
        functools.partial(pooled_forward_body, pieces=len(key_pieces)),
        (docs, pairs // PAIRS),
        (place, slots),
        [whole(a) for a in (*key_pieces, *value_pieces, q2, middle, wpo, bpo)]
        + [raw(we), raw(wr)],
        [
            out_raw((docs, count, width), BF16),
            out_raw((docs, count, width), BF16),
            (
                (docs, pairs, count, 2 * rows),
                F32,
                (1, PAIRS, count, 2 * rows),
                lambda doc, pair, *_: (doc, pair, 0, 0),
            ),
            out_whole((docs, rows, width), BF16),
            out_whole((docs, rows, width), F32),
            out_whole(we.shape, BF16),
            out_whole(wr.shape, BF16),
        ],
        [
            pltpu.VMEM((docs, count, width), BF16),
            pltpu.VMEM((docs, count, width), BF16),
            pltpu.VMEM((count, rows), F32),
            pltpu.SemaphoreType.DMA((2 + 2 * docs,)),
        ],
    )


def pooled_backward_body(
    places, token, q2, keys, values, probs, grads, dq, dk_kept, dk_sent, dv_kept, dv_sent, sums
):
    doc, step = pl.program_id(0), pl.program_id(1)
    size = dk_kept.shape[2]
    half = dk_kept.shape[0]
    rows = keys.shape[1]
    for each in range(PAIRS):
        inner = slice(each * LANES, (each + 1) * LANES)
        lanes = pl.ds(pl.multiple_of((step * PAIRS + each) * LANES, LANES), LANES)
        grad_q, *total = attention_back(
            keys[0, :, inner], values[0, :, inner], q2[0, :, inner], grads[0, :, inner],
            probs[0, each],
        )
        dq[doc, :, lanes] = grad_q.astype(BF16)
        for which, (kept, sent) in enumerate(((dk_kept, dk_sent), (dv_kept, dv_sent))):
            sums[each, which, :rows] = total[which]
            sums[each, which, rows:] = jnp.zeros((8, LANES), F32)
            for block in range(half + sent.shape[0]):
                start = pl.multiple_of(places[which, block] * (size - 8), size - 8)
                part = sums[each, which, pl.ds(start, size), :]
                if block < half:
                    kept[block, doc, :, lanes] = part
                else:
                    sent[block - half, doc, :, lanes] = part.astype(BF16)


def pooled_backward(places, token, q2, keys, values, probs, grads, size, kept):
    docs, rows, width = q2.shape
    count = keys.shape[1]
    blocks = count // size
    tiles = rows // TILE

    def lanes_of(array):
        return (array, (1, array.shape[1], PAIRS * LANES), lambda doc, pair, *_: (doc, 0, pair))

    return call(
        pooled_backward_body,
        (docs, width // LANES // PAIRS),
        (places, token),
        [
            lanes_of(q2),
            lanes_of(keys),
            lanes_of(values),
            (
                probs,
                (1, PAIRS, count, 2 * rows),
                lambda doc, pair, *_: (doc, pair, 0, 0),
            ),
            lanes_of(grads),
        ],
        [
            out_whole((docs, rows, width), BF16),
            out_whole((kept, docs, size + 8, width), F32),
            out_whole((blocks - kept, docs, size + 8, width), BF16),
            out_whole((kept, docs, size + 8, width), F32),
            out_whole((blocks - kept, docs, size + 8, width), BF16),
        ],
        [pltpu.VMEM((PAIRS, 2, count + 8, LANES), F32)],
    )


def feed_body(
    place, summed, cotangent, we, be, wr, br, ng, ns, fg, fs, wpo,
    outputs_far, normed_low, hidden, grad_branch, grad_pre, grad_summed_far, grad_second,
    grad_mix_far, vec, vec_wide,
    normed, slope, work, unit, outputs, grad_mix, sems,
):
    docs, rows = cotangent.shape[0], cotangent.shape[1]
    width = summed.shape[2]
    wide = we.shape[1]
    steps = rows // ROWS
    blocks = [
        (doc, step * ROWS, doc * rows + step * ROWS)
        for doc in range(docs)
        for step in range(steps)
    ]
    leaving = []

    def leave(source, target, doc, start, row):
        copy = pltpu.make_async_copy(
            source.at[pl.ds(row, ROWS)],
            target.at[doc, pl.ds(start, ROWS)],
            sems.at[len(leaving)],
        )
        copy.start()
        leaving.append(copy)


    def normal(value):
        centred = value - jnp.mean(value, axis=-1, keepdims=True)
        scale = lax.rsqrt(jnp.mean(centred * centred, axis=-1, keepdims=True) + EPSILON)
        return centred * scale, scale

    scales = []
    for doc, start, row in blocks:
        norm, scale = normal(summed[doc, start : start + ROWS])
        scales.append(scale)
        unit[row : row + ROWS] = norm
        full = norm * ng[...] + ns[...]
        normed[row : row + ROWS] = full
        normed_low[row : row + ROWS] = full.astype(BF16)

    def expand(index):
        part = slice(index * CHUNK, (index + 1) * CHUNK)
        pre = nn(normed_low[...], we[:, part]) + be[:, part]
        cdf = 0.5 * (1.0 + lax.erf(pre * math.sqrt(0.5)))
        hidden[:, part] = (pre * cdf).astype(BF16)
        slope[:, part] = cdf + pre * (jnp.exp(pre * pre * -0.5) * (1.0 / math.sqrt(2.0 * math.pi)))
    for index in range(wide // CHUNK):
        expand(index)

    for start in range(0, width, CHUNK):
        part = slice(start, start + CHUNK)
        work[:, part] = normed[:, part] + (nn(hidden[...], wr[:, part]) + br[:, part])

    sums = [jnp.zeros((1, width), F32) for _ in range(6)]
    for doc, start, row in blocks:
        norm, scale = normal(work[row : row + ROWS])
        spot = place[0] + start + positions((ROWS, 1), 0)
        valid = (spot < place[1 + doc]).astype(F32)
        outputs[row : row + ROWS] = (valid * (norm * fg[...] + fs[...])).astype(BF16)
        leave(outputs, outputs_far, doc, start, row)
        error = valid * cotangent[doc, start : start + ROWS].astype(F32)
        sums[0] += column_sum(error * norm)
        sums[1] += column_sum(error)
        scaled = error * fg[...]
        rest = (
            scaled
            - jnp.mean(scaled, axis=-1, keepdims=True)
            - norm * jnp.mean(scaled * norm, axis=-1, keepdims=True)
        ) * scale
        work[row : row + ROWS] = rest
        low = rest.astype(BF16)
        grad_branch[row : row + ROWS] = low
        sums[2] += column_sum(low)

    def reduce(index):
        part = slice(index * CHUNK, (index + 1) * CHUNK)
        low = (nt(grad_branch[...], wr[part, :]) * slope[:, part]).astype(BF16)
        grad_pre[:, part] = low
        vec_wide[:, part] = column_sum(low)

    for index in range(wide // CHUNK):
        reduce(index)

    for start in range(0, width, CHUNK):
        part = slice(start, start + CHUNK)
        work[:, part] += nt(grad_pre[...], we[part, :])

    for (doc, start, row), scale in zip(blocks, scales):
        error = work[row : row + ROWS]
        norm = unit[row : row + ROWS]
        sums[3] += column_sum(error * norm)
        sums[4] += column_sum(error)
        scaled = error * ng[...]
        grad = (
            scaled
            - jnp.mean(scaled, axis=-1, keepdims=True)
            - norm * jnp.mean(scaled * norm, axis=-1, keepdims=True)
        ) * scale
        unit[row : row + ROWS] = grad
        leave(unit, grad_summed_far, doc, start, row)
        low = grad.astype(BF16)
        grad_second[row : row + ROWS] = low
        sums[5] += column_sum(low)
        grad_mix[row : row + ROWS] = nt(low, wpo[...]).astype(BF16)
        leave(grad_mix, grad_mix_far, doc, start, row)
    for index, value in enumerate(sums):
        vec[index : index + 1] = value
    vec[6:8] = jnp.zeros((2, width), F32)
    for copy in leaving:
        copy.wait()


def feed(place, summed, cotangent, we, be, wr, br, ng, ns, fg, fs, wpo):
    docs, rows, width = summed.shape
    wide = we.shape[1]
    tokens = docs * rows
    return call(
        feed_body,
        (1,),
        (place,),
        [whole(a) for a in (summed, cotangent, we, be, wr, br, ng, ns, fg, fs, wpo)],
        [
            out_raw((docs, rows, width), BF16),
            out_whole((tokens, width), BF16),
            out_whole((tokens, wide), BF16),
            out_whole((tokens, width), BF16),
            out_whole((tokens, wide), BF16),
            out_raw((docs, rows, width), F32),
            out_whole((tokens, width), BF16),
            out_raw((docs, rows, width), BF16),
            out_whole((8, width), F32),
            out_whole((1, wide), F32),
        ],
        [
            pltpu.VMEM((tokens, width), F32),
            pltpu.VMEM((tokens, wide), F32),
            pltpu.VMEM((tokens, width), F32),
            pltpu.VMEM((tokens, width), F32),
            pltpu.VMEM((tokens, width), BF16),
            pltpu.VMEM((tokens, width), BF16),
            pltpu.SemaphoreType.DMA((3 * tokens // ROWS,)),
        ],
        spare=12,
    )


def key_value_body(place, *refs, docs):
    gk_kept, gk_came, gv_kept, gv_came, kx, vx, ck, cv = refs[:8]
    own, from_left, from_right, dq = refs[8:12]
    gk, gv, vec, rows_in, pooled, total = refs[12:]
    offset = place[0]
    rows, width = gk.shape[0] // docs, gk.shape[1]
    count = rows // STRIDE
    vec[...] = jnp.zeros_like(vec)
    for doc in range(docs):
        length = place[1 + doc]
        spot = offset - HALF + positions((rows + WIN, 1), 0)
        valid = (spot >= 0) & (spot < length)
        first = doc * rows
        for which, (kept, came, ext, taps, out, row) in enumerate(
            (
                (gk_kept, gk_came, kx, ck, gk, 0),
                (gv_kept, gv_came, vx, cv, gv, KER),
            )
        ):
            pooled[...] = kept[doc].astype(F32) + came[doc].astype(F32)
            masked = jnp.where(valid, ext[doc].astype(F32), 0.0)
            for group in range(width // LANES):
                lanes = slice(group * LANES, (group + 1) * LANES)
                grown = pooled[:count, lanes]
                shifted = pooled[1 : count + 1, lanes]
                rows_in[group] = masked[:, lanes]
                for tap in range(KER):
                    start = HALF - KER // 2 + tap
                    read = rows_in[group, pl.ds(start, count, stride=STRIDE), :]
                    vec[row + tap : row + tap + 1, lanes] += column_sum(grown * read)
                if which == 1:
                    vec[2 * KER : 2 * KER + 1, lanes] += column_sum(grown)
                total[group] = own[doc, which, :, lanes]
                total[group, :HALF] += from_left[doc, which, :, lanes].astype(F32)
                total[group, rows - HALF :] += from_right[doc, which, :, lanes].astype(F32)
                for phase, terms in enumerate(
                    (
                        ((2, grown),),
                        ((3, grown),),
                        ((4, grown), (0, shifted)),
                        ((1, shifted),),
                    )
                ):
                    part = pl.ds(phase, count, stride=STRIDE)
                    added = None
                    for tap, values in terms:
                        term = values * taps[tap : tap + 1, lanes]
                        added = term if added is None else added + term
                    inside = offset + phase + STRIDE * positions((count, 1), 0) < length
                    total[group, part, :] = total[group, part, :] + jnp.where(inside, added, 0.0)
                out[first : first + rows, lanes] = total[group].astype(BF16)
        vec[11:12] += column_sum(dq[doc])
    vec[12:13] += column_sum(gv[...])


def key_value_gradients(place, pooled_grads, kx, vx, ck, cv, own, left, right, dq):
    docs, rows, width = dq.shape
    return call(
        functools.partial(key_value_body, docs=docs),
        (1,),
        (place,),
        [
            whole(a)
            for a in (*pooled_grads, kx, vx, ck, cv, own, left, right, dq)
        ],
        [out_whole((docs * rows, width), BF16)] * 2 + [out_whole((16, width), F32)],
        [
            pltpu.VMEM((width // LANES, rows + WIN, LANES), F32),
            pltpu.VMEM((rows // STRIDE + 8, width), F32),
            pltpu.VMEM((width // LANES, rows, LANES), F32),
        ],
    )


def input_body(place, dq, gk, gv, gmid, wq, wk, wv, dx):
    total = nt(dq[...], wq[...]) + nt(gk[...], wk[...]) + nt(gv[...], wv[...])
    dx[...] = (gmid[...] + total.reshape(gmid.shape)).astype(BF16)


def input_gradient(place, dq, gk, gv, gmid, wq, wk, wv):
    docs, rows, width = gmid.shape
    (dx,) = call(
        input_body,
        (1,),
        (place,),
        [whole(a) for a in (dq, gk, gv, gmid, wq, wk, wv)],
        [out_whole((docs, rows, width), BF16)],
    )
    return dx


def scatter_body(bits, *refs, kinds, order, vectors, quartered):
    count = len(kinds)
    operands = [refs[2 * index : 2 * index + 2] for index in range(count)]
    extra = refs[2 * count : 2 * count + vectors]
    rest = refs[2 * count + vectors :]
    if quartered:
        results, (ordered, rounded, *small) = (rest[0], rest[0]), rest[1:]
    else:
        results, (ordered, rounded, *small) = rest[:2], rest[2:]
    core = bits[0]
    sides = 2 if ("batch", 1) in order else 1
    owners = 8

    def start_of(which, size):
        if quartered:
            return which * size
        return pl.multiple_of((which ^ core) * size, LANES)

    def place_tile(which, side, owner, target, size, value):
        index = []
        for at, (axis, bit) in enumerate(order):
            if axis == "batch":
                index += [side, which] if quartered else [side ^ bits[1 + at]]
            else:
                index.append(((owner >> bit) & 1) ^ bits[1 + at])
        results[which][(*index, slice(target, target + size), slice(None))] = value

    base = 0
    for (left, right), kind in zip(operands, kinds):
        tall = left.shape[1]
        turned = left[...].T
        if kind == "wide":
            half = right.shape[1] // 2
            size = tall // owners // sides
            for which in range(2):
                start = start_of(which, half)
                for part in range(half // 768):
                    rounded[...] = nn(turned, right[:, pl.ds(start + part * 768, 768)]).astype(BF16)
                    for column in range(2):
                        target = base + (2 * part + column) * size
                        for owner in range(owners):
                            for side in range(sides):
                                row = (owner * sides + side) * size
                                value = rounded[row : row + size, column * 384 : column * 384 + 384]
                                place_tile(which, side, owner, target, size, value)
            base += half // 384 * size
        elif kind == "tall":
            ordered[...] = turned
            size = tall // 2 // sides
            for part in range(right.shape[1] // 768):
                product = nn(ordered[...], right[:, part * 768 : part * 768 + 768])
                rounded[...] = product.astype(BF16)
                for column in range(2):
                    owner = 2 * part + column
                    for side in range(sides):
                        for which in range(2):
                            row = start_of(which, 384) + side * size
                            value = rounded[pl.ds(row, size), column * 384 : column * 384 + 384]
                            place_tile(which, side, owner, base, size, value)
            base += size
        else:
            size = tall // owners // sides
            if quartered:
                columns = right[...]
            else:
                columns = jnp.concatenate(
                    [right[:, pl.ds(start_of(which, 384), 384)] for which in range(2)], axis=1
                )
            rounded[...] = nn(turned, columns).astype(BF16)
            for which in range(2):
                for owner in range(owners):
                    for side in range(sides):
                        row = (owner * sides + side) * size
                        value = rounded[row : row + size, which * 384 : which * 384 + 384]
                        place_tile(which, side, owner, base, size, value)
            base += size
    if vectors:
        (block,) = small
        vec_feed, vec_first, vec_input, vec_wide = extra
        for owner in range(owners):
            lanes = slice(owner * 96, owner * 96 + 96)
            block[0, owner] = jnp.zeros(block.shape[2:], F32)
            block[1, owner] = jnp.zeros(block.shape[2:], F32)
            block[0, owner, 0:8, 0:96] = vec_feed[:, lanes]
            block[0, owner, 0:8, LANES : LANES + 96] = vec_first[:, lanes]
            block[1, owner, 0:16, 0:96] = vec_input[:, lanes]
            for part in range(4):
                at = owner * 384 + part * 96
                block[0, owner, 8 + part : 9 + part, 0:96] = vec_wide[:, at : at + 96]
        for owner in range(owners):
            for which in range(2):
                place_tile(which, 0, owner, base, 16, block[which ^ core, owner].astype(BF16))


def scatter_products(bits, order, items, extra=(), quartered=False):
    sides = 2 if ("batch", 1) in order else 1
    rows = 0
    for kind, left, right in items:
        if kind == "wide":
            rows += right.shape[1] // 768 * (left.shape[1] // 8 // sides)
        elif kind == "tall":
            rows += 384 // sides
        else:
            rows += 96 // sides
    rows += 16 if extra else 0
    shape = (2,) * (len(order) + quartered) + (rows, 384)
    operands = [array for _, left, right in items for array in (left, right)]
    return call(
        functools.partial(
            scatter_body,
            kinds=tuple(kind for kind, _, _ in items),
            order=tuple(order),
            vectors=len(extra),
            quartered=quartered,
        ),
        (1,),
        (bits,),
        [whole(a) for a in (*operands, *extra)],
        [out_whole(shape, BF16)] * (1 if quartered else 2),
        [pltpu.VMEM((768, operands[0].shape[0]), BF16), pltpu.VMEM((768, 768), BF16)]
        + ([pltpu.VMEM((2, 8, 16, 384), F32)] if extra else []),
    )


def quarter_products_body(bits, *refs, kinds, levels):
    count = len(kinds)
    operands = [refs[2 * index : 2 * index + 2] for index in range(count)]
    out, turned, by_owner, by_half, sems = refs[2 * count :]
    sides, cores, owners = 2, 2, 1 << levels
    pending = {}
    turns = {}

    def digits(owner):
        return tuple(((owner >> level) & 1) ^ bits[level] for level in range(levels))

    def next_slot(buffer):
        slot = turns.get(buffer, 0) % 2
        turns[buffer] = turns.get(buffer, 0) + 1
        for copy in pending.pop((buffer, slot), []):
            copy.wait()
        return slot

    def leave(buffer, slot, source, target):
        copies = pending.setdefault((buffer, slot), [])
        copy = pltpu.make_async_copy(source, target, sems.at[buffer, slot, len(copies)])
        copy.start()
        copies.append(copy)

    def spread_rows(value):
        slot = next_slot(0)
        size = 768 // owners // sides
        for owner in range(owners):
            for side in range(sides):
                row = (owner * sides + side) * size
                for column in range(2):
                    part = value[row : row + size, column * 384 : column * 384 + 384]
                    by_owner[(slot, column, side, *digits(owner))] = part
        return slot

    def leave_rows(slot, column, which, base):
        middle = (slice(None),) * levels
        leave(0, slot, by_owner.at[slot, column], out.at[(slice(None), which, *middle, pl.ds(base, 48))])

    base = 0
    for (left, right), kind in zip(operands, kinds):
        turned[...] = left[...].T
        if kind == "wide":
            for which in range(cores):
                for part in range(2):
                    start = which * 1536 + part * 768
                    value = nn(turned[...], right[:, start : start + 768]).astype(BF16)
                    slot = spread_rows(value)
                    for column in range(2):
                        leave_rows(slot, column, which, base + (2 * part + column) * 48)
            base += 192
        elif kind == "tall":
            for part in range(4):
                value = nn(turned[...], right[:, part * 768 : part * 768 + 768]).astype(BF16)
                slot = next_slot(1)
                for which in range(cores):
                    for side in range(sides):
                        row = (which * sides + side) * 192
                        for column in range(2):
                            part_value = value[row : row + 192, column * 384 : column * 384 + 384]
                            by_half[slot, column, side, which] = part_value
                for column in range(2):
                    owner = digits(2 * part + column)
                    target = out.at[(slice(None), slice(None), *owner, pl.ds(base, 192))]
                    leave(1, slot, by_half.at[slot, column], target)
            base += 192
        else:
            slot = spread_rows(nn(turned[...], right[...]).astype(BF16))
            for which in range(cores):
                leave_rows(slot, which, which, base)
            base += 48
    for copies in pending.values():
        for copy in copies:
            copy.wait()


def quarter_products(bits, items, levels):
    rows = sum(48 if kind == "square" else 192 for kind, _, _ in items)
    operands = [array for _, left, right in items for array in (left, right)]
    (out,) = call(
        functools.partial(
            quarter_products_body, kinds=tuple(kind for kind, _, _ in items), levels=levels
        ),
        (1,),
        (bits,),
        [whole(a) for a in operands],
        [out_raw((2, 2) + (2,) * levels + (rows, 384), BF16)],
        [
            pltpu.VMEM((768, operands[0].shape[0]), BF16),
            pltpu.VMEM((2, 2, 2) + (2,) * levels + (48, 384), BF16),
            pltpu.VMEM((2, 2, 2, 2, 192, 384), BF16),
            pltpu.SemaphoreType.DMA((2, 2, 2)),
        ],
    )
    return out


def order_quarters(spots, low, other, across, quarters):
    odd, upper = spots[0], spots[1]
    quarters[odd, upper] = low[...]
    quarters[odd, 1 - upper] = other[...]
    quarters[1 - odd, upper] = across[0]
    quarters[1 - odd, 1 - upper] = across[1]


def join_square(quarters, start, out):
    for core in range(2):
        for side in range(2):
            block = quarters[core, side, start : start + 48]
            out[side * 48 : side * 48 + 48, core * 384 : core * 384 + 384] = block.astype(F32)


def collect_feed_body(spots, low, other, across, expand, reduce, pooled_out, quarters, tall):
    order_quarters(spots, low, other, across, quarters)
    for core in range(2):
        for side in range(2):
            rows = slice(side * 48, side * 48 + 48)
            for part in range(4):
                column = core * 1536 + part * 384
                block = quarters[core, side, part * 48 : part * 48 + 48]
                expand[rows, column : column + 384] = block.astype(F32)
            at = core * 384 + side * 192
            tall[at : at + 192] = quarters[core, side, 192:384].astype(F32)
    reduce[...] = tall[...].T
    join_square(quarters, 384, pooled_out)


def collect_feed(spots, low, other, across):
    return call(
        collect_feed_body,
        (1,),
        (spots,),
        [whole(low), whole(other), whole(across)],
        [out_whole((96, 3072), F32), out_whole((384, 768), F32), out_whole((96, 768), F32)],
        [pltpu.VMEM((2, 2) + low.shape, BF16), pltpu.VMEM((768, 384), F32)],
    )


def collect_last_body(spots, low, other, across, *refs, cut):
    pq, lo, lq, lk, lv, vectors, quarters = refs
    order_quarters(spots, low, other, across, quarters)
    for index, out in enumerate((pq, lo, lq)):
        join_square(quarters, index * 48, out)
    for core in range(2):
        half = quarters[core, 0, cut:].astype(F32) + quarters[core, 1, cut:].astype(F32)
        lk[:, core * 384 : core * 384 + 384] = half[:96]
        lv[:, core * 384 : core * 384 + 384] = half[96:192]
        vectors[core] = half[192:208]


def collect_last(spots, low, other, across, cut):
    return call(
        functools.partial(collect_last_body, cut=cut),
        (1,),
        (spots,),
        [whole(low), whole(other), whole(across)],
        [out_whole((96, 768), F32)] * 5 + [out_whole((2, 16, 384), F32)],
        [pltpu.VMEM((2, 2) + low.shape, BF16)],
    )


def swap(value, axis, bit):
    count = lax.axis_size(axis)
    return lax.ppermute(value, axis, [(i, i ^ (1 << bit)) for i in range(count)])


def shift(value, axis, by):
    count = lax.axis_size(axis)
    pairs = [(i, i + by) for i in range(count) if 0 <= i + by < count]
    return lax.ppermute(value, axis, pairs)


def fold(kept, came):
    low = (kept[1].astype(F32) + came[1].astype(F32)).astype(BF16)
    return low, kept[0].astype(F32) + came[0].astype(F32)


def total_of(terms, *index):
    total = None
    for term in terms:
        value = term[index].astype(F32)
        total = value if total is None else total + value
    return total


def advance(terms, hop):
    came = swap(total_of(terms, 1).astype(BF16), *hop)
    return [term[0] for term in terms], came


def cut(quarters, start, size):
    return quarters[:, :, start : start + size]


def device_step(
    inputs, lengths, cotangent,
    local_query, local_query_bias, local_key, local_value, local_value_bias,
    local_output, local_output_bias, pooled_query, pooled_query_bias,
    pooled_output, pooled_output_bias, conv_key, conv_value, conv_value_bias,
    norm_gain, norm_shift, expand_weight, expand_bias, reduce_weight, reduce_bias,
    final_gain, final_shift,
):
    docs, rows, width = inputs.shape
    devices = lax.axis_size("seq")
    me = lax.axis_index("seq")
    mine = lax.axis_index("batch")
    levels = devices.bit_length() - 1
    size = rows // STRIDE
    flat = docs * rows
    offset = me * rows
    reach = -(-REACH // size)
    gathered = devices <= 2 * reach
    fast = devices == 8 and width == 768 and lax.axis_size("batch") == 4
    base = jnp.where(gathered, 0, offset // STRIDE - reach * size)
    place = jnp.concatenate([offset[None], lengths, base[None]]).astype(jnp.int32)

    def line(vector):
        return vector[None]

    def tokens(array):
        return array.reshape(flat, array.shape[-1])

    taps_key, taps_value = conv_key.T, conv_value.T

    left = shift(inputs[:, rows - HALF :], "seq", 1)
    right = shift(inputs[:, :HALF], "seq", -1)
    q, k_own, v_own, key_near, value_near = project(
        place, inputs, local_query, line(local_query_bias), local_key, local_value,
        line(local_value_bias),
    )
    left, right, k_own = sync(left, right, k_own)
    kx, vx, pooled = pool(
        place, left, right, k_own, v_own, key_near, value_near, line(local_value_bias),
        taps_key, taps_value, line(conv_value_bias),
    )
    own = [pooled[which][None] for which in range(2)]

    mixes, probs_one = [], []

    def local_step(doc, token):
        mix, probs = local_forward(token, q, kx, vx, doc)
        mixes.append(mix)
        probs_one.append(probs)
        return mix

    if gathered:
        orders = ([2, 1, 0], [0, 2, 1]) if levels == 3 else (list(range(levels)),) * 2
        have = own
        pieces = [[own[0]], [own[1]]]
        relative = [[0], [0]]
        token = place
        for stage in range(levels):
            came = [swap(have[which], "seq", orders[which][stage]) for which in range(2)]
            if stage == 0:
                came[0], came[1], token = sync(came[0], came[1], token)
            if 0 < stage <= docs:
                done = local_step(stage - 1, token)
            if stage == levels - 1:
                while len(mixes) < docs:
                    local_step(len(mixes), token)
                mix_one, middle, middle_low, q2 = middle_forward(
                    token, inputs, local_output, line(local_output_bias), pooled_query,
                    line(pooled_query_bias), mixes,
                )
                came[0], came[1], q2, token = sync(came[0], came[1], q2, token)
            elif stage > 0:
                came[0], came[1], mixes[stage - 1], token = sync(
                    came[0], came[1], done, token
                )
            for which in range(2):
                pieces[which].append(came[which])
                relative[which] += [r ^ (1 << orders[which][stage]) for r in relative[which]]
                if stage < levels - 1:
                    have[which] = jnp.concatenate([have[which], came[which]])
        slots = jnp.stack([me ^ jnp.array(r, jnp.int32) for r in relative])
    else:
        pieces = [
            [own[which]]
            + [
                shift(own[which], "seq", sign * distance)
                for distance in range(1, reach + 1)
                for sign in (1, -1)
            ]
            for which in range(2)
        ]
        spots = [reach] + [
            reach - sign * distance for distance in range(1, reach + 1) for sign in (1, -1)
        ]
        slots = jnp.array([spots, spots], jnp.int32)
        token = place
        for doc in range(docs):
            local_step(doc, token)
        mix_one, middle, middle_low, q2 = middle_forward(
            token, inputs, local_output, line(local_output_bias), pooled_query,
            line(pooled_query_bias), mixes,
        )

    keys, values, probs_two, mix_two, summed, expand_near, reduce_near = pooled_forward(
        token, slots, pieces[0], pieces[1], q2, middle, pooled_output, line(pooled_output_bias),
        expand_weight, reduce_weight,
    )
    (
        outputs, normed_low, hidden, grad_branch, grad_pre, grad_summed, grad_second, grad_mix_two,
        vec_feed, vec_wide,
    ) = feed(
        token, summed, cotangent, expand_near, line(expand_bias), reduce_near,
        line(reduce_bias), line(norm_gain), line(norm_shift), line(final_gain),
        line(final_shift), pooled_output,
    )

    order_first = [("batch", 1)] + [("seq", level) for level in range(levels)]
    order_last = order_first[1:]

    def bits_of(order):
        ids = [mine & 1] + [(mine if axis == "batch" else me) >> bit & 1 for axis, bit in order]
        return jnp.stack(ids).astype(jnp.int32)

    seq_bits = jnp.stack([me >> level & 1 for level in range(levels)]).astype(jnp.int32)

    def over_batch(blocks):
        part = blocks.shape[2:]
        flat_blocks = blocks.reshape(-1, blocks.shape[-1])
        mine_part = lax.psum_scatter(flat_blocks, "batch", scatter_dimension=0, tiled=True)
        return mine_part.reshape(part)

    if fast:
        feed_blocks = quarter_products(
            seq_bits,
            [
                ("wide", normed_low, grad_pre),
                ("tall", grad_branch, hidden),
                ("square", tokens(mix_two), grad_second),
            ],
            levels,
        )
        feed_blocks, grad_mix_two, token = sync(feed_blocks, grad_mix_two, token)
        feed_part = over_batch(feed_blocks)

    blocks = devices if gathered else 2 * reach + 1
    if gathered:
        back = ([0, 1, 2], [1, 2, 0]) if levels == 3 else (list(range(levels)),) * 2
        places = []
        for which in range(2):
            spots = []
            for block in range(devices):
                relative = 0
                for at, bit in enumerate(back[which]):
                    relative |= (block >> (levels - 1 - at) & 1) << bit
                spots.append(relative)
            places.append(me ^ jnp.array(spots, jnp.int32))
        places = jnp.stack(places)
        half_blocks = devices // 2
    else:
        middle_first = [reach] + [spot for spot in range(blocks) if spot != reach]
        places = jnp.array([middle_first, middle_first], jnp.int32)
        half_blocks = 1
    grad_q2, dk_kept, dk_sent, dv_kept, dv_sent = pooled_backward(
        places, token, q2, keys, values, probs_two, grad_mix_two, size, half_blocks
    )
    grad_middle, grad_first, grad_mix_one, vec_first = first_backward(
        token, grad_q2, grad_summed, pooled_query, local_output
    )
    back_parts = ()

    def back_step(doc, token):
        return local_backward(
            token, q, kx, vx, grad_mix_one, probs_one[doc], doc, back_parts
        )

    if gathered:
        kept = [part.reshape((2,) * (levels - 1) + part.shape[1:]) for part in (dk_kept, dv_kept)]
        sent = [part.reshape((2,) * (levels - 1) + part.shape[1:]) for part in (dk_sent, dv_sent)]
        for stage in range(levels):
            came = [swap(sent[which], "seq", back[which][stage]) for which in range(2)]
            if stage < docs:
                back_parts = list(back_step(stage, token))
            if stage == docs - 1:
                from_left = shift(back_parts[3], "seq", 1)
                from_right = shift(back_parts[2], "seq", -1)
            if fast and stage == 0:
                came[0], came[1], back_parts[0], token = sync(
                    came[0], came[1], back_parts[0], token
                )
            if fast and stage == 1:
                came[0], came[1], from_left, from_right, token = sync(
                    came[0], came[1], from_left, from_right, token
                )
            if fast and stage == 2:
                middle_kept, middle_sent = scatter_products(
                    bits_of(order_first) + 0 * token[0],
                    order_first,
                    [
                        ("square", tokens(middle_low), tokens(grad_q2)),
                        ("square", tokens(mix_one), grad_first),
                        ("square", tokens(inputs), tokens(back_parts[0])),
                    ],
                )
                came[0], came[1], middle_sent, token = sync(
                    came[0], came[1], middle_sent, token
                )
            if stage < levels - 1:
                for which in range(2):
                    sent[which], kept[which] = fold(kept[which], came[which])
        pooled_grads = [kept[0], came[0], kept[1], came[1]]
    else:
        pooled_grads = []
        for kept, sent in ((dk_kept, dk_sent), (dv_kept, dv_sent)):
            total = kept[0]
            for distance in range(1, reach + 1):
                total = total + shift(sent[reach - distance], "seq", -distance).astype(F32)
                total = total + shift(sent[reach + distance - 1], "seq", distance).astype(F32)
            after = shift(total[:, :1].astype(BF16), "seq", -1).astype(F32)
            total = jnp.concatenate([total[:, :size], jnp.tile(after, (1, 8, 1))], axis=1)
            pooled_grads += [total, jnp.zeros_like(total)]
        for doc in range(docs):
            back_parts = back_step(doc, token)
        from_left = shift(back_parts[3], "seq", 1)
        from_right = shift(back_parts[2], "seq", -1)
    dq, own_grads = back_parts[:2]
    if fast:
        middle_came = swap(middle_sent, "batch", 0)
    grad_k, grad_v, vec_input = key_value_gradients(
        token, pooled_grads, kx, vx, taps_key, taps_value,
        own_grads, from_left, from_right, dq,
    )
    if fast:
        last_kept, last_sent = scatter_products(
            bits_of(order_last),
            order_last,
            [("square", tokens(inputs), grad_k), ("square", tokens(inputs), grad_v)],
            (vec_feed, vec_first, vec_input, vec_wide),
        )
        last_sent, middle_came, token = sync(last_sent, middle_came, token)
        last_came = swap(last_sent, "batch", 0)
        middle_terms, middle_came = advance([middle_kept, middle_came], ("batch", 1))
    input_grad = input_gradient(
        token, tokens(dq), grad_k, grad_v, grad_middle, local_query, local_key, local_value
    )

    if fast:
        cut_feed = feed_part.shape[-2] // 2
        one = [feed_part[..., :cut_feed, :]]
        two = [feed_part[..., cut_feed:, :]]

        def advance_second(terms, hop):
            came = swap(total_of(terms, slice(None), 1).astype(BF16), *hop)
            return [term[:, 0] for term in terms], came

        one, one_came = advance(one, ("seq", 0))
        two, two_came = advance_second(two, ("seq", 1))
        input_grad, last_came, middle_came, one_came, two_came = sync(
            input_grad, last_came, middle_came, one_came, two_came
        )
        last_terms, last_came = advance([last_kept, last_came], ("seq", 0))
        middle_terms, middle_came = advance_second(middle_terms + [middle_came], ("seq", 1))
        one, one_came = advance(one + [one_came], ("seq", 1))
        two, two_came = advance(two + [two_came], ("seq", 0))
        last_came, middle_came, one_came, two_came = sync(
            last_came, middle_came, one_came, two_came
        )

        last_terms, last_came = advance(last_terms + [last_came], ("seq", 1))
        one, two = one + [one_came], two + [two_came]
        feed_came = swap(
            jnp.concatenate([total_of(one, 1), total_of(two, 1)]).astype(BF16), "seq", 2
        )
        middle_terms, middle_came = advance(middle_terms + [middle_came], ("seq", 0))
        last_came, middle_came, feed_came = sync(last_came, middle_came, feed_came)

        last_terms, last_came = advance(last_terms + [last_came], ("seq", 2))
        middle_terms, middle_came = advance(middle_terms + [middle_came], ("seq", 2))
        feed_low = (
            jnp.concatenate([total_of(one, 0), total_of(two, 0)]) + feed_came.astype(F32)
        ).astype(BF16)
        feed_other = swap(feed_low, "batch", 1)
        last_came, middle_came, feed_other = sync(last_came, middle_came, feed_other)
        cut_at = middle_came.shape[0]
        low = jnp.concatenate(
            [
                total_of(middle_terms + [middle_came], Ellipsis),
                total_of(last_terms + [last_came], Ellipsis),
            ]
        ).astype(BF16)
        other = swap(low, "batch", 1)
        feed_across = swap(jnp.stack([feed_low, feed_other]), "batch", 0)
        low, other, feed_across = sync(low, other, feed_across)
        across = swap(jnp.stack([low, other]), "batch", 0)
        spots = jnp.stack([mine & 1, mine >> 1]).astype(jnp.int32)
        grad_expand, grad_reduce, grad_po = collect_feed(spots, feed_low, feed_other, feed_across)
        grad_pq, grad_lo, grad_lq, grad_lk, grad_lv, lines = collect_last(
            spots, low, other, across, cut_at
        )
        vec_low, vec_high = lines[0, :, :96], lines[1, :, :96]
        (fg, fs, rb, ng, ns, pob) = [vec_low[index] for index in range(6)]
        pqb, lob = lines[0, 0, LANES : LANES + 96], lines[0, 1, LANES : LANES + 96]
        grad_eb = vec_low[8:12].reshape(-1)
    else:

        def plain(left_array, right_array):
            product = tn(left_array, right_array)
            part = lax.psum_scatter(product, "seq", scatter_dimension=0, tiled=True)
            return lax.psum(part.astype(BF16), "batch").astype(F32)

        grad_expand = plain(normed_low, grad_pre)
        grad_reduce = plain(hidden, grad_branch)
        grad_po = plain(tokens(mix_two), grad_second)
        grad_pq = plain(tokens(middle_low), tokens(grad_q2))
        grad_lo = plain(tokens(mix_one), grad_first)
        grad_lq = plain(tokens(inputs), tokens(dq))
        grad_lk = plain(tokens(inputs), grad_k)
        grad_lv = plain(tokens(inputs), grad_v)
        vectors = jnp.concatenate(
            [vec_feed, vec_first, vec_input, vec_wide.reshape(-1, width)], axis=0
        )
        vectors = lax.psum(vectors, ("seq", "batch"))
        share = width // devices
        part = lax.dynamic_slice_in_dim(vectors, me * share, share, axis=1)
        wide = vectors[32:].reshape(-1)
        wide_share = wide.shape[0] // devices
        grad_eb = lax.dynamic_slice_in_dim(wide, me * wide_share, wide_share, axis=0)
        (fg, fs, rb, ng, ns, pob) = [part[index] for index in range(6)]
        pqb, lob = part[8], part[9]
        vec_high = part[16:32]
    grad_ck = vec_high[:KER].T
    grad_cv = vec_high[KER : 2 * KER].T
    cvb, lqb, lvb = vec_high[10], vec_high[11], vec_high[12]
    return (
        outputs, input_grad,
        grad_lq, lqb, grad_lk, grad_lv, lvb, grad_lo, lob, grad_pq, pqb, grad_po, pob,
        grad_ck, grad_cv, cvb, ng, ns, grad_expand, grad_eb, grad_reduce, rb, fg, fs,
    )


def solution(mesh):
    vector = P("seq")
    matrix = P("seq", None)
    return jax.shard_map(
        device_step,
        mesh=mesh,
        in_specs=(P("batch", "seq", None), P("batch"), P("batch", "seq", None)) + (P(),) * 22,
        out_specs=(
            P("batch", "seq", None), P("batch", "seq", None),
            matrix, vector, matrix, matrix, vector, matrix, vector, matrix, vector, matrix, vector,
            matrix, matrix, vector, vector, vector, matrix, vector, matrix, vector, vector, vector,
        ),
        check_vma=False,
    )
```

```python
import functools
import math

import jax
import jax.numpy as jnp
from jax import lax
from jax.experimental import pallas as pl
from jax.experimental.pallas import tpu as pltpu
from jax.sharding import PartitionSpec as P

HEADS = 12
HD = 64
WIN = 128
PWIN = 512
KER = 5
STRIDE = 4
HALF = WIN // 2
REACH = PWIN // 2
NEGATIVE = -1e30
SCALE = 1.0 / math.sqrt(HD)
EPSILON = 1e-05
LANES = 128
TILE = 128
ROWS = 128
CHUNK = 768
PAIRS = 2
F32 = jnp.float32
BF16 = jnp.bfloat16


def nn(left, right):
    return jnp.dot(left, right, preferred_element_type=F32)


def nt(left, right):
    return lax.dot_general(left, right, (((1,), (1,)), ((), ())), preferred_element_type=F32)


def tn(left, right):
    return lax.dot_general(left, right, (((0,), (0,)), ((), ())), preferred_element_type=F32)


def column_sum(block):
    return jnp.sum(block.astype(F32), axis=0, keepdims=True)


def call(body, grid, scalars, inputs, outputs, scratch=(), spare=8):
    used = spare * 2**20
    arrays, in_specs, out_specs, shapes = [], [], [], []

    def spec(shape, dtype, block, index):
        nonlocal used
        if block is None:
            return pl.BlockSpec(memory_space=pltpu.VMEM)
        if block == "raw":
            return pl.BlockSpec(memory_space=pl.ANY)
        used += 2 * math.prod(block) * jnp.dtype(dtype).itemsize
        return pl.BlockSpec(block, index)

    for array, block, index in inputs:
        in_specs.append(spec(array.shape, array.dtype, block, index))
        if block is not None:
            array = pltpu.with_memory_space_constraint(array, pltpu.HBM)
        arrays.append(array)
    for shape, dtype, block, index in outputs:
        out_specs.append(spec(shape, dtype, block, index))
        plain = block is None
        shapes.append((jax.ShapeDtypeStruct if plain else pltpu.HBM)(shape, dtype))
    for item in scratch:
        if hasattr(item, "shape") and item.memory_space == pltpu.VMEM:
            used += math.prod(item.shape) * jnp.dtype(item.dtype).itemsize
    return pl.pallas_call(
        body,
        grid_spec=pltpu.PrefetchScalarGridSpec(
            num_scalar_prefetch=len(scalars),
            grid=grid,
            in_specs=in_specs,
            out_specs=out_specs,
            scratch_shapes=list(scratch),
        ),
        out_shape=shapes,
        compiler_params=pltpu.CompilerParams(
            dimension_semantics=("arbitrary",) * len(grid), vmem_limit_bytes=used
        ),
        cost_estimate=pl.CostEstimate(flops=1000, bytes_accessed=1000, transcendentals=0),
    )(*scalars, *arrays)


def raw(array):
    return (array, "raw", None)


def out_raw(shape, dtype):
    return (shape, dtype, "raw", None)


def whole(array):
    return (array, None, None)


def out_whole(shape, dtype):
    return (shape, dtype, None, None)


def sync(*values):
    return lax.optimization_barrier(values)


def stack_heads(block):
    lane = lax.broadcasted_iota(jnp.int32, block.shape, 1)
    zero = jnp.zeros_like(block)
    return jnp.concatenate(
        [jnp.where(lane < HD, block, zero), jnp.where(lane < HD, zero, block)], axis=0
    )


def unstack(block):
    half = block.shape[1] // 2
    joined = jnp.concatenate([block[:HD, :half], block[HD:, half:]], axis=0)
    return joined.T


def positions(shape, dim):
    return lax.broadcasted_iota(jnp.int32, shape, dim)


def project_body(place, x_far, wq_far, bq, wk_far, wv_far, bv, q, k, v, wk, wv, x, wq, sems):
    docs, rows, width = x.shape
    fetches = [
        pltpu.make_async_copy(far, near, sems.at[index])
        for index, (far, near) in enumerate(
            ((x_far, x), (wq_far, wq), (wk_far, wk), (wv_far, wv))
        )
    ]
    for fetch in fetches:
        fetch.start()
    fetches[0].wait()
    flat = x[...].reshape(docs * rows, width)
    fetches[1].wait()
    q[...] = (nn(flat, wq[...]) + bq[...]).astype(BF16).reshape(q.shape)
    fetches[2].wait()
    k[...] = nn(flat, wk[...]).astype(BF16).reshape(k.shape)
    fetches[3].wait()
    v[...] = (nn(flat, wv[...]) + bv[...]).astype(BF16).reshape(v.shape)


def project(place, x, wq, bq, wk, wv, bv):
    return call(
        project_body,
        (1,),
        (place,),
        [raw(x), raw(wq), whole(bq), raw(wk), raw(wv), whole(bv)],
        [out_whole(x.shape, BF16)] * 3 + [out_whole(wk.shape, BF16)] * 2,
        [
            pltpu.VMEM(x.shape, BF16),
            pltpu.VMEM(wq.shape, BF16),
            pltpu.SemaphoreType.DMA((4,)),
        ],
    )


def pool_body(place, left, right, k, v, wk, wv, bv, ck, cv, bcv, kx, vx, pooled, rows):
    offset = place[0]
    docs, own_rows, width = k.shape
    rims = jnp.concatenate(
        [part[doc] for doc in range(docs) for part in (left, right)], axis=0
    )
    size = own_rows + WIN
    count = pooled.shape[2]
    spot = offset - HALF + positions((size, 1), 0)
    for which, (weight, bias, taps, own, out) in enumerate(
        ((wk, None, ck, k, kx), (wv, bv, cv, v, vx))
    ):
        value = nn(rims, weight[...])
        if bias is not None:
            value = value + bias[...]
        value = value.astype(BF16)
        for doc in range(docs):
            at = doc * WIN
            out[doc, :HALF] = value[at : at + HALF]
            out[doc, HALF : HALF + own_rows] = own[doc]
            out[doc, HALF + own_rows :] = value[at + HALF : at + WIN]
            valid = (spot >= 0) & (spot < place[1 + doc])
            for group in range(width // LANES):
                lanes = slice(group * LANES, (group + 1) * LANES)
                rows[group] = jnp.where(valid, out[doc, :, lanes].astype(F32), 0.0)
                total = jnp.zeros((count, LANES), F32)
                for tap in range(KER):
                    start = HALF - KER // 2 + tap
                    read = rows[group, pl.ds(start, count, stride=STRIDE), :]
                    total = total + read * taps[tap : tap + 1, lanes]
                if which == 1:
                    total = total + bcv[:, lanes]
                pooled[which, doc, :, lanes] = total.astype(BF16)


def pool(place, left, right, k, v, wk, wv, bv, ck, cv, bcv):
    docs, rows, width = k.shape
    extended = rows + WIN
    return call(
        pool_body,
        (1,),
        (place,),
        [whole(a) for a in (left, right, k, v, wk, wv, bv, ck, cv, bcv)],
        [
            out_whole((docs, extended, width), BF16),
            out_whole((docs, extended, width), BF16),
            out_whole((2, docs, rows // STRIDE, width), BF16),
        ],
        [pltpu.VMEM((width // LANES, extended, LANES), F32)],
    )


def local_bias(tile, offset, length):
    shape = (TILE + WIN, TILE)
    key = positions(shape, 0)
    query = positions(shape, 1)
    spot = offset + tile * TILE - HALF + key
    allowed = (
        (key >= query) & (key < query + WIN) & (spot >= 0) & (spot < length)
    ) | (key == query + HALF)
    return jnp.where(allowed, 0.0, NEGATIVE)


def softmax_columns(scores):
    top = jnp.max(scores, axis=0, keepdims=True)
    grown = jnp.exp(scores - top)
    return grown * (1.0 / jnp.sum(grown, axis=0, keepdims=True))


def local_forward_body(place, q, kx, vx, mix, probs, *, doc):
    offset, length = place[0], place[1 + doc]
    span = TILE + WIN
    for tile in range(q.shape[1] // TILE):
        half_bias = local_bias(tile, offset, length)
        bias = jnp.concatenate([half_bias, half_bias], axis=1)
        first = tile * TILE
        for pair in range(q.shape[2] // LANES):
            lanes = slice(pair * LANES, (pair + 1) * LANES)
            queries = stack_heads(q[doc, first : first + TILE, lanes]) * SCALE
            scores = nt(kx[doc, first : first + span, lanes], queries) + bias
            chance = softmax_columns(scores)
            probs[pair, tile] = chance
            turned = vx[doc, first : first + span, lanes].T
            mixed = nn(turned, chance.astype(BF16))
            mix[first : first + TILE, lanes] = unstack(mixed).astype(BF16)


def local_forward(place, q, kx, vx, doc):
    _, rows, width = q.shape
    pairs, tiles, span = width // LANES, rows // TILE, TILE + WIN
    return call(
        functools.partial(local_forward_body, doc=doc),
        (1,),
        (place,),
        [whole(a) for a in (q, kx, vx)],
        [
            out_whole((rows, width), BF16),
            out_whole((pairs, tiles, span, 2 * TILE), F32),
        ],
    )


def middle_body(place, x, wo, bo, wpq, bpq, *refs):
    docs, rows = x.shape[0], x.shape[1]
    mixes, (mix, middle, middle_low, q2) = refs[:docs], refs[docs:]
    for doc in range(docs):
        mix[doc] = mixes[doc][...]
    flat = docs * rows
    branch = nn(mix[...].reshape(flat, x.shape[2]), wo[...]) + bo[...]
    total = x[...].reshape(flat, x.shape[2]).astype(F32) + branch
    middle[...] = total.reshape(middle.shape)
    low = total.astype(BF16)
    middle_low[...] = low.reshape(middle_low.shape)
    q2[...] = (nn(low, wpq[...]) + bpq[...]).astype(BF16).reshape(q2.shape)


def middle_forward(place, x, wo, bo, wpq, bpq, mixes):
    docs, rows, width = x.shape
    return call(
        middle_body,
        (1,),
        (place,),
        [whole(a) for a in (x, wo, bo, wpq, bpq, *mixes)],
        [
            out_whole((docs, rows, width), BF16),
            out_whole((docs, rows, width), F32),
            out_whole((docs, rows, width), BF16),
            out_whole((docs, rows, width), BF16),
        ],
    )


def attention_back(keys, values, queries, grads, chance):
    stacked_grads = stack_heads(grads)
    stacked_queries = stack_heads(queries)
    grad_chance = nt(values, stacked_grads * SCALE)
    dots = jnp.sum(chance * grad_chance, axis=0, keepdims=True)
    grad_raw = (chance * (grad_chance - dots)).astype(BF16)
    grad_keys = nn(grad_raw, stacked_queries)
    grad_values = nn(chance.astype(BF16), stacked_grads)
    grad_queries = unstack(nn(keys.T, grad_raw))
    return grad_queries, grad_keys, grad_values


def first_back_body(place, gq2, gsum, wpq, wo, gmid, gfirst, gmix, vec):
    docs, rows, width = gsum.shape
    flat = docs * rows
    grads = gq2[...].reshape(flat, width)
    total = gsum[...].reshape(flat, width) + nt(grads, wpq[...])
    gmid[...] = total.reshape(gmid.shape)
    low = total.astype(BF16)
    gfirst[...] = low
    gmix[...] = nt(low, wo[...]).astype(BF16).reshape(gmix.shape)
    vec[...] = jnp.zeros_like(vec)
    vec[0:1] = column_sum(grads)
    vec[1:2] = column_sum(low)


def first_backward(place, gq2, gsum, wpq, wo):
    docs, rows, width = gsum.shape
    return call(
        first_back_body,
        (1,),
        (place,),
        [whole(a) for a in (gq2, gsum, wpq, wo)],
        [
            out_whole((docs, rows, width), F32),
            out_whole((docs * rows, width), BF16),
            out_whole((docs, rows, width), BF16),
            out_whole((8, width), F32),
        ],
    )


def local_backward_body(place, q, kx, vx, gmix, probs, *refs, doc):
    earlier = refs[: len(refs) - 6]
    dq, own, low_left, low_right, dk, dv = refs[len(refs) - 6 :]
    rows = q.shape[1]
    for old, new in zip(earlier, (dq, own, low_left, low_right)):
        new[:doc] = old[...]
    span = TILE + WIN
    dk[...] = jnp.zeros_like(dk)
    dv[...] = jnp.zeros_like(dv)
    for tile in range(rows // TILE):
        first = tile * TILE
        for pair in range(q.shape[2] // LANES):
            lanes = slice(pair * LANES, (pair + 1) * LANES)
            grad_q, grad_k, grad_v = attention_back(
                kx[doc, first : first + span, lanes],
                vx[doc, first : first + span, lanes],
                q[doc, first : first + TILE, lanes],
                gmix[doc, first : first + TILE, lanes],
                probs[pair, tile],
            )
            dq[doc, first : first + TILE, lanes] = grad_q.astype(BF16)
            dk[first : first + span, lanes] += grad_k
            dv[first : first + span, lanes] += grad_v
    for which, part in enumerate((dk, dv)):
        own[doc, which] = part[HALF : HALF + rows]
        low_left[doc, which] = part[:HALF].astype(BF16)
        low_right[doc, which] = part[HALF + rows :].astype(BF16)


def local_backward(place, q, kx, vx, gmix, probs, doc, earlier=()):
    _, rows, width = q.shape
    span = TILE + WIN
    return call(
        functools.partial(local_backward_body, doc=doc),
        (1,),
        (place,),
        [whole(a) for a in (q, kx, vx, gmix, probs, *earlier)],
        [
            out_whole((doc + 1, rows, width), BF16),
            out_whole((doc + 1, 2, rows, width), F32),
            out_whole((doc + 1, 2, HALF, width), BF16),
            out_whole((doc + 1, 2, HALF, width), BF16),
        ],
        [
            pltpu.VMEM((rows + WIN, width), F32),
            pltpu.VMEM((rows + WIN, width), F32),
        ],
    )


def pooled_forward_body(place, slots, *refs, pieces):
    key_pieces = refs[:pieces]
    value_pieces = refs[pieces : 2 * pieces]
    (
        q2, middle, wpo, bpo, we, wr,
        keys_out, values_out, probs, mix, summed, we_near, wr_near,
        keys, values, bias, sems,
    ) = refs[2 * pieces :]
    doc, pair = pl.program_id(0), pl.program_id(1)
    fetches = [
        pltpu.make_async_copy(we, we_near, sems.at[0]),
        pltpu.make_async_copy(wr, wr_near, sems.at[1]),
    ]
    last = (pair == pl.num_programs(1) - 1) & (doc == pl.num_programs(0) - 1)
    leaves = [
        pltpu.make_async_copy(keys.at[each], keys_out.at[each], sems.at[2 + each])
        for each in range(keys.shape[0])
    ] + [
        pltpu.make_async_copy(
            values.at[each], values_out.at[each], sems.at[2 + keys.shape[0] + each]
        )
        for each in range(keys.shape[0])
    ]

    @pl.when((pair == 0) & (doc == 0))
    def _():
        for fetch in fetches:
            fetch.start()

    offset, length, base = place[0], place[1 + doc], place[1 + pl.num_programs(0)]
    count = keys.shape[1]

    @pl.when(pair == 0)
    def _():
        for where, group, out in ((0, key_pieces, keys), (1, value_pieces, values)):
            at = 0
            for piece in group:
                size = piece.shape[2]
                for block in range(piece.shape[0]):
                    spot = pl.multiple_of(slots[where, at] * size, size)
                    out[doc, pl.ds(spot, size), :] = piece[block, doc]
                    at += 1
        if True:
            shape = (count, q2.shape[1])
            spot = base + positions(shape, 0)
            centre = offset // STRIDE + positions(shape, 1) // STRIDE
            allowed = (
                (spot >= centre - REACH)
                & (spot < centre + REACH)
                & (spot >= 0)
                & (spot * STRIDE < length)
            ) | (spot == centre)
            bias[...] = jnp.where(allowed, 0.0, NEGATIVE)
        for each in range(keys.shape[0]):

            @pl.when(doc == each)
            def _():
                leaves[each].start()
                leaves[keys.shape[0] + each].start()

    for each in range(PAIRS):
        lanes = pl.ds(pl.multiple_of((pair * PAIRS + each) * LANES, LANES), LANES)
        queries = stack_heads(q2[doc, :, lanes]) * SCALE
        half_bias = bias[...]
        scores = nt(keys[doc, :, lanes], queries) + jnp.concatenate([half_bias, half_bias], axis=1)
        chance = softmax_columns(scores)
        probs[0, each] = chance
        mixed = nn(values[doc, :, lanes].T, chance.astype(BF16))
        mix[doc, :, lanes] = unstack(mixed).astype(BF16)

    @pl.when(last)
    def _():
        for copy in fetches + leaves:
            copy.wait()
        flat = (mix.shape[0] * mix.shape[1], mix.shape[2])
        second = nn(mix[...].reshape(flat), wpo[...]) + bpo[...]
        summed[...] = middle[...] + second.reshape(summed.shape)


def pooled_forward(place, slots, key_pieces, value_pieces, q2, middle, wpo, bpo, we, wr):
    docs, rows, width = q2.shape
    pairs, tiles = width // LANES, rows // TILE
    size = key_pieces[0].shape[2]
    count = size * slots.shape[1]

    return call(
        functools.partial(pooled_forward_body, pieces=len(key_pieces)),
        (docs, pairs // PAIRS),
        (place, slots),
        [whole(a) for a in (*key_pieces, *value_pieces, q2, middle, wpo, bpo)]
        + [raw(we), raw(wr)],
        [
            out_raw((docs, count, width), BF16),
            out_raw((docs, count, width), BF16),
            (
                (docs, pairs, count, 2 * rows),
                F32,
                (1, PAIRS, count, 2 * rows),
                lambda doc, pair, *_: (doc, pair, 0, 0),
            ),
            out_whole((docs, rows, width), BF16),
            out_whole((docs, rows, width), F32),
            out_whole(we.shape, BF16),
            out_whole(wr.shape, BF16),
        ],
        [
            pltpu.VMEM((docs, count, width), BF16),
            pltpu.VMEM((docs, count, width), BF16),
            pltpu.VMEM((count, rows), F32),
            pltpu.SemaphoreType.DMA((2 + 2 * docs,)),
        ],
    )


def pooled_backward_body(
    places, token, q2, keys, values, probs, grads, dq, dk_kept, dk_sent, dv_kept, dv_sent, sums
):
    doc, step = pl.program_id(0), pl.program_id(1)
    size = dk_kept.shape[2]
    half = dk_kept.shape[0]
    rows = keys.shape[1]
    for each in range(PAIRS):
        inner = slice(each * LANES, (each + 1) * LANES)
        lanes = pl.ds(pl.multiple_of((step * PAIRS + each) * LANES, LANES), LANES)
        grad_q, *total = attention_back(
            keys[0, :, inner], values[0, :, inner], q2[0, :, inner], grads[0, :, inner],
            probs[0, each],
        )
        dq[doc, :, lanes] = grad_q.astype(BF16)
        for which, (kept, sent) in enumerate(((dk_kept, dk_sent), (dv_kept, dv_sent))):
            sums[each, which, :rows] = total[which]
            sums[each, which, rows:] = jnp.zeros((8, LANES), F32)
            for block in range(half + sent.shape[0]):
                start = pl.multiple_of(places[which, block] * (size - 8), size - 8)
                part = sums[each, which, pl.ds(start, size), :]
                if block < half:
                    kept[block, doc, :, lanes] = part
                else:
                    sent[block - half, doc, :, lanes] = part.astype(BF16)


def pooled_backward(places, token, q2, keys, values, probs, grads, size, kept):
    docs, rows, width = q2.shape
    count = keys.shape[1]
    blocks = count // size
    tiles = rows // TILE

    def lanes_of(array):
        return (array, (1, array.shape[1], PAIRS * LANES), lambda doc, pair, *_: (doc, 0, pair))

    return call(
        pooled_backward_body,
        (docs, width // LANES // PAIRS),
        (places, token),
        [
            lanes_of(q2),
            lanes_of(keys),
            lanes_of(values),
            (
                probs,
                (1, PAIRS, count, 2 * rows),
                lambda doc, pair, *_: (doc, pair, 0, 0),
            ),
            lanes_of(grads),
        ],
        [
            out_whole((docs, rows, width), BF16),
            out_whole((kept, docs, size + 8, width), F32),
            out_whole((blocks - kept, docs, size + 8, width), BF16),
            out_whole((kept, docs, size + 8, width), F32),
            out_whole((blocks - kept, docs, size + 8, width), BF16),
        ],
        [pltpu.VMEM((PAIRS, 2, count + 8, LANES), F32)],
    )


def feed_body(
    place, summed, cotangent, we, be, wr, br, ng, ns, fg, fs, wpo,
    outputs_far, normed_low, hidden, grad_branch, grad_pre, grad_summed_far, grad_second,
    grad_mix_far, vec, vec_wide,
    normed, slope, work, unit, outputs, grad_mix, sems,
):
    docs, rows = cotangent.shape[0], cotangent.shape[1]
    width = summed.shape[2]
    wide = we.shape[1]
    steps = rows // ROWS
    blocks = [
        (doc, step * ROWS, doc * rows + step * ROWS)
        for doc in range(docs)
        for step in range(steps)
    ]
    leaving = []

    def leave(source, target, doc, start, row):
        copy = pltpu.make_async_copy(
            source.at[pl.ds(row, ROWS)],
            target.at[doc, pl.ds(start, ROWS)],
            sems.at[len(leaving)],
        )
        copy.start()
        leaving.append(copy)


    def normal(value):
        centred = value - jnp.mean(value, axis=-1, keepdims=True)
        scale = lax.rsqrt(jnp.mean(centred * centred, axis=-1, keepdims=True) + EPSILON)
        return centred * scale, scale

    scales = []
    for doc, start, row in blocks:
        norm, scale = normal(summed[doc, start : start + ROWS])
        scales.append(scale)
        unit[row : row + ROWS] = norm
        full = norm * ng[...] + ns[...]
        normed[row : row + ROWS] = full
        normed_low[row : row + ROWS] = full.astype(BF16)

    def expand(index):
        part = slice(index * CHUNK, (index + 1) * CHUNK)
        pre = nn(normed_low[...], we[:, part]) + be[:, part]
        cdf = 0.5 * (1.0 + lax.erf(pre * math.sqrt(0.5)))
        hidden[:, part] = (pre * cdf).astype(BF16)
        slope[:, part] = cdf + pre * (jnp.exp(pre * pre * -0.5) * (1.0 / math.sqrt(2.0 * math.pi)))
    for index in range(wide // CHUNK):
        expand(index)

    for start in range(0, width, CHUNK):
        part = slice(start, start + CHUNK)
        work[:, part] = normed[:, part] + (nn(hidden[...], wr[:, part]) + br[:, part])

    sums = [jnp.zeros((1, width), F32) for _ in range(6)]
    for doc, start, row in blocks:
        norm, scale = normal(work[row : row + ROWS])
        spot = place[0] + start + positions((ROWS, 1), 0)
        valid = (spot < place[1 + doc]).astype(F32)
        outputs[row : row + ROWS] = (valid * (norm * fg[...] + fs[...])).astype(BF16)
        leave(outputs, outputs_far, doc, start, row)
        error = valid * cotangent[doc, start : start + ROWS].astype(F32)
        sums[0] += column_sum(error * norm)
        sums[1] += column_sum(error)
        scaled = error * fg[...]
        rest = (
            scaled
            - jnp.mean(scaled, axis=-1, keepdims=True)
            - norm * jnp.mean(scaled * norm, axis=-1, keepdims=True)
        ) * scale
        work[row : row + ROWS] = rest
        low = rest.astype(BF16)
        grad_branch[row : row + ROWS] = low
        sums[2] += column_sum(low)

    def reduce(index):
        part = slice(index * CHUNK, (index + 1) * CHUNK)
        low = (nt(grad_branch[...], wr[part, :]) * slope[:, part]).astype(BF16)
        grad_pre[:, part] = low
        vec_wide[:, part] = column_sum(low)

    for index in range(wide // CHUNK):
        reduce(index)

    for start in range(0, width, CHUNK):
        part = slice(start, start + CHUNK)
        work[:, part] += nt(grad_pre[...], we[part, :])

    for (doc, start, row), scale in zip(blocks, scales):
        error = work[row : row + ROWS]
        norm = unit[row : row + ROWS]
        sums[3] += column_sum(error * norm)
        sums[4] += column_sum(error)
        scaled = error * ng[...]
        grad = (
            scaled
            - jnp.mean(scaled, axis=-1, keepdims=True)
            - norm * jnp.mean(scaled * norm, axis=-1, keepdims=True)
        ) * scale
        unit[row : row + ROWS] = grad
        leave(unit, grad_summed_far, doc, start, row)
        low = grad.astype(BF16)
        grad_second[row : row + ROWS] = low
        sums[5] += column_sum(low)
        grad_mix[row : row + ROWS] = nt(low, wpo[...]).astype(BF16)
        leave(grad_mix, grad_mix_far, doc, start, row)
    for index, value in enumerate(sums):
        vec[index : index + 1] = value
    vec[6:8] = jnp.zeros((2, width), F32)
    for copy in leaving:
        copy.wait()


def feed(place, summed, cotangent, we, be, wr, br, ng, ns, fg, fs, wpo):
    docs, rows, width = summed.shape
    wide = we.shape[1]
    tokens = docs * rows
    return call(
        feed_body,
        (1,),
        (place,),
        [whole(a) for a in (summed, cotangent, we, be, wr, br, ng, ns, fg, fs, wpo)],
        [
            out_raw((docs, rows, width), BF16),
            out_whole((tokens, width), BF16),
            out_whole((tokens, wide), BF16),
            out_whole((tokens, width), BF16),
            out_whole((tokens, wide), BF16),
            out_raw((docs, rows, width), F32),
            out_whole((tokens, width), BF16),
            out_raw((docs, rows, width), BF16),
            out_whole((8, width), F32),
            out_whole((1, wide), F32),
        ],
        [
            pltpu.VMEM((tokens, width), F32),
            pltpu.VMEM((tokens, wide), F32),
            pltpu.VMEM((tokens, width), F32),
            pltpu.VMEM((tokens, width), F32),
            pltpu.VMEM((tokens, width), BF16),
            pltpu.VMEM((tokens, width), BF16),
            pltpu.SemaphoreType.DMA((3 * tokens // ROWS,)),
        ],
        spare=12,
    )


def key_value_body(place, *refs, docs):
    gk_kept, gk_came, gv_kept, gv_came, kx, vx, ck, cv = refs[:8]
    own, from_left, from_right, dq = refs[8:12]
    gk, gv, vec, rows_in, pooled, total = refs[12:]
    offset = place[0]
    rows, width = gk.shape[0] // docs, gk.shape[1]
    count = rows // STRIDE
    vec[...] = jnp.zeros_like(vec)
    for doc in range(docs):
        length = place[1 + doc]
        spot = offset - HALF + positions((rows + WIN, 1), 0)
        valid = (spot >= 0) & (spot < length)
        first = doc * rows
        for which, (kept, came, ext, taps, out, row) in enumerate(
            (
                (gk_kept, gk_came, kx, ck, gk, 0),
                (gv_kept, gv_came, vx, cv, gv, KER),
            )
        ):
            pooled[...] = kept[doc].astype(F32) + came[doc].astype(F32)
            masked = jnp.where(valid, ext[doc].astype(F32), 0.0)
            for group in range(width // LANES):
                lanes = slice(group * LANES, (group + 1) * LANES)
                grown = pooled[:count, lanes]
                shifted = pooled[1 : count + 1, lanes]
                rows_in[group] = masked[:, lanes]
                for tap in range(KER):
                    start = HALF - KER // 2 + tap
                    read = rows_in[group, pl.ds(start, count, stride=STRIDE), :]
                    vec[row + tap : row + tap + 1, lanes] += column_sum(grown * read)
                if which == 1:
                    vec[2 * KER : 2 * KER + 1, lanes] += column_sum(grown)
                total[group] = own[doc, which, :, lanes]
                total[group, :HALF] += from_left[doc, which, :, lanes].astype(F32)
                total[group, rows - HALF :] += from_right[doc, which, :, lanes].astype(F32)
                for phase, terms in enumerate(
                    (
                        ((2, grown),),
                        ((3, grown),),
                        ((4, grown), (0, shifted)),
                        ((1, shifted),),
                    )
                ):
                    part = pl.ds(phase, count, stride=STRIDE)
                    added = None
                    for tap, values in terms:
                        term = values * taps[tap : tap + 1, lanes]
                        added = term if added is None else added + term
                    inside = offset + phase + STRIDE * positions((count, 1), 0) < length
                    total[group, part, :] = total[group, part, :] + jnp.where(inside, added, 0.0)
                out[first : first + rows, lanes] = total[group].astype(BF16)
        vec[11:12] += column_sum(dq[doc])
    vec[12:13] += column_sum(gv[...])


def key_value_gradients(place, pooled_grads, kx, vx, ck, cv, own, left, right, dq):
    docs, rows, width = dq.shape
    return call(
        functools.partial(key_value_body, docs=docs),
        (1,),
        (place,),
        [
            whole(a)
            for a in (*pooled_grads, kx, vx, ck, cv, own, left, right, dq)
        ],
        [out_whole((docs * rows, width), BF16)] * 2 + [out_whole((16, width), F32)],
        [
            pltpu.VMEM((width // LANES, rows + WIN, LANES), F32),
            pltpu.VMEM((rows // STRIDE + 8, width), F32),
            pltpu.VMEM((width // LANES, rows, LANES), F32),
        ],
    )


def input_body(place, dq, gk, gv, gmid, wq, wk, wv, dx):
    total = nt(dq[...], wq[...]) + nt(gk[...], wk[...]) + nt(gv[...], wv[...])
    dx[...] = (gmid[...] + total.reshape(gmid.shape)).astype(BF16)


def input_gradient(place, dq, gk, gv, gmid, wq, wk, wv):
    docs, rows, width = gmid.shape
    (dx,) = call(
        input_body,
        (1,),
        (place,),
        [whole(a) for a in (dq, gk, gv, gmid, wq, wk, wv)],
        [out_whole((docs, rows, width), BF16)],
    )
    return dx


def scatter_body(bits, *refs, kinds, order, vectors, quartered):
    count = len(kinds)
    operands = [refs[2 * index : 2 * index + 2] for index in range(count)]
    extra = refs[2 * count : 2 * count + vectors]
    rest = refs[2 * count + vectors :]
    if quartered:
        results, (ordered, rounded, *small) = (rest[0], rest[0]), rest[1:]
    else:
        results, (ordered, rounded, *small) = rest[:2], rest[2:]
    core = bits[0]
    sides = 2 if ("batch", 1) in order else 1
    owners = 8

    def start_of(which, size):
        if quartered:
            return which * size
        return pl.multiple_of((which ^ core) * size, LANES)

    def place_tile(which, side, owner, target, size, value):
        index = []
        for at, (axis, bit) in enumerate(order):
            if axis == "batch":
                index += [side, which] if quartered else [side ^ bits[1 + at]]
            else:
                index.append(((owner >> bit) & 1) ^ bits[1 + at])
        results[which][(*index, slice(target, target + size), slice(None))] = value

    base = 0
    for (left, right), kind in zip(operands, kinds):
        tall = left.shape[1]
        turned = left[...].T
        if kind == "wide":
            half = right.shape[1] // 2
            size = tall // owners // sides
            for which in range(2):
                start = start_of(which, half)
                for part in range(half // 768):
                    rounded[...] = nn(turned, right[:, pl.ds(start + part * 768, 768)]).astype(BF16)
                    for column in range(2):
                        target = base + (2 * part + column) * size
                        for owner in range(owners):
                            for side in range(sides):
                                row = (owner * sides + side) * size
                                value = rounded[row : row + size, column * 384 : column * 384 + 384]
                                place_tile(which, side, owner, target, size, value)
            base += half // 384 * size
        elif kind == "tall":
            ordered[...] = turned
            size = tall // 2 // sides
            for part in range(right.shape[1] // 768):
                product = nn(ordered[...], right[:, part * 768 : part * 768 + 768])
                rounded[...] = product.astype(BF16)
                for column in range(2):
                    owner = 2 * part + column
                    for side in range(sides):
                        for which in range(2):
                            row = start_of(which, 384) + side * size
                            value = rounded[pl.ds(row, size), column * 384 : column * 384 + 384]
                            place_tile(which, side, owner, base, size, value)
            base += size
        else:
            size = tall // owners // sides
            if quartered:
                columns = right[...]
            else:
                columns = jnp.concatenate(
                    [right[:, pl.ds(start_of(which, 384), 384)] for which in range(2)], axis=1
                )
            rounded[...] = nn(turned, columns).astype(BF16)
            for which in range(2):
                for owner in range(owners):
                    for side in range(sides):
                        row = (owner * sides + side) * size
                        value = rounded[row : row + size, which * 384 : which * 384 + 384]
                        place_tile(which, side, owner, base, size, value)
            base += size
    if vectors:
        (block,) = small
        vec_feed, vec_first, vec_input, vec_wide = extra
        for owner in range(owners):
            lanes = slice(owner * 96, owner * 96 + 96)
            block[0, owner] = jnp.zeros(block.shape[2:], F32)
            block[1, owner] = jnp.zeros(block.shape[2:], F32)
            block[0, owner, 0:8, 0:96] = vec_feed[:, lanes]
            block[0, owner, 0:8, LANES : LANES + 96] = vec_first[:, lanes]
            block[1, owner, 0:16, 0:96] = vec_input[:, lanes]
            for part in range(4):
                at = owner * 384 + part * 96
                block[0, owner, 8 + part : 9 + part, 0:96] = vec_wide[:, at : at + 96]
        for owner in range(owners):
            for which in range(2):
                place_tile(which, 0, owner, base, 16, block[which ^ core, owner].astype(BF16))


def scatter_products(bits, order, items, extra=(), quartered=False):
    sides = 2 if ("batch", 1) in order else 1
    rows = 0
    for kind, left, right in items:
        if kind == "wide":
            rows += right.shape[1] // 768 * (left.shape[1] // 8 // sides)
        elif kind == "tall":
            rows += 384 // sides
        else:
            rows += 96 // sides
    rows += 16 if extra else 0
    shape = (2,) * (len(order) + quartered) + (rows, 384)
    operands = [array for _, left, right in items for array in (left, right)]
    return call(
        functools.partial(
            scatter_body,
            kinds=tuple(kind for kind, _, _ in items),
            order=tuple(order),
            vectors=len(extra),
            quartered=quartered,
        ),
        (1,),
        (bits,),
        [whole(a) for a in (*operands, *extra)],
        [out_whole(shape, BF16)] * (1 if quartered else 2),
        [pltpu.VMEM((768, operands[0].shape[0]), BF16), pltpu.VMEM((768, 768), BF16)]
        + ([pltpu.VMEM((2, 8, 16, 384), F32)] if extra else []),
    )


def quarter_products_body(bits, *refs, kinds, levels):
    count = len(kinds)
    operands = [refs[2 * index : 2 * index + 2] for index in range(count)]
    out, turned, by_owner, by_half, sems = refs[2 * count :]
    sides, cores, owners = 2, 2, 1 << levels
    pending = {}
    turns = {}

    def digits(owner):
        return tuple(((owner >> level) & 1) ^ bits[level] for level in range(levels))

    def next_slot(buffer):
        slot = turns.get(buffer, 0) % 2
        turns[buffer] = turns.get(buffer, 0) + 1
        for copy in pending.pop((buffer, slot), []):
            copy.wait()
        return slot

    def leave(buffer, slot, source, target):
        copies = pending.setdefault((buffer, slot), [])
        copy = pltpu.make_async_copy(source, target, sems.at[buffer, slot, len(copies)])
        copy.start()
        copies.append(copy)

    def spread_rows(value):
        slot = next_slot(0)
        size = 768 // owners // sides
        for owner in range(owners):
            for side in range(sides):
                row = (owner * sides + side) * size
                for column in range(2):
                    part = value[row : row + size, column * 384 : column * 384 + 384]
                    by_owner[(slot, column, side, *digits(owner))] = part
        return slot

    def leave_rows(slot, column, which, base):
        middle = (slice(None),) * levels
        leave(0, slot, by_owner.at[slot, column], out.at[(slice(None), which, *middle, pl.ds(base, 48))])

    base = 0
    for (left, right), kind in zip(operands, kinds):
        turned[...] = left[...].T
        if kind == "wide":
            for which in range(cores):
                for part in range(2):
                    start = which * 1536 + part * 768
                    value = nn(turned[...], right[:, start : start + 768]).astype(BF16)
                    slot = spread_rows(value)
                    for column in range(2):
                        leave_rows(slot, column, which, base + (2 * part + column) * 48)
            base += 192
        elif kind == "tall":
            for part in range(4):
                value = nn(turned[...], right[:, part * 768 : part * 768 + 768]).astype(BF16)
                slot = next_slot(1)
                for which in range(cores):
                    for side in range(sides):
                        row = (which * sides + side) * 192
                        for column in range(2):
                            part_value = value[row : row + 192, column * 384 : column * 384 + 384]
                            by_half[slot, column, side, which] = part_value
                for column in range(2):
                    owner = digits(2 * part + column)
                    target = out.at[(slice(None), slice(None), *owner, pl.ds(base, 192))]
                    leave(1, slot, by_half.at[slot, column], target)
            base += 192
        else:
            slot = spread_rows(nn(turned[...], right[...]).astype(BF16))
            for which in range(cores):
                leave_rows(slot, which, which, base)
            base += 48
    for copies in pending.values():
        for copy in copies:
            copy.wait()


def quarter_products(bits, items, levels):
    rows = sum(48 if kind == "square" else 192 for kind, _, _ in items)
    operands = [array for _, left, right in items for array in (left, right)]
    (out,) = call(
        functools.partial(
            quarter_products_body, kinds=tuple(kind for kind, _, _ in items), levels=levels
        ),
        (1,),
        (bits,),
        [whole(a) for a in operands],
        [out_raw((2, 2) + (2,) * levels + (rows, 384), BF16)],
        [
            pltpu.VMEM((768, operands[0].shape[0]), BF16),
            pltpu.VMEM((2, 2, 2) + (2,) * levels + (48, 384), BF16),
            pltpu.VMEM((2, 2, 2, 2, 192, 384), BF16),
            pltpu.SemaphoreType.DMA((2, 2, 2)),
        ],
    )
    return out


def order_quarters(spots, low, other, across, quarters):
    odd, upper = spots[0], spots[1]
    quarters[odd, upper] = low[...]
    quarters[odd, 1 - upper] = other[...]
    quarters[1 - odd, upper] = across[0]
    quarters[1 - odd, 1 - upper] = across[1]


def order_parts(spots, parts, quarters):
    odd, upper = spots[0], spots[1]
    for flip, part in enumerate(parts):
        quarters[odd ^ (flip & 1), upper ^ (flip >> 1)] = part[...]


def join_square(quarters, start, out):
    for core in range(2):
        for side in range(2):
            block = quarters[core, side, start : start + 48]
            out[side * 48 : side * 48 + 48, core * 384 : core * 384 + 384] = block.astype(F32)


def collect_feed_body(spots, low, other, across, expand, reduce, pooled_out, quarters, tall):
    order_quarters(spots, low, other, across, quarters)
    for core in range(2):
        for side in range(2):
            rows = slice(side * 48, side * 48 + 48)
            for part in range(4):
                column = core * 1536 + part * 384
                block = quarters[core, side, part * 48 : part * 48 + 48]
                expand[rows, column : column + 384] = block.astype(F32)
            at = core * 384 + side * 192
            tall[at : at + 192] = quarters[core, side, 192:384].astype(F32)
    reduce[...] = tall[...].T
    join_square(quarters, 384, pooled_out)


def collect_feed(spots, low, other, across):
    return call(
        collect_feed_body,
        (1,),
        (spots,),
        [whole(low), whole(other), whole(across)],
        [out_whole((96, 3072), F32), out_whole((384, 768), F32), out_whole((96, 768), F32)],
        [pltpu.VMEM((2, 2) + low.shape, BF16), pltpu.VMEM((768, 384), F32)],
    )


def collect_last_body(spots, *refs, cut):
    pq, lo, lq, lk, lv, vectors, quarters = refs[4:]
    order_parts(spots, refs[:4], quarters)
    for index, out in enumerate((pq, lo, lq)):
        join_square(quarters, index * 48, out)
    for core in range(2):
        half = quarters[core, 0, cut:].astype(F32) + quarters[core, 1, cut:].astype(F32)
        lk[:, core * 384 : core * 384 + 384] = half[:96]
        lv[:, core * 384 : core * 384 + 384] = half[96:192]
        vectors[core] = half[192:208]


def collect_last(spots, parts, cut):
    return call(
        functools.partial(collect_last_body, cut=cut),
        (1,),
        (spots,),
        [whole(part) for part in parts],
        [out_whole((96, 768), F32)] * 5 + [out_whole((2, 16, 384), F32)],
        [pltpu.VMEM((2, 2) + parts[0].shape, BF16)],
    )


def swap(value, axis, bit):
    count = lax.axis_size(axis)
    return lax.ppermute(value, axis, [(i, i ^ (1 << bit)) for i in range(count)])


def shift(value, axis, by):
    count = lax.axis_size(axis)
    pairs = [(i, i + by) for i in range(count) if 0 <= i + by < count]
    return lax.ppermute(value, axis, pairs)


def fold(kept, came):
    low = (kept[1].astype(F32) + came[1].astype(F32)).astype(BF16)
    return low, kept[0].astype(F32) + came[0].astype(F32)


def total_of(terms, *index):
    total = None
    for term in terms:
        value = term[index].astype(F32)
        total = value if total is None else total + value
    return total


def advance(terms, hop):
    came = swap(total_of(terms, 1).astype(BF16), *hop)
    return [term[0] for term in terms], came


def cut(quarters, start, size):
    return quarters[:, :, start : start + size]


def device_step(
    inputs, lengths, cotangent,
    local_query, local_query_bias, local_key, local_value, local_value_bias,
    local_output, local_output_bias, pooled_query, pooled_query_bias,
    pooled_output, pooled_output_bias, conv_key, conv_value, conv_value_bias,
    norm_gain, norm_shift, expand_weight, expand_bias, reduce_weight, reduce_bias,
    final_gain, final_shift,
):
    docs, rows, width = inputs.shape
    devices = lax.axis_size("seq")
    me = lax.axis_index("seq")
    mine = lax.axis_index("batch")
    levels = devices.bit_length() - 1
    size = rows // STRIDE
    flat = docs * rows
    offset = me * rows
    reach = -(-REACH // size)
    gathered = devices <= 2 * reach
    fast = devices == 8 and width == 768 and lax.axis_size("batch") == 4
    base = jnp.where(gathered, 0, offset // STRIDE - reach * size)
    place = jnp.concatenate([offset[None], lengths, base[None]]).astype(jnp.int32)

    def line(vector):
        return vector[None]

    def tokens(array):
        return array.reshape(flat, array.shape[-1])

    taps_key, taps_value = conv_key.T, conv_value.T

    left = shift(inputs[:, rows - HALF :], "seq", 1)
    right = shift(inputs[:, :HALF], "seq", -1)
    q, k_own, v_own, key_near, value_near = project(
        place, inputs, local_query, line(local_query_bias), local_key, local_value,
        line(local_value_bias),
    )
    left, right, k_own = sync(left, right, k_own)
    kx, vx, pooled = pool(
        place, left, right, k_own, v_own, key_near, value_near, line(local_value_bias),
        taps_key, taps_value, line(conv_value_bias),
    )
    own = [pooled[which][None] for which in range(2)]

    mixes, probs_one = [], []

    def local_step(doc, token):
        mix, probs = local_forward(token, q, kx, vx, doc)
        mixes.append(mix)
        probs_one.append(probs)
        return mix

    if gathered:
        orders = ([2, 1, 0], [0, 2, 1]) if levels == 3 else (list(range(levels)),) * 2
        have = own
        pieces = [[own[0]], [own[1]]]
        relative = [[0], [0]]
        token = place
        for stage in range(levels):
            came = [swap(have[which], "seq", orders[which][stage]) for which in range(2)]
            if stage == 0:
                came[0], came[1], token = sync(came[0], came[1], token)
            if 0 < stage <= docs:
                done = local_step(stage - 1, token)
            if stage == levels - 1:
                while len(mixes) < docs:
                    local_step(len(mixes), token)
                mix_one, middle, middle_low, q2 = middle_forward(
                    token, inputs, local_output, line(local_output_bias), pooled_query,
                    line(pooled_query_bias), mixes,
                )
                came[0], came[1], q2, token = sync(came[0], came[1], q2, token)
            elif stage > 0:
                came[0], came[1], mixes[stage - 1], token = sync(
                    came[0], came[1], done, token
                )
            for which in range(2):
                pieces[which].append(came[which])
                relative[which] += [r ^ (1 << orders[which][stage]) for r in relative[which]]
                if stage < levels - 1:
                    have[which] = jnp.concatenate([have[which], came[which]])
        slots = jnp.stack([me ^ jnp.array(r, jnp.int32) for r in relative])
    else:
        pieces = [
            [own[which]]
            + [
                shift(own[which], "seq", sign * distance)
                for distance in range(1, reach + 1)
                for sign in (1, -1)
            ]
            for which in range(2)
        ]
        spots = [reach] + [
            reach - sign * distance for distance in range(1, reach + 1) for sign in (1, -1)
        ]
        slots = jnp.array([spots, spots], jnp.int32)
        token = place
        for doc in range(docs):
            local_step(doc, token)
        mix_one, middle, middle_low, q2 = middle_forward(
            token, inputs, local_output, line(local_output_bias), pooled_query,
            line(pooled_query_bias), mixes,
        )

    keys, values, probs_two, mix_two, summed, expand_near, reduce_near = pooled_forward(
        token, slots, pieces[0], pieces[1], q2, middle, pooled_output, line(pooled_output_bias),
        expand_weight, reduce_weight,
    )
    (
        outputs, normed_low, hidden, grad_branch, grad_pre, grad_summed, grad_second, grad_mix_two,
        vec_feed, vec_wide,
    ) = feed(
        token, summed, cotangent, expand_near, line(expand_bias), reduce_near,
        line(reduce_bias), line(norm_gain), line(norm_shift), line(final_gain),
        line(final_shift), pooled_output,
    )

    order_first = [("batch", 1)] + [("seq", level) for level in range(levels)]
    order_last = order_first[1:]

    def bits_of(order):
        ids = [mine & 1] + [(mine if axis == "batch" else me) >> bit & 1 for axis, bit in order]
        return jnp.stack(ids).astype(jnp.int32)

    seq_bits = jnp.stack([me >> level & 1 for level in range(levels)]).astype(jnp.int32)

    def over_batch(blocks):
        part = blocks.shape[2:]
        flat_blocks = blocks.reshape(-1, blocks.shape[-1])
        mine_part = lax.psum_scatter(flat_blocks, "batch", scatter_dimension=0, tiled=True)
        return mine_part.reshape(part)

    if fast:
        feed_blocks = quarter_products(
            seq_bits,
            [
                ("wide", normed_low, grad_pre),
                ("tall", grad_branch, hidden),
                ("square", tokens(mix_two), grad_second),
            ],
            levels,
        )
        feed_blocks, grad_mix_two, token = sync(feed_blocks, grad_mix_two, token)
        feed_part = over_batch(feed_blocks)

    blocks = devices if gathered else 2 * reach + 1
    if gathered:
        back = ([0, 1, 2], [1, 2, 0]) if levels == 3 else (list(range(levels)),) * 2
        places = []
        for which in range(2):
            spots = []
            for block in range(devices):
                relative = 0
                for at, bit in enumerate(back[which]):
                    relative |= (block >> (levels - 1 - at) & 1) << bit
                spots.append(relative)
            places.append(me ^ jnp.array(spots, jnp.int32))
        places = jnp.stack(places)
        half_blocks = devices // 2
    else:
        middle_first = [reach] + [spot for spot in range(blocks) if spot != reach]
        places = jnp.array([middle_first, middle_first], jnp.int32)
        half_blocks = 1
    grad_q2, dk_kept, dk_sent, dv_kept, dv_sent = pooled_backward(
        places, token, q2, keys, values, probs_two, grad_mix_two, size, half_blocks
    )
    grad_middle, grad_first, grad_mix_one, vec_first = first_backward(
        token, grad_q2, grad_summed, pooled_query, local_output
    )
    back_parts = ()

    def back_step(doc, token):
        return local_backward(
            token, q, kx, vx, grad_mix_one, probs_one[doc], doc, back_parts
        )

    if gathered:
        kept = [part.reshape((2,) * (levels - 1) + part.shape[1:]) for part in (dk_kept, dv_kept)]
        sent = [part.reshape((2,) * (levels - 1) + part.shape[1:]) for part in (dk_sent, dv_sent)]
        for stage in range(levels):
            came = [swap(sent[which], "seq", back[which][stage]) for which in range(2)]
            if stage < docs:
                back_parts = list(back_step(stage, token))
            if fast and stage == 0:
                came[0], came[1], back_parts[0], token = sync(
                    came[0], came[1], back_parts[0], token
                )
            if fast and stage == 1:
                came[0], came[1], back_parts[2], back_parts[3], token = sync(
                    came[0], came[1], back_parts[2], back_parts[3], token
                )
            if fast and stage == 2:
                middle_kept, middle_sent = scatter_products(
                    bits_of(order_first) + 0 * token[0],
                    order_first,
                    [
                        ("square", tokens(middle_low), tokens(grad_q2)),
                        ("square", tokens(mix_one), grad_first),
                        ("square", tokens(inputs), tokens(back_parts[0])),
                    ],
                )
                from_left = shift(back_parts[3], "seq", 1)
                from_right = shift(back_parts[2], "seq", -1)
                came[0], came[1], from_left, from_right, middle_sent, token = sync(
                    came[0], came[1], from_left, from_right, middle_sent, token
                )
            if stage < levels - 1:
                for which in range(2):
                    sent[which], kept[which] = fold(kept[which], came[which])
        pooled_grads = [kept[0], came[0], kept[1], came[1]]
    else:
        pooled_grads = []
        for kept, sent in ((dk_kept, dk_sent), (dv_kept, dv_sent)):
            total = kept[0]
            for distance in range(1, reach + 1):
                total = total + shift(sent[reach - distance], "seq", -distance).astype(F32)
                total = total + shift(sent[reach + distance - 1], "seq", distance).astype(F32)
            after = shift(total[:, :1].astype(BF16), "seq", -1).astype(F32)
            total = jnp.concatenate([total[:, :size], jnp.tile(after, (1, 8, 1))], axis=1)
            pooled_grads += [total, jnp.zeros_like(total)]
        for doc in range(docs):
            back_parts = back_step(doc, token)
    if not fast:
        from_left = shift(back_parts[3], "seq", 1)
        from_right = shift(back_parts[2], "seq", -1)
    dq, own_grads = back_parts[:2]
    if fast:
        middle_came = swap(middle_sent, "batch", 0)
    grad_k, grad_v, vec_input = key_value_gradients(
        token, pooled_grads, kx, vx, taps_key, taps_value,
        own_grads, from_left, from_right, dq,
    )
    if fast:
        last_kept, last_sent = scatter_products(
            bits_of(order_last),
            order_last,
            [("square", tokens(inputs), grad_k), ("square", tokens(inputs), grad_v)],
            (vec_feed, vec_first, vec_input, vec_wide),
        )
        last_sent, middle_came, token = sync(last_sent, middle_came, token)
        last_came = swap(last_sent, "batch", 0)
        middle_terms, middle_came = advance([middle_kept, middle_came], ("batch", 1))
    input_grad = input_gradient(
        token, tokens(dq), grad_k, grad_v, grad_middle, local_query, local_key, local_value
    )

    if fast:
        cut_feed = 240
        one = [feed_part[..., :cut_feed, :]]
        two = [feed_part[..., cut_feed:, :]]

        def advance_second(terms, hop):
            came = swap(total_of(terms, slice(None), 1).astype(BF16), *hop)
            return [term[:, 0] for term in terms], came

        one, one_came = advance(one, ("seq", 0))
        two, two_came = advance_second(two, ("seq", 1))
        input_grad, last_came, middle_came, one_came, two_came = sync(
            input_grad, last_came, middle_came, one_came, two_came
        )
        last_terms, last_came = advance([last_kept, last_came], ("seq", 0))
        middle_terms, middle_came = advance_second(middle_terms + [middle_came], ("seq", 1))
        one, one_came = advance(one + [one_came], ("seq", 1))
        two, two_came = advance(two + [two_came], ("seq", 0))
        last_came, middle_came, one_came, two_came = sync(
            last_came, middle_came, one_came, two_came
        )

        last_terms, last_came = advance(last_terms + [last_came], ("seq", 1))
        one, two = one + [one_came], two + [two_came]
        feed_came = swap(
            jnp.concatenate([total_of(one, 1), total_of(two, 1)]).astype(BF16), "seq", 2
        )
        middle_terms, middle_came = advance(middle_terms + [middle_came], ("seq", 0))
        last_came, middle_came, feed_came = sync(last_came, middle_came, feed_came)

        last_terms, last_came = advance(last_terms + [last_came], ("seq", 2))
        middle_terms, middle_came = advance(middle_terms + [middle_came], ("seq", 2))
        feed_low = (
            jnp.concatenate([total_of(one, 0), total_of(two, 0)]) + feed_came.astype(F32)
        ).astype(BF16)
        feed_other = swap(feed_low, "batch", 1)
        last_came, middle_came, feed_other = sync(last_came, middle_came, feed_other)
        cut_at = middle_came.shape[0]
        low = jnp.concatenate(
            [
                total_of(middle_terms + [middle_came], Ellipsis),
                total_of(last_terms + [last_came], Ellipsis),
            ]
        ).astype(BF16)
        parts = [low] + [
            lax.ppermute(low, "batch", [(each, each ^ flip) for each in range(4)])
            for flip in range(1, 4)
        ]
        feed_across = swap(jnp.stack([feed_low, feed_other]), "batch", 0)
        spots = jnp.stack([mine & 1, mine >> 1]).astype(jnp.int32)
        grad_expand, grad_reduce, grad_po = collect_feed(spots, feed_low, feed_other, feed_across)
        *others, grad_expand, grad_reduce, grad_po = sync(
            *parts[1:], grad_expand, grad_reduce, grad_po
        )
        parts = parts[:1] + others
        grad_pq, grad_lo, grad_lq, grad_lk, grad_lv, lines = collect_last(
            spots, parts, cut_at
        )
        vec_low, vec_high = lines[0, :, :96], lines[1, :, :96]
        (fg, fs, rb, ng, ns, pob) = [vec_low[index] for index in range(6)]
        pqb, lob = lines[0, 0, LANES : LANES + 96], lines[0, 1, LANES : LANES + 96]
        grad_eb = vec_low[8:12].reshape(-1)
    else:

        def plain(left_array, right_array):
            product = tn(left_array, right_array)
            part = lax.psum_scatter(product, "seq", scatter_dimension=0, tiled=True)
            return lax.psum(part.astype(BF16), "batch").astype(F32)

        grad_expand = plain(normed_low, grad_pre)
        grad_reduce = plain(hidden, grad_branch)
        grad_po = plain(tokens(mix_two), grad_second)
        grad_pq = plain(tokens(middle_low), tokens(grad_q2))
        grad_lo = plain(tokens(mix_one), grad_first)
        grad_lq = plain(tokens(inputs), tokens(dq))
        grad_lk = plain(tokens(inputs), grad_k)
        grad_lv = plain(tokens(inputs), grad_v)
        vectors = jnp.concatenate(
            [vec_feed, vec_first, vec_input, vec_wide.reshape(-1, width)], axis=0
        )
        vectors = lax.psum(vectors, ("seq", "batch"))
        share = width // devices
        part = lax.dynamic_slice_in_dim(vectors, me * share, share, axis=1)
        wide = vectors[32:].reshape(-1)
        wide_share = wide.shape[0] // devices
        grad_eb = lax.dynamic_slice_in_dim(wide, me * wide_share, wide_share, axis=0)
        (fg, fs, rb, ng, ns, pob) = [part[index] for index in range(6)]
        pqb, lob = part[8], part[9]
        vec_high = part[16:32]
    grad_ck = vec_high[:KER].T
    grad_cv = vec_high[KER : 2 * KER].T
    cvb, lqb, lvb = vec_high[10], vec_high[11], vec_high[12]
    return (
        outputs, input_grad,
        grad_lq, lqb, grad_lk, grad_lv, lvb, grad_lo, lob, grad_pq, pqb, grad_po, pob,
        grad_ck, grad_cv, cvb, ng, ns, grad_expand, grad_eb, grad_reduce, rb, fg, fs,
    )


def solution(mesh):
    vector = P("seq")
    matrix = P("seq", None)
    return jax.shard_map(
        device_step,
        mesh=mesh,
        in_specs=(P("batch", "seq", None), P("batch"), P("batch", "seq", None)) + (P(),) * 22,
        out_specs=(
            P("batch", "seq", None), P("batch", "seq", None),
            matrix, vector, matrix, matrix, vector, matrix, vector, matrix, vector, matrix, vector,
            matrix, matrix, vector, vector, vector, matrix, vector, matrix, vector, vector, vector,
        ),
        check_vma=False,
    )
```

```python
import functools
import math

import jax
import jax.numpy as jnp
from jax import lax
from jax.experimental import pallas as pl
from jax.experimental.pallas import tpu as pltpu
from jax.sharding import PartitionSpec as P

HEADS = 12
HD = 64
WIN = 128
PWIN = 512
KER = 5
STRIDE = 4
HALF = WIN // 2
REACH = PWIN // 2
NEGATIVE = -1e30
SCALE = 1.0 / math.sqrt(HD)
EPSILON = 1e-05
LANES = 128
TILE = 128
ROWS = 128
CHUNK = 768
PAIRS = 3
F32 = jnp.float32
BF16 = jnp.bfloat16


def nn(left, right):
    return jnp.dot(left, right, preferred_element_type=F32)


def nt(left, right):
    return lax.dot_general(left, right, (((1,), (1,)), ((), ())), preferred_element_type=F32)


def tn(left, right):
    return lax.dot_general(left, right, (((0,), (0,)), ((), ())), preferred_element_type=F32)


def column_sum(block):
    return jnp.sum(block.astype(F32), axis=0, keepdims=True)


def call(body, grid, scalars, inputs, outputs, scratch=(), spare=8):
    used = spare * 2**20
    arrays, in_specs, out_specs, shapes = [], [], [], []

    def spec(shape, dtype, block, index):
        nonlocal used
        if block is None:
            return pl.BlockSpec(memory_space=pltpu.VMEM)
        if block == "raw":
            return pl.BlockSpec(memory_space=pl.ANY)
        used += 2 * math.prod(block) * jnp.dtype(dtype).itemsize
        return pl.BlockSpec(block, index)

    for array, block, index in inputs:
        in_specs.append(spec(array.shape, array.dtype, block, index))
        if block is not None:
            array = pltpu.with_memory_space_constraint(array, pltpu.HBM)
        arrays.append(array)
    for shape, dtype, block, index in outputs:
        out_specs.append(spec(shape, dtype, block, index))
        plain = block is None
        shapes.append((jax.ShapeDtypeStruct if plain else pltpu.HBM)(shape, dtype))
    for item in scratch:
        if hasattr(item, "shape") and item.memory_space == pltpu.VMEM:
            used += math.prod(item.shape) * jnp.dtype(item.dtype).itemsize
    return pl.pallas_call(
        body,
        grid_spec=pltpu.PrefetchScalarGridSpec(
            num_scalar_prefetch=len(scalars),
            grid=grid,
            in_specs=in_specs,
            out_specs=out_specs,
            scratch_shapes=list(scratch),
        ),
        out_shape=shapes,
        compiler_params=pltpu.CompilerParams(
            dimension_semantics=("arbitrary",) * len(grid), vmem_limit_bytes=used
        ),
        cost_estimate=pl.CostEstimate(flops=1000, bytes_accessed=1000, transcendentals=0),
    )(*scalars, *arrays)


def raw(array):
    return (array, "raw", None)


def out_raw(shape, dtype):
    return (shape, dtype, "raw", None)


def whole(array):
    return (array, None, None)


def out_whole(shape, dtype):
    return (shape, dtype, None, None)


def sync(*values):
    return lax.optimization_barrier(values)


def stack_heads(block):
    lane = lax.broadcasted_iota(jnp.int32, block.shape, 1)
    zero = jnp.zeros_like(block)
    return jnp.concatenate(
        [jnp.where(lane < HD, block, zero), jnp.where(lane < HD, zero, block)], axis=0
    )


def unstack(block):
    half = block.shape[1] // 2
    joined = jnp.concatenate([block[:HD, :half], block[HD:, half:]], axis=0)
    return joined.T


def positions(shape, dim):
    return lax.broadcasted_iota(jnp.int32, shape, dim)


def project_body(place, x_far, wq_far, bq, wk_far, wv_far, bv, q, k, v, wk, wv, x, wq, sems):
    docs, rows, width = x.shape
    fetches = [
        pltpu.make_async_copy(far, near, sems.at[index])
        for index, (far, near) in enumerate(
            ((x_far, x), (wq_far, wq), (wk_far, wk), (wv_far, wv))
        )
    ]
    for fetch in fetches:
        fetch.start()
    fetches[0].wait()
    flat = x[...].reshape(docs * rows, width)
    fetches[1].wait()
    q[...] = (nn(flat, wq[...]) + bq[...]).astype(BF16).reshape(q.shape)
    fetches[2].wait()
    k[...] = nn(flat, wk[...]).astype(BF16).reshape(k.shape)
    fetches[3].wait()
    v[...] = (nn(flat, wv[...]) + bv[...]).astype(BF16).reshape(v.shape)


def project(place, x, wq, bq, wk, wv, bv):
    return call(
        project_body,
        (1,),
        (place,),
        [raw(x), raw(wq), whole(bq), raw(wk), raw(wv), whole(bv)],
        [out_whole(x.shape, BF16)] * 3 + [out_whole(wk.shape, BF16)] * 2,
        [
            pltpu.VMEM(x.shape, BF16),
            pltpu.VMEM(wq.shape, BF16),
            pltpu.SemaphoreType.DMA((4,)),
        ],
    )


def pool_body(place, left, right, k, v, wk, wv, bv, ck, cv, bcv, kx, vx, pooled, rows):
    offset = place[0]
    docs, own_rows, width = k.shape
    rims = jnp.concatenate(
        [part[doc] for doc in range(docs) for part in (left, right)], axis=0
    )
    size = own_rows + WIN
    count = pooled.shape[2]
    spot = offset - HALF + positions((size, 1), 0)
    for which, (weight, bias, taps, own, out) in enumerate(
        ((wk, None, ck, k, kx), (wv, bv, cv, v, vx))
    ):
        value = nn(rims, weight[...])
        if bias is not None:
            value = value + bias[...]
        value = value.astype(BF16)
        for doc in range(docs):
            at = doc * WIN
            out[doc, :HALF] = value[at : at + HALF]
            out[doc, HALF : HALF + own_rows] = own[doc]
            out[doc, HALF + own_rows :] = value[at + HALF : at + WIN]
            valid = (spot >= 0) & (spot < place[1 + doc])
            for group in range(width // LANES):
                lanes = slice(group * LANES, (group + 1) * LANES)
                rows[group] = jnp.where(valid, out[doc, :, lanes].astype(F32), 0.0)
                total = jnp.zeros((count, LANES), F32)
                for tap in range(KER):
                    start = HALF - KER // 2 + tap
                    read = rows[group, pl.ds(start, count, stride=STRIDE), :]
                    total = total + read * taps[tap : tap + 1, lanes]
                if which == 1:
                    total = total + bcv[:, lanes]
                pooled[which, doc, :, lanes] = total.astype(BF16)


def pool(place, left, right, k, v, wk, wv, bv, ck, cv, bcv):
    docs, rows, width = k.shape
    extended = rows + WIN
    return call(
        pool_body,
        (1,),
        (place,),
        [whole(a) for a in (left, right, k, v, wk, wv, bv, ck, cv, bcv)],
        [
            out_whole((docs, extended, width), BF16),
            out_whole((docs, extended, width), BF16),
            out_whole((2, docs, rows // STRIDE, width), BF16),
        ],
        [pltpu.VMEM((width // LANES, extended, LANES), F32)],
    )


def local_bias(tile, offset, length):
    shape = (TILE + WIN, TILE)
    key = positions(shape, 0)
    query = positions(shape, 1)
    spot = offset + tile * TILE - HALF + key
    allowed = (
        (key >= query) & (key < query + WIN) & (spot >= 0) & (spot < length)
    ) | (key == query + HALF)
    return jnp.where(allowed, 0.0, NEGATIVE)


def softmax_columns(scores):
    top = jnp.max(scores, axis=0, keepdims=True)
    grown = jnp.exp(scores - top)
    return grown * (1.0 / jnp.sum(grown, axis=0, keepdims=True))


def local_forward_body(place, q, kx, vx, mix, probs, *, doc):
    offset, length = place[0], place[1 + doc]
    span = TILE + WIN
    for tile in range(q.shape[1] // TILE):
        half_bias = local_bias(tile, offset, length)
        bias = jnp.concatenate([half_bias, half_bias], axis=1)
        first = tile * TILE
        for pair in range(q.shape[2] // LANES):
            lanes = slice(pair * LANES, (pair + 1) * LANES)
            queries = stack_heads(q[doc, first : first + TILE, lanes]) * SCALE
            scores = nt(kx[doc, first : first + span, lanes], queries) + bias
            chance = softmax_columns(scores)
            probs[pair, tile] = chance
            turned = vx[doc, first : first + span, lanes].T
            mixed = nn(turned, chance.astype(BF16))
            mix[first : first + TILE, lanes] = unstack(mixed).astype(BF16)


def local_forward(place, q, kx, vx, doc):
    _, rows, width = q.shape
    pairs, tiles, span = width // LANES, rows // TILE, TILE + WIN
    return call(
        functools.partial(local_forward_body, doc=doc),
        (1,),
        (place,),
        [whole(a) for a in (q, kx, vx)],
        [
            out_whole((rows, width), BF16),
            out_whole((pairs, tiles, span, 2 * TILE), F32),
        ],
    )


def middle_body(place, x, wo, bo, wpq, bpq, *refs):
    docs, rows = x.shape[0], x.shape[1]
    mixes, (mix, middle, middle_low, q2) = refs[:docs], refs[docs:]
    for doc in range(docs):
        mix[doc] = mixes[doc][...]
    flat = docs * rows
    branch = nn(mix[...].reshape(flat, x.shape[2]), wo[...]) + bo[...]
    total = x[...].reshape(flat, x.shape[2]).astype(F32) + branch
    middle[...] = total.reshape(middle.shape)
    low = total.astype(BF16)
    middle_low[...] = low.reshape(middle_low.shape)
    q2[...] = (nn(low, wpq[...]) + bpq[...]).astype(BF16).reshape(q2.shape)


def middle_forward(place, x, wo, bo, wpq, bpq, mixes):
    docs, rows, width = x.shape
    return call(
        middle_body,
        (1,),
        (place,),
        [whole(a) for a in (x, wo, bo, wpq, bpq, *mixes)],
        [
            out_whole((docs, rows, width), BF16),
            out_whole((docs, rows, width), F32),
            out_whole((docs, rows, width), BF16),
            out_whole((docs, rows, width), BF16),
        ],
    )


def attention_back(keys, values, queries, grads, chance):
    stacked_grads = stack_heads(grads)
    stacked_queries = stack_heads(queries)
    grad_chance = nt(values, stacked_grads * SCALE)
    dots = jnp.sum(chance * grad_chance, axis=0, keepdims=True)
    grad_raw = (chance * (grad_chance - dots)).astype(BF16)
    grad_keys = nn(grad_raw, stacked_queries)
    grad_values = nn(chance.astype(BF16), stacked_grads)
    grad_queries = unstack(nn(keys.T, grad_raw))
    return grad_queries, grad_keys, grad_values


def first_back_body(place, gq2, gsum, wpq, wo, gmid, gfirst, gmix, vec):
    docs, rows, width = gsum.shape
    flat = docs * rows
    grads = gq2[...].reshape(flat, width)
    total = gsum[...].reshape(flat, width) + nt(grads, wpq[...])
    gmid[...] = total.reshape(gmid.shape)
    low = total.astype(BF16)
    gfirst[...] = low
    gmix[...] = nt(low, wo[...]).astype(BF16).reshape(gmix.shape)
    vec[...] = jnp.zeros_like(vec)
    vec[0:1] = column_sum(grads)
    vec[1:2] = column_sum(low)


def first_backward(place, gq2, gsum, wpq, wo):
    docs, rows, width = gsum.shape
    return call(
        first_back_body,
        (1,),
        (place,),
        [whole(a) for a in (gq2, gsum, wpq, wo)],
        [
            out_whole((docs, rows, width), F32),
            out_whole((docs * rows, width), BF16),
            out_whole((docs, rows, width), BF16),
            out_whole((8, width), F32),
        ],
    )


def local_backward_body(place, q, kx, vx, gmix, probs, *refs, doc):
    earlier = refs[: len(refs) - 6]
    dq, own, low_left, low_right, dk, dv = refs[len(refs) - 6 :]
    rows = q.shape[1]
    for old, new in zip(earlier, (dq, own, low_left, low_right)):
        new[:doc] = old[...]
    span = TILE + WIN
    dk[...] = jnp.zeros_like(dk)
    dv[...] = jnp.zeros_like(dv)
    for tile in range(rows // TILE):
        first = tile * TILE
        for pair in range(q.shape[2] // LANES):
            lanes = slice(pair * LANES, (pair + 1) * LANES)
            grad_q, grad_k, grad_v = attention_back(
                kx[doc, first : first + span, lanes],
                vx[doc, first : first + span, lanes],
                q[doc, first : first + TILE, lanes],
                gmix[doc, first : first + TILE, lanes],
                probs[pair, tile],
            )
            dq[doc, first : first + TILE, lanes] = grad_q.astype(BF16)
            dk[first : first + span, lanes] += grad_k
            dv[first : first + span, lanes] += grad_v
    for which, part in enumerate((dk, dv)):
        own[doc, which] = part[HALF : HALF + rows]
        low_left[doc, which] = part[:HALF].astype(BF16)
        low_right[doc, which] = part[HALF + rows :].astype(BF16)


def local_backward(place, q, kx, vx, gmix, probs, doc, earlier=()):
    _, rows, width = q.shape
    span = TILE + WIN
    return call(
        functools.partial(local_backward_body, doc=doc),
        (1,),
        (place,),
        [whole(a) for a in (q, kx, vx, gmix, probs, *earlier)],
        [
            out_whole((doc + 1, rows, width), BF16),
            out_whole((doc + 1, 2, rows, width), F32),
            out_whole((doc + 1, 2, HALF, width), BF16),
            out_whole((doc + 1, 2, HALF, width), BF16),
        ],
        [
            pltpu.VMEM((rows + WIN, width), F32),
            pltpu.VMEM((rows + WIN, width), F32),
        ],
    )


def pooled_forward_body(place, slots, *refs, pieces):
    key_pieces = refs[:pieces]
    value_pieces = refs[pieces : 2 * pieces]
    (
        q2, middle, wpo, bpo, we, wr,
        keys_out, values_out, probs, mix, summed, we_near, wr_near,
        keys, values, bias, sems,
    ) = refs[2 * pieces :]
    doc, pair = pl.program_id(0), pl.program_id(1)
    fetches = [
        pltpu.make_async_copy(we, we_near, sems.at[0]),
        pltpu.make_async_copy(wr, wr_near, sems.at[1]),
    ]
    last = (pair == pl.num_programs(1) - 1) & (doc == pl.num_programs(0) - 1)
    leaves = [
        pltpu.make_async_copy(keys.at[each], keys_out.at[each], sems.at[2 + each])
        for each in range(keys.shape[0])
    ] + [
        pltpu.make_async_copy(
            values.at[each], values_out.at[each], sems.at[2 + keys.shape[0] + each]
        )
        for each in range(keys.shape[0])
    ]

    @pl.when((pair == 0) & (doc == 0))
    def _():
        for fetch in fetches:
            fetch.start()

    offset, length, base = place[0], place[1 + doc], place[1 + pl.num_programs(0)]
    count = keys.shape[1]

    @pl.when(pair == 0)
    def _():
        for where, group, out in ((0, key_pieces, keys), (1, value_pieces, values)):
            at = 0
            for piece in group:
                size = piece.shape[2]
                for block in range(piece.shape[0]):
                    spot = pl.multiple_of(slots[where, at] * size, size)
                    out[doc, pl.ds(spot, size), :] = piece[block, doc]
                    at += 1
        if True:
            shape = (count, q2.shape[1])
            spot = base + positions(shape, 0)
            centre = offset // STRIDE + positions(shape, 1) // STRIDE
            allowed = (
                (spot >= centre - REACH)
                & (spot < centre + REACH)
                & (spot >= 0)
                & (spot * STRIDE < length)
            ) | (spot == centre)
            bias[...] = jnp.where(allowed, 0.0, NEGATIVE)
        for each in range(keys.shape[0]):

            @pl.when(doc == each)
            def _():
                leaves[each].start()
                leaves[keys.shape[0] + each].start()

    for each in range(PAIRS):
        lanes = pl.ds(pl.multiple_of((pair * PAIRS + each) * LANES, LANES), LANES)
        queries = stack_heads(q2[doc, :, lanes]) * SCALE
        half_bias = bias[...]
        scores = nt(keys[doc, :, lanes], queries) + jnp.concatenate([half_bias, half_bias], axis=1)
        chance = softmax_columns(scores)
        probs[0, each] = chance
        mixed = nn(values[doc, :, lanes].T, chance.astype(BF16))
        mix[doc, :, lanes] = unstack(mixed).astype(BF16)

    @pl.when(last)
    def _():
        for copy in fetches + leaves:
            copy.wait()
        flat = (mix.shape[0] * mix.shape[1], mix.shape[2])
        second = nn(mix[...].reshape(flat), wpo[...]) + bpo[...]
        summed[...] = middle[...] + second.reshape(summed.shape)


def pooled_forward(place, slots, key_pieces, value_pieces, q2, middle, wpo, bpo, we, wr):
    docs, rows, width = q2.shape
    pairs, tiles = width // LANES, rows // TILE
    size = key_pieces[0].shape[2]
    count = size * slots.shape[1]

    return call(
        functools.partial(pooled_forward_body, pieces=len(key_pieces)),
        (docs, pairs // PAIRS),
        (place, slots),
        [whole(a) for a in (*key_pieces, *value_pieces, q2, middle, wpo, bpo)]
        + [raw(we), raw(wr)],
        [
            out_raw((docs, count, width), BF16),
            out_raw((docs, count, width), BF16),
            (
                (docs, pairs, count, 2 * rows),
                F32,
                (1, PAIRS, count, 2 * rows),
                lambda doc, pair, *_: (doc, pair, 0, 0),
            ),
            out_whole((docs, rows, width), BF16),
            out_whole((docs, rows, width), F32),
            out_whole(we.shape, BF16),
            out_whole(wr.shape, BF16),
        ],
        [
            pltpu.VMEM((docs, count, width), BF16),
            pltpu.VMEM((docs, count, width), BF16),
            pltpu.VMEM((count, rows), F32),
            pltpu.SemaphoreType.DMA((2 + 2 * docs,)),
        ],
    )


def pooled_backward_body(
    places, token, q2, keys, values, probs, grads, dq, dk_kept, dk_sent, dv_kept, dv_sent, sums
):
    doc, step = pl.program_id(0), pl.program_id(1)
    size = dk_kept.shape[2]
    half = dk_kept.shape[0]
    rows = keys.shape[1]
    for each in range(PAIRS):
        inner = slice(each * LANES, (each + 1) * LANES)
        lanes = pl.ds(pl.multiple_of((step * PAIRS + each) * LANES, LANES), LANES)
        grad_q, *total = attention_back(
            keys[0, :, inner], values[0, :, inner], q2[0, :, inner], grads[0, :, inner],
            probs[0, each],
        )
        dq[doc, :, lanes] = grad_q.astype(BF16)
        for which, (kept, sent) in enumerate(((dk_kept, dk_sent), (dv_kept, dv_sent))):
            sums[each, which, :rows] = total[which]
            sums[each, which, rows:] = jnp.zeros((8, LANES), F32)
            for block in range(half + sent.shape[0]):
                start = pl.multiple_of(places[which, block] * (size - 8), size - 8)
                part = sums[each, which, pl.ds(start, size), :]
                if block < half:
                    kept[block, doc, :, lanes] = part
                else:
                    sent[block - half, doc, :, lanes] = part.astype(BF16)


def pooled_backward(places, token, q2, keys, values, probs, grads, size, kept):
    docs, rows, width = q2.shape
    count = keys.shape[1]
    blocks = count // size
    tiles = rows // TILE

    def lanes_of(array):
        return (array, (1, array.shape[1], PAIRS * LANES), lambda doc, pair, *_: (doc, 0, pair))

    return call(
        pooled_backward_body,
        (docs, width // LANES // PAIRS),
        (places, token),
        [
            lanes_of(q2),
            lanes_of(keys),
            lanes_of(values),
            (
                probs,
                (1, PAIRS, count, 2 * rows),
                lambda doc, pair, *_: (doc, pair, 0, 0),
            ),
            lanes_of(grads),
        ],
        [
            out_whole((docs, rows, width), BF16),
            out_whole((kept, docs, size + 8, width), F32),
            out_whole((blocks - kept, docs, size + 8, width), BF16),
            out_whole((kept, docs, size + 8, width), F32),
            out_whole((blocks - kept, docs, size + 8, width), BF16),
        ],
        [pltpu.VMEM((PAIRS, 2, count + 8, LANES), F32)],
    )


def feed_body(
    place, summed, cotangent, we, be, wr, br, ng, ns, fg, fs, wpo,
    outputs_far, normed_low, hidden, grad_branch, grad_pre, grad_summed_far, grad_second,
    grad_mix_far, vec, vec_wide,
    normed, slope, work, unit, outputs, grad_mix, sems,
):
    docs, rows = cotangent.shape[0], cotangent.shape[1]
    width = summed.shape[2]
    wide = we.shape[1]
    steps = rows // ROWS
    blocks = [
        (doc, step * ROWS, doc * rows + step * ROWS)
        for doc in range(docs)
        for step in range(steps)
    ]
    leaving = []

    def leave(source, target, doc, start, row):
        copy = pltpu.make_async_copy(
            source.at[pl.ds(row, ROWS)],
            target.at[doc, pl.ds(start, ROWS)],
            sems.at[len(leaving)],
        )
        copy.start()
        leaving.append(copy)


    def normal(value):
        centred = value - jnp.mean(value, axis=-1, keepdims=True)
        scale = lax.rsqrt(jnp.mean(centred * centred, axis=-1, keepdims=True) + EPSILON)
        return centred * scale, scale

    scales = []
    for doc, start, row in blocks:
        norm, scale = normal(summed[doc, start : start + ROWS])
        scales.append(scale)
        unit[row : row + ROWS] = norm
        full = norm * ng[...] + ns[...]
        normed[row : row + ROWS] = full
        normed_low[row : row + ROWS] = full.astype(BF16)

    def expand(index):
        part = slice(index * CHUNK, (index + 1) * CHUNK)
        pre = nn(normed_low[...], we[:, part]) + be[:, part]
        cdf = 0.5 * (1.0 + lax.erf(pre * math.sqrt(0.5)))
        hidden[:, part] = (pre * cdf).astype(BF16)
        slope[:, part] = cdf + pre * (jnp.exp(pre * pre * -0.5) * (1.0 / math.sqrt(2.0 * math.pi)))
    for index in range(wide // CHUNK):
        expand(index)

    for start in range(0, width, CHUNK):
        part = slice(start, start + CHUNK)
        work[:, part] = normed[:, part] + (nn(hidden[...], wr[:, part]) + br[:, part])

    sums = [jnp.zeros((1, width), F32) for _ in range(6)]
    for doc, start, row in blocks:
        norm, scale = normal(work[row : row + ROWS])
        spot = place[0] + start + positions((ROWS, 1), 0)
        valid = (spot < place[1 + doc]).astype(F32)
        outputs[row : row + ROWS] = (valid * (norm * fg[...] + fs[...])).astype(BF16)
        leave(outputs, outputs_far, doc, start, row)
        error = valid * cotangent[doc, start : start + ROWS].astype(F32)
        sums[0] += column_sum(error * norm)
        sums[1] += column_sum(error)
        scaled = error * fg[...]
        rest = (
            scaled
            - jnp.mean(scaled, axis=-1, keepdims=True)
            - norm * jnp.mean(scaled * norm, axis=-1, keepdims=True)
        ) * scale
        work[row : row + ROWS] = rest
        low = rest.astype(BF16)
        grad_branch[row : row + ROWS] = low
        sums[2] += column_sum(low)

    def reduce(index):
        part = slice(index * CHUNK, (index + 1) * CHUNK)
        low = (nt(grad_branch[...], wr[part, :]) * slope[:, part]).astype(BF16)
        grad_pre[:, part] = low
        vec_wide[:, part] = column_sum(low)

    for index in range(wide // CHUNK):
        reduce(index)

    for start in range(0, width, CHUNK):
        part = slice(start, start + CHUNK)
        work[:, part] += nt(grad_pre[...], we[part, :])

    for (doc, start, row), scale in zip(blocks, scales):
        error = work[row : row + ROWS]
        norm = unit[row : row + ROWS]
        sums[3] += column_sum(error * norm)
        sums[4] += column_sum(error)
        scaled = error * ng[...]
        grad = (
            scaled
            - jnp.mean(scaled, axis=-1, keepdims=True)
            - norm * jnp.mean(scaled * norm, axis=-1, keepdims=True)
        ) * scale
        unit[row : row + ROWS] = grad
        leave(unit, grad_summed_far, doc, start, row)
        low = grad.astype(BF16)
        grad_second[row : row + ROWS] = low
        sums[5] += column_sum(low)
        grad_mix[row : row + ROWS] = nt(low, wpo[...]).astype(BF16)
        leave(grad_mix, grad_mix_far, doc, start, row)
    for index, value in enumerate(sums):
        vec[index : index + 1] = value
    vec[6:8] = jnp.zeros((2, width), F32)
    for copy in leaving:
        copy.wait()


def feed(place, summed, cotangent, we, be, wr, br, ng, ns, fg, fs, wpo):
    docs, rows, width = summed.shape
    wide = we.shape[1]
    tokens = docs * rows
    return call(
        feed_body,
        (1,),
        (place,),
        [whole(a) for a in (summed, cotangent, we, be, wr, br, ng, ns, fg, fs, wpo)],
        [
            out_raw((docs, rows, width), BF16),
            out_whole((tokens, width), BF16),
            out_whole((tokens, wide), BF16),
            out_whole((tokens, width), BF16),
            out_whole((tokens, wide), BF16),
            out_raw((docs, rows, width), F32),
            out_whole((tokens, width), BF16),
            out_raw((docs, rows, width), BF16),
            out_whole((8, width), F32),
            out_whole((1, wide), F32),
        ],
        [
            pltpu.VMEM((tokens, width), F32),
            pltpu.VMEM((tokens, wide), F32),
            pltpu.VMEM((tokens, width), F32),
            pltpu.VMEM((tokens, width), F32),
            pltpu.VMEM((tokens, width), BF16),
            pltpu.VMEM((tokens, width), BF16),
            pltpu.SemaphoreType.DMA((3 * tokens // ROWS,)),
        ],
        spare=12,
    )


def key_value_body(place, *refs, docs):
    gk_kept, gk_came, gv_kept, gv_came, kx, vx, ck, cv = refs[:8]
    own, from_left, from_right, dq = refs[8:12]
    gk, gv, vec, rows_in, pooled, total = refs[12:]
    offset = place[0]
    rows, width = gk.shape[0] // docs, gk.shape[1]
    count = rows // STRIDE
    vec[...] = jnp.zeros_like(vec)
    for doc in range(docs):
        length = place[1 + doc]
        spot = offset - HALF + positions((rows + WIN, 1), 0)
        valid = (spot >= 0) & (spot < length)
        first = doc * rows
        for which, (kept, came, ext, taps, out, row) in enumerate(
            (
                (gk_kept, gk_came, kx, ck, gk, 0),
                (gv_kept, gv_came, vx, cv, gv, KER),
            )
        ):
            pooled[...] = kept[doc].astype(F32) + came[doc].astype(F32)
            masked = jnp.where(valid, ext[doc].astype(F32), 0.0)
            for group in range(width // LANES):
                lanes = slice(group * LANES, (group + 1) * LANES)
                grown = pooled[:count, lanes]
                shifted = pooled[1 : count + 1, lanes]
                rows_in[group] = masked[:, lanes]
                for tap in range(KER):
                    start = HALF - KER // 2 + tap
                    read = rows_in[group, pl.ds(start, count, stride=STRIDE), :]
                    vec[row + tap : row + tap + 1, lanes] += column_sum(grown * read)
                if which == 1:
                    vec[2 * KER : 2 * KER + 1, lanes] += column_sum(grown)
                total[group] = own[doc, which, :, lanes]
                total[group, :HALF] += from_left[doc, which, :, lanes].astype(F32)
                total[group, rows - HALF :] += from_right[doc, which, :, lanes].astype(F32)
                for phase, terms in enumerate(
                    (
                        ((2, grown),),
                        ((3, grown),),
                        ((4, grown), (0, shifted)),
                        ((1, shifted),),
                    )
                ):
                    part = pl.ds(phase, count, stride=STRIDE)
                    added = None
                    for tap, values in terms:
                        term = values * taps[tap : tap + 1, lanes]
                        added = term if added is None else added + term
                    inside = offset + phase + STRIDE * positions((count, 1), 0) < length
                    total[group, part, :] = total[group, part, :] + jnp.where(inside, added, 0.0)
                out[first : first + rows, lanes] = total[group].astype(BF16)
        vec[11:12] += column_sum(dq[doc])
    vec[12:13] += column_sum(gv[...])


def key_value_gradients(place, pooled_grads, kx, vx, ck, cv, own, left, right, dq):
    docs, rows, width = dq.shape
    return call(
        functools.partial(key_value_body, docs=docs),
        (1,),
        (place,),
        [
            whole(a)
            for a in (*pooled_grads, kx, vx, ck, cv, own, left, right, dq)
        ],
        [out_whole((docs * rows, width), BF16)] * 2 + [out_whole((16, width), F32)],
        [
            pltpu.VMEM((width // LANES, rows + WIN, LANES), F32),
            pltpu.VMEM((rows // STRIDE + 8, width), F32),
            pltpu.VMEM((width // LANES, rows, LANES), F32),
        ],
    )


def input_body(place, dq, gk, gv, gmid, wq, wk, wv, dx):
    total = nt(dq[...], wq[...]) + nt(gk[...], wk[...]) + nt(gv[...], wv[...])
    dx[...] = (gmid[...] + total.reshape(gmid.shape)).astype(BF16)


def input_gradient(place, dq, gk, gv, gmid, wq, wk, wv):
    docs, rows, width = gmid.shape
    (dx,) = call(
        input_body,
        (1,),
        (place,),
        [whole(a) for a in (dq, gk, gv, gmid, wq, wk, wv)],
        [out_whole((docs, rows, width), BF16)],
    )
    return dx


def scatter_body(bits, *refs, kinds, order, vectors, quartered):
    count = len(kinds)
    operands = [refs[2 * index : 2 * index + 2] for index in range(count)]
    extra = refs[2 * count : 2 * count + vectors]
    rest = refs[2 * count + vectors :]
    if quartered:
        results, (ordered, rounded, *small) = (rest[0], rest[0]), rest[1:]
    else:
        results, (ordered, rounded, *small) = rest[:2], rest[2:]
    core = bits[0]
    sides = 2 if ("batch", 1) in order else 1
    owners = 8

    def start_of(which, size):
        if quartered:
            return which * size
        return pl.multiple_of((which ^ core) * size, LANES)

    def place_tile(which, side, owner, target, size, value):
        index = []
        for at, (axis, bit) in enumerate(order):
            if axis == "batch":
                index += [side, which] if quartered else [side ^ bits[1 + at]]
            else:
                index.append(((owner >> bit) & 1) ^ bits[1 + at])
        results[which][(*index, slice(target, target + size), slice(None))] = value

    base = 0
    for (left, right), kind in zip(operands, kinds):
        tall = left.shape[1]
        turned = left[...].T
        if kind == "wide":
            half = right.shape[1] // 2
            size = tall // owners // sides
            for which in range(2):
                start = start_of(which, half)
                for part in range(half // 768):
                    rounded[...] = nn(turned, right[:, pl.ds(start + part * 768, 768)]).astype(BF16)
                    for column in range(2):
                        target = base + (2 * part + column) * size
                        for owner in range(owners):
                            for side in range(sides):
                                row = (owner * sides + side) * size
                                value = rounded[row : row + size, column * 384 : column * 384 + 384]
                                place_tile(which, side, owner, target, size, value)
            base += half // 384 * size
        elif kind == "tall":
            ordered[...] = turned
            size = tall // 2 // sides
            for part in range(right.shape[1] // 768):
                product = nn(ordered[...], right[:, part * 768 : part * 768 + 768])
                rounded[...] = product.astype(BF16)
                for column in range(2):
                    owner = 2 * part + column
                    for side in range(sides):
                        for which in range(2):
                            row = start_of(which, 384) + side * size
                            value = rounded[pl.ds(row, size), column * 384 : column * 384 + 384]
                            place_tile(which, side, owner, base, size, value)
            base += size
        else:
            size = tall // owners // sides
            if quartered:
                columns = right[...]
            else:
                columns = jnp.concatenate(
                    [right[:, pl.ds(start_of(which, 384), 384)] for which in range(2)], axis=1
                )
            rounded[...] = nn(turned, columns).astype(BF16)
            for which in range(2):
                for owner in range(owners):
                    for side in range(sides):
                        row = (owner * sides + side) * size
                        value = rounded[row : row + size, which * 384 : which * 384 + 384]
                        place_tile(which, side, owner, base, size, value)
            base += size
    if vectors:
        (block,) = small
        vec_feed, vec_first, vec_input, vec_wide = extra
        for owner in range(owners):
            lanes = slice(owner * 96, owner * 96 + 96)
            block[0, owner] = jnp.zeros(block.shape[2:], F32)
            block[1, owner] = jnp.zeros(block.shape[2:], F32)
            block[0, owner, 0:8, 0:96] = vec_feed[:, lanes]
            block[0, owner, 0:8, LANES : LANES + 96] = vec_first[:, lanes]
            block[1, owner, 0:16, 0:96] = vec_input[:, lanes]
            for part in range(4):
                at = owner * 384 + part * 96
                block[0, owner, 8 + part : 9 + part, 0:96] = vec_wide[:, at : at + 96]
        for owner in range(owners):
            for which in range(2):
                place_tile(which, 0, owner, base, 16, block[which ^ core, owner].astype(BF16))


def scatter_products(bits, order, items, extra=(), quartered=False):
    sides = 2 if ("batch", 1) in order else 1
    rows = 0
    for kind, left, right in items:
        if kind == "wide":
            rows += right.shape[1] // 768 * (left.shape[1] // 8 // sides)
        elif kind == "tall":
            rows += 384 // sides
        else:
            rows += 96 // sides
    rows += 16 if extra else 0
    shape = (2,) * (len(order) + quartered) + (rows, 384)
    operands = [array for _, left, right in items for array in (left, right)]
    return call(
        functools.partial(
            scatter_body,
            kinds=tuple(kind for kind, _, _ in items),
            order=tuple(order),
            vectors=len(extra),
            quartered=quartered,
        ),
        (1,),
        (bits,),
        [whole(a) for a in (*operands, *extra)],
        [out_whole(shape, BF16)] * (1 if quartered else 2),
        [pltpu.VMEM((768, operands[0].shape[0]), BF16), pltpu.VMEM((768, 768), BF16)]
        + ([pltpu.VMEM((2, 8, 16, 384), F32)] if extra else []),
    )


def quarter_products_body(bits, *refs, kinds, levels):
    count = len(kinds)
    operands = [refs[2 * index : 2 * index + 2] for index in range(count)]
    out, turned, by_owner, by_half, sems = refs[2 * count :]
    sides, cores, owners = 2, 2, 1 << levels
    pending = {}
    turns = {}

    def digits(owner):
        return tuple(((owner >> level) & 1) ^ bits[level] for level in range(levels))

    def next_slot(buffer):
        slot = turns.get(buffer, 0) % 2
        turns[buffer] = turns.get(buffer, 0) + 1
        for copy in pending.pop((buffer, slot), []):
            copy.wait()
        return slot

    def leave(buffer, slot, source, target):
        copies = pending.setdefault((buffer, slot), [])
        copy = pltpu.make_async_copy(source, target, sems.at[buffer, slot, len(copies)])
        copy.start()
        copies.append(copy)

    def spread_rows(value):
        slot = next_slot(0)
        size = 768 // owners // sides
        for owner in range(owners):
            for side in range(sides):
                row = (owner * sides + side) * size
                for column in range(2):
                    part = value[row : row + size, column * 384 : column * 384 + 384]
                    by_owner[(slot, column, side, *digits(owner))] = part
        return slot

    def leave_rows(slot, column, which, base):
        middle = (slice(None),) * levels
        leave(0, slot, by_owner.at[slot, column], out.at[(slice(None), which, *middle, pl.ds(base, 48))])

    base = 0
    for (left, right), kind in zip(operands, kinds):
        turned[...] = left[...].T
        if kind == "wide":
            for which in range(cores):
                for part in range(2):
                    start = which * 1536 + part * 768
                    value = nn(turned[...], right[:, start : start + 768]).astype(BF16)
                    slot = spread_rows(value)
                    for column in range(2):
                        leave_rows(slot, column, which, base + (2 * part + column) * 48)
            base += 192
        elif kind == "tall":
            for part in range(4):
                value = nn(turned[...], right[:, part * 768 : part * 768 + 768]).astype(BF16)
                slot = next_slot(1)
                for which in range(cores):
                    for side in range(sides):
                        row = (which * sides + side) * 192
                        for column in range(2):
                            part_value = value[row : row + 192, column * 384 : column * 384 + 384]
                            by_half[slot, column, side, which] = part_value
                for column in range(2):
                    owner = digits(2 * part + column)
                    target = out.at[(slice(None), slice(None), *owner, pl.ds(base, 192))]
                    leave(1, slot, by_half.at[slot, column], target)
            base += 192
        else:
            slot = spread_rows(nn(turned[...], right[...]).astype(BF16))
            for which in range(cores):
                leave_rows(slot, which, which, base)
            base += 48
    for copies in pending.values():
        for copy in copies:
            copy.wait()


def quarter_products(bits, items, levels):
    rows = sum(48 if kind == "square" else 192 for kind, _, _ in items)
    operands = [array for _, left, right in items for array in (left, right)]
    (out,) = call(
        functools.partial(
            quarter_products_body, kinds=tuple(kind for kind, _, _ in items), levels=levels
        ),
        (1,),
        (bits,),
        [whole(a) for a in operands],
        [out_raw((2, 2) + (2,) * levels + (rows, 384), BF16)],
        [
            pltpu.VMEM((768, operands[0].shape[0]), BF16),
            pltpu.VMEM((2, 2, 2) + (2,) * levels + (48, 384), BF16),
            pltpu.VMEM((2, 2, 2, 2, 192, 384), BF16),
            pltpu.SemaphoreType.DMA((2, 2, 2)),
        ],
    )
    return out


def order_quarters(spots, low, other, across, quarters):
    odd, upper = spots[0], spots[1]
    quarters[odd, upper] = low[...]
    quarters[odd, 1 - upper] = other[...]
    quarters[1 - odd, upper] = across[0]
    quarters[1 - odd, 1 - upper] = across[1]


def order_parts(spots, parts, quarters):
    odd, upper = spots[0], spots[1]
    for flip, part in enumerate(parts):
        quarters[odd ^ (flip & 1), upper ^ (flip >> 1)] = part[...]


def join_square(quarters, start, out):
    for core in range(2):
        for side in range(2):
            block = quarters[core, side, start : start + 48]
            out[side * 48 : side * 48 + 48, core * 384 : core * 384 + 384] = block.astype(F32)


def collect_feed_body(spots, low, other, across, expand, reduce, pooled_out, quarters, tall):
    order_quarters(spots, low, other, across, quarters)
    for core in range(2):
        for side in range(2):
            rows = slice(side * 48, side * 48 + 48)
            for part in range(4):
                column = core * 1536 + part * 384
                block = quarters[core, side, part * 48 : part * 48 + 48]
                expand[rows, column : column + 384] = block.astype(F32)
            at = core * 384 + side * 192
            tall[at : at + 192] = quarters[core, side, 192:384].astype(F32)
    reduce[...] = tall[...].T
    join_square(quarters, 384, pooled_out)


def collect_feed(spots, low, other, across):
    return call(
        collect_feed_body,
        (1,),
        (spots,),
        [whole(low), whole(other), whole(across)],
        [out_whole((96, 3072), F32), out_whole((384, 768), F32), out_whole((96, 768), F32)],
        [pltpu.VMEM((2, 2) + low.shape, BF16), pltpu.VMEM((768, 384), F32)],
    )


def collect_last_body(spots, *refs, cut):
    pq, lo, lq, lk, lv, vectors, quarters = refs[4:]
    order_parts(spots, refs[:4], quarters)
    for index, out in enumerate((pq, lo, lq)):
        join_square(quarters, index * 48, out)
    for core in range(2):
        half = quarters[core, 0, cut:].astype(F32) + quarters[core, 1, cut:].astype(F32)
        lk[:, core * 384 : core * 384 + 384] = half[:96]
        lv[:, core * 384 : core * 384 + 384] = half[96:192]
        vectors[core] = half[192:208]


def collect_last(spots, parts, cut):
    return call(
        functools.partial(collect_last_body, cut=cut),
        (1,),
        (spots,),
        [whole(part) for part in parts],
        [out_whole((96, 768), F32)] * 5 + [out_whole((2, 16, 384), F32)],
        [pltpu.VMEM((2, 2) + parts[0].shape, BF16)],
    )


def swap(value, axis, bit):
    count = lax.axis_size(axis)
    return lax.ppermute(value, axis, [(i, i ^ (1 << bit)) for i in range(count)])


def shift(value, axis, by):
    count = lax.axis_size(axis)
    pairs = [(i, i + by) for i in range(count) if 0 <= i + by < count]
    return lax.ppermute(value, axis, pairs)


def fold(kept, came):
    low = (kept[1].astype(F32) + came[1].astype(F32)).astype(BF16)
    return low, kept[0].astype(F32) + came[0].astype(F32)


def total_of(terms, *index):
    total = None
    for term in terms:
        value = term[index].astype(F32)
        total = value if total is None else total + value
    return total


def advance(terms, hop):
    came = swap(total_of(terms, 1).astype(BF16), *hop)
    return [term[0] for term in terms], came


def cut(quarters, start, size):
    return quarters[:, :, start : start + size]


def device_step(
    inputs, lengths, cotangent,
    local_query, local_query_bias, local_key, local_value, local_value_bias,
    local_output, local_output_bias, pooled_query, pooled_query_bias,
    pooled_output, pooled_output_bias, conv_key, conv_value, conv_value_bias,
    norm_gain, norm_shift, expand_weight, expand_bias, reduce_weight, reduce_bias,
    final_gain, final_shift,
):
    docs, rows, width = inputs.shape
    devices = lax.axis_size("seq")
    me = lax.axis_index("seq")
    mine = lax.axis_index("batch")
    levels = devices.bit_length() - 1
    size = rows // STRIDE
    flat = docs * rows
    offset = me * rows
    reach = -(-REACH // size)
    gathered = devices <= 2 * reach
    fast = devices == 8 and width == 768 and lax.axis_size("batch") == 4
    base = jnp.where(gathered, 0, offset // STRIDE - reach * size)
    place = jnp.concatenate([offset[None], lengths, base[None]]).astype(jnp.int32)

    def line(vector):
        return vector[None]

    def tokens(array):
        return array.reshape(flat, array.shape[-1])

    taps_key, taps_value = conv_key.T, conv_value.T

    left = shift(inputs[:, rows - HALF :], "seq", 1)
    right = shift(inputs[:, :HALF], "seq", -1)
    q, k_own, v_own, key_near, value_near = project(
        place, inputs, local_query, line(local_query_bias), local_key, local_value,
        line(local_value_bias),
    )
    left, right, k_own = sync(left, right, k_own)
    kx, vx, pooled = pool(
        place, left, right, k_own, v_own, key_near, value_near, line(local_value_bias),
        taps_key, taps_value, line(conv_value_bias),
    )
    own = [pooled[which][None] for which in range(2)]

    mixes, probs_one = [], []

    def local_step(doc, token):
        mix, probs = local_forward(token, q, kx, vx, doc)
        mixes.append(mix)
        probs_one.append(probs)
        return mix

    if gathered:
        orders = ([2, 1, 0], [0, 2, 1]) if levels == 3 else (list(range(levels)),) * 2
        have = own
        pieces = [[own[0]], [own[1]]]
        relative = [[0], [0]]
        token = place
        for stage in range(levels):
            came = [swap(have[which], "seq", orders[which][stage]) for which in range(2)]
            if stage == 0:
                came[0], came[1], token = sync(came[0], came[1], token)
            if 0 < stage <= docs:
                done = local_step(stage - 1, token)
            if stage == levels - 1:
                while len(mixes) < docs:
                    local_step(len(mixes), token)
                mix_one, middle, middle_low, q2 = middle_forward(
                    token, inputs, local_output, line(local_output_bias), pooled_query,
                    line(pooled_query_bias), mixes,
                )
                came[0], came[1], q2, token = sync(came[0], came[1], q2, token)
            elif stage > 0:
                came[0], came[1], mixes[stage - 1], token = sync(
                    came[0], came[1], done, token
                )
            for which in range(2):
                pieces[which].append(came[which])
                relative[which] += [r ^ (1 << orders[which][stage]) for r in relative[which]]
                if stage < levels - 1:
                    have[which] = jnp.concatenate([have[which], came[which]])
        slots = jnp.stack([me ^ jnp.array(r, jnp.int32) for r in relative])
    else:
        pieces = [
            [own[which]]
            + [
                shift(own[which], "seq", sign * distance)
                for distance in range(1, reach + 1)
                for sign in (1, -1)
            ]
            for which in range(2)
        ]
        spots = [reach] + [
            reach - sign * distance for distance in range(1, reach + 1) for sign in (1, -1)
        ]
        slots = jnp.array([spots, spots], jnp.int32)
        token = place
        for doc in range(docs):
            local_step(doc, token)
        mix_one, middle, middle_low, q2 = middle_forward(
            token, inputs, local_output, line(local_output_bias), pooled_query,
            line(pooled_query_bias), mixes,
        )

    keys, values, probs_two, mix_two, summed, expand_near, reduce_near = pooled_forward(
        token, slots, pieces[0], pieces[1], q2, middle, pooled_output, line(pooled_output_bias),
        expand_weight, reduce_weight,
    )
    (
        outputs, normed_low, hidden, grad_branch, grad_pre, grad_summed, grad_second, grad_mix_two,
        vec_feed, vec_wide,
    ) = feed(
        token, summed, cotangent, expand_near, line(expand_bias), reduce_near,
        line(reduce_bias), line(norm_gain), line(norm_shift), line(final_gain),
        line(final_shift), pooled_output,
    )

    order_first = [("batch", 1)] + [("seq", level) for level in range(levels)]
    order_last = order_first[1:]

    def bits_of(order):
        ids = [mine & 1] + [(mine if axis == "batch" else me) >> bit & 1 for axis, bit in order]
        return jnp.stack(ids).astype(jnp.int32)

    seq_bits = jnp.stack([me >> level & 1 for level in range(levels)]).astype(jnp.int32)

    def over_batch(blocks):
        part = blocks.shape[2:]
        flat_blocks = blocks.reshape(-1, blocks.shape[-1])
        mine_part = lax.psum_scatter(flat_blocks, "batch", scatter_dimension=0, tiled=True)
        return mine_part.reshape(part)

    if fast:
        feed_blocks = quarter_products(
            seq_bits,
            [
                ("wide", normed_low, grad_pre),
                ("tall", grad_branch, hidden),
                ("square", tokens(mix_two), grad_second),
            ],
            levels,
        )
        feed_blocks, grad_mix_two, token = sync(feed_blocks, grad_mix_two, token)
        feed_part = over_batch(feed_blocks)

    blocks = devices if gathered else 2 * reach + 1
    if gathered:
        back = ([0, 1, 2], [1, 2, 0]) if levels == 3 else (list(range(levels)),) * 2
        places = []
        for which in range(2):
            spots = []
            for block in range(devices):
                relative = 0
                for at, bit in enumerate(back[which]):
                    relative |= (block >> (levels - 1 - at) & 1) << bit
                spots.append(relative)
            places.append(me ^ jnp.array(spots, jnp.int32))
        places = jnp.stack(places)
        half_blocks = devices // 2
    else:
        middle_first = [reach] + [spot for spot in range(blocks) if spot != reach]
        places = jnp.array([middle_first, middle_first], jnp.int32)
        half_blocks = 1
    grad_q2, dk_kept, dk_sent, dv_kept, dv_sent = pooled_backward(
        places, token, q2, keys, values, probs_two, grad_mix_two, size, half_blocks
    )
    grad_middle, grad_first, grad_mix_one, vec_first = first_backward(
        token, grad_q2, grad_summed, pooled_query, local_output
    )
    back_parts = ()

    def back_step(doc, token):
        return local_backward(
            token, q, kx, vx, grad_mix_one, probs_one[doc], doc, back_parts
        )

    if gathered:
        kept = [part.reshape((2,) * (levels - 1) + part.shape[1:]) for part in (dk_kept, dv_kept)]
        sent = [part.reshape((2,) * (levels - 1) + part.shape[1:]) for part in (dk_sent, dv_sent)]
        for stage in range(levels):
            came = [swap(sent[which], "seq", back[which][stage]) for which in range(2)]
            if stage < docs:
                back_parts = list(back_step(stage, token))
            if fast and stage == 0:
                came[0], came[1], back_parts[0], token = sync(
                    came[0], came[1], back_parts[0], token
                )
            if fast and stage == 1:
                came[0], came[1], back_parts[2], back_parts[3], token = sync(
                    came[0], came[1], back_parts[2], back_parts[3], token
                )
            if fast and stage == 2:
                middle_kept, middle_sent = scatter_products(
                    bits_of(order_first) + 0 * token[0],
                    order_first,
                    [
                        ("square", tokens(middle_low), tokens(grad_q2)),
                        ("square", tokens(mix_one), grad_first),
                        ("square", tokens(inputs), tokens(back_parts[0])),
                    ],
                )
                from_left = shift(back_parts[3], "seq", 1)
                from_right = shift(back_parts[2], "seq", -1)
                came[0], came[1], from_left, from_right, middle_sent, token = sync(
                    came[0], came[1], from_left, from_right, middle_sent, token
                )
            if stage < levels - 1:
                for which in range(2):
                    sent[which], kept[which] = fold(kept[which], came[which])
        pooled_grads = [kept[0], came[0], kept[1], came[1]]
    else:
        pooled_grads = []
        for kept, sent in ((dk_kept, dk_sent), (dv_kept, dv_sent)):
            total = kept[0]
            for distance in range(1, reach + 1):
                total = total + shift(sent[reach - distance], "seq", -distance).astype(F32)
                total = total + shift(sent[reach + distance - 1], "seq", distance).astype(F32)
            after = shift(total[:, :1].astype(BF16), "seq", -1).astype(F32)
            total = jnp.concatenate([total[:, :size], jnp.tile(after, (1, 8, 1))], axis=1)
            pooled_grads += [total, jnp.zeros_like(total)]
        for doc in range(docs):
            back_parts = back_step(doc, token)
    if not fast:
        from_left = shift(back_parts[3], "seq", 1)
        from_right = shift(back_parts[2], "seq", -1)
    dq, own_grads = back_parts[:2]
    if fast:
        middle_came = swap(middle_sent, "batch", 0)
    grad_k, grad_v, vec_input = key_value_gradients(
        token, pooled_grads, kx, vx, taps_key, taps_value,
        own_grads, from_left, from_right, dq,
    )
    if fast:
        last_kept, last_sent = scatter_products(
            bits_of(order_last),
            order_last,
            [("square", tokens(inputs), grad_k), ("square", tokens(inputs), grad_v)],
            (vec_feed, vec_first, vec_input, vec_wide),
        )
        last_sent, middle_came, token = sync(last_sent, middle_came, token)
        last_came = swap(last_sent, "batch", 0)
        middle_terms, middle_came = advance([middle_kept, middle_came], ("batch", 1))
    input_grad = input_gradient(
        token, tokens(dq), grad_k, grad_v, grad_middle, local_query, local_key, local_value
    )

    if fast:
        cut_feed = 240
        one = [feed_part[..., :cut_feed, :]]
        two = [feed_part[..., cut_feed:, :]]

        def advance_second(terms, hop):
            came = swap(total_of(terms, slice(None), 1).astype(BF16), *hop)
            return [term[:, 0] for term in terms], came

        one, one_came = advance(one, ("seq", 0))
        two, two_came = advance_second(two, ("seq", 1))
        input_grad, last_came, middle_came, one_came, two_came = sync(
            input_grad, last_came, middle_came, one_came, two_came
        )
        last_terms, last_came = advance([last_kept, last_came], ("seq", 0))
        middle_terms, middle_came = advance_second(middle_terms + [middle_came], ("seq", 1))
        one, one_came = advance(one + [one_came], ("seq", 1))
        two, two_came = advance(two + [two_came], ("seq", 0))
        last_came, middle_came, one_came, two_came = sync(
            last_came, middle_came, one_came, two_came
        )

        last_terms, last_came = advance(last_terms + [last_came], ("seq", 1))
        one, two = one + [one_came], two + [two_came]
        feed_came = swap(
            jnp.concatenate([total_of(one, 1), total_of(two, 1)]).astype(BF16), "seq", 2
        )
        middle_terms, middle_came = advance(middle_terms + [middle_came], ("seq", 0))
        last_came, middle_came, feed_came = sync(last_came, middle_came, feed_came)

        last_terms, last_came = advance(last_terms + [last_came], ("seq", 2))
        middle_terms, middle_came = advance(middle_terms + [middle_came], ("seq", 2))
        feed_low = (
            jnp.concatenate([total_of(one, 0), total_of(two, 0)]) + feed_came.astype(F32)
        ).astype(BF16)
        feed_other = swap(feed_low, "batch", 1)
        last_came, middle_came, feed_other = sync(last_came, middle_came, feed_other)
        cut_at = middle_came.shape[0]
        low = jnp.concatenate(
            [
                total_of(middle_terms + [middle_came], Ellipsis),
                total_of(last_terms + [last_came], Ellipsis),
            ]
        ).astype(BF16)
        parts = [low] + [
            lax.ppermute(low, "batch", [(each, each ^ flip) for each in range(4)])
            for flip in range(1, 4)
        ]
        feed_across = swap(jnp.stack([feed_low, feed_other]), "batch", 0)
        spots = jnp.stack([mine & 1, mine >> 1]).astype(jnp.int32)
        grad_expand, grad_reduce, grad_po = collect_feed(spots, feed_low, feed_other, feed_across)
        *others, grad_expand, grad_reduce, grad_po = sync(
            *parts[1:], grad_expand, grad_reduce, grad_po
        )
        parts = parts[:1] + others
        grad_pq, grad_lo, grad_lq, grad_lk, grad_lv, lines = collect_last(
            spots, parts, cut_at
        )
        vec_low, vec_high = lines[0, :, :96], lines[1, :, :96]
        (fg, fs, rb, ng, ns, pob) = [vec_low[index] for index in range(6)]
        pqb, lob = lines[0, 0, LANES : LANES + 96], lines[0, 1, LANES : LANES + 96]
        grad_eb = vec_low[8:12].reshape(-1)
    else:

        def plain(left_array, right_array):
            product = tn(left_array, right_array)
            part = lax.psum_scatter(product, "seq", scatter_dimension=0, tiled=True)
            return lax.psum(part.astype(BF16), "batch").astype(F32)

        grad_expand = plain(normed_low, grad_pre)
        grad_reduce = plain(hidden, grad_branch)
        grad_po = plain(tokens(mix_two), grad_second)
        grad_pq = plain(tokens(middle_low), tokens(grad_q2))
        grad_lo = plain(tokens(mix_one), grad_first)
        grad_lq = plain(tokens(inputs), tokens(dq))
        grad_lk = plain(tokens(inputs), grad_k)
        grad_lv = plain(tokens(inputs), grad_v)
        vectors = jnp.concatenate(
            [vec_feed, vec_first, vec_input, vec_wide.reshape(-1, width)], axis=0
        )
        vectors = lax.psum(vectors, ("seq", "batch"))
        share = width // devices
        part = lax.dynamic_slice_in_dim(vectors, me * share, share, axis=1)
        wide = vectors[32:].reshape(-1)
        wide_share = wide.shape[0] // devices
        grad_eb = lax.dynamic_slice_in_dim(wide, me * wide_share, wide_share, axis=0)
        (fg, fs, rb, ng, ns, pob) = [part[index] for index in range(6)]
        pqb, lob = part[8], part[9]
        vec_high = part[16:32]
    grad_ck = vec_high[:KER].T
    grad_cv = vec_high[KER : 2 * KER].T
    cvb, lqb, lvb = vec_high[10], vec_high[11], vec_high[12]
    return (
        outputs, input_grad,
        grad_lq, lqb, grad_lk, grad_lv, lvb, grad_lo, lob, grad_pq, pqb, grad_po, pob,
        grad_ck, grad_cv, cvb, ng, ns, grad_expand, grad_eb, grad_reduce, rb, fg, fs,
    )


def solution(mesh):
    vector = P("seq")
    matrix = P("seq", None)
    return jax.shard_map(
        device_step,
        mesh=mesh,
        in_specs=(P("batch", "seq", None), P("batch"), P("batch", "seq", None)) + (P(),) * 22,
        out_specs=(
            P("batch", "seq", None), P("batch", "seq", None),
            matrix, vector, matrix, matrix, vector, matrix, vector, matrix, vector, matrix, vector,
            matrix, matrix, vector, vector, vector, matrix, vector, matrix, vector, vector, vector,
        ),
        check_vma=False,
    )
```
